32 devices in a mesh: band: 4 (over y, x), dx: 4 (over z), dy: 2 (over core).
Axes of the slice: x: 2, y: 2, z: 4, core: 2. Of those that a mesh axis runs over, the one named last changes fastest.
Arguments:
- wave_bands: float32 [4, 32, 32, 128], P('band', 'dx', 'dy'), may hold values from -6 to 6
- potential: float32 [32, 32, 128], P('dx', 'dy', 'band'), may hold values from -1.5 to 0.5
- atom_offsets: int32 [4, 2, 4, 3], P('dx', 'dy'), may hold values from 0 to 95, as said below
- proj_counts: int32 [4, 2, 4], P('dx', 'dy'), may hold values from 0 to 9, as said below
- dh_matrix: float32 [4, 2, 4, 9, 9], P('dx', 'dy'), as said below
- ds_matrix: float32 [4, 2, 4, 9, 9], P('dx', 'dy'), as said below
Outputs:
- new_bands: float32 [4, 32, 32, 128], P('band', 'dx', 'dy')
- new_residual: float32 [4, 32, 32, 128], P('band', 'dx', 'dy')
- band_energy: float32 [4], P('band')
The draws below stay inside these ranges and needn't reach their ends.
Inputs may be any that keep to these rules, and one draw needn't show every extreme that they name: `atom_offsets`: columns are x in 0..7, y in 0..15, z in 32..3*128/4-1. `proj_counts`: each count is 0 (empty slot), 1, 4 or 9. `dh_matrix`: each matrix is symmetric. `ds_matrix`: each matrix is symmetric, and each diagonal entry exceeds the sum of the magnitudes of the other entries in its row.
All inputs are finite; a program needn't handle non-finite values.
Results may differ from the reference program's by a relative error of at most 0.00017.
Values sent between devices are 32-bit elements; how exact they have to be, the bound alone decides.
No kernel may reach another device: no remote copies, remote signals or barrier semaphores. Data moves between devices by JAX's collectives and lax.ppermute only.
A program may use at most 64 MiB of HBM per device.

```python
import jax
import jax.numpy as jnp
from jax import lax

CX = 8
CY = 16
NZ = 128
ATOM_DEV = 4
NPROJ = 9
COARSE_SWEEPS = 2
BANDS = 4
TILES_X = 4
TILES_Y = 2
NX = 32
NY = 32


def draw_atom_offsets(key, part):
    key_x, key_y, key_z = jax.random.split(key, 3)
    array_shape = (TILES_X, TILES_Y, ATOM_DEV)
    offset_x = jax.random.randint(key_x, array_shape, 0, CX)
    offset_y = jax.random.randint(key_y, array_shape, 0, CY)
    offset_z = jax.random.randint(key_z, array_shape, NZ // 4, 3 * NZ // 4)
    offset_x = offset_x.at[0, 0, 0].set(CX - 1).at[0, 0, 1].set(0)
    offset_y = offset_y.at[0, 0, 0].set(CY - 1)
    offset_z = offset_z.at[0, 0, 0].set(3 * NZ // 4 - 1)
    return jnp.stack([offset_x, offset_y, offset_z], axis=-1).astype(jnp.int32)


def draw_proj_counts(key, part):
    drawn_kind = jax.random.randint(key, (TILES_X, TILES_Y, ATOM_DEV), 0, 4)
    counts = jnp.where(drawn_kind == 0, 0, jnp.where(drawn_kind == 1, 1, jnp.where(drawn_kind == 2, 4, NPROJ)))
    return counts.at[0, 0, 0].set(NPROJ).at[0, 0, 1].set(0).astype(jnp.int32)


def draw_dh_matrix(key, part):
    key_off, key_diag = jax.random.split(jax.random.fold_in(key, 11))
    array_shape = (TILES_X, TILES_Y, ATOM_DEV, NPROJ, NPROJ)
    gaussian = jax.random.normal(key_off, array_shape, jnp.float32) * 0.4
    symmetric = 0.5 * (gaussian + jnp.swapaxes(gaussian, -1, -2))
    identity = jnp.eye(NPROJ, dtype=jnp.float32)
    diagonal = jax.random.uniform(key_diag, array_shape[:-1], jnp.float32, -2.0, 2.0)
    return symmetric * (1.0 - identity) + diagonal[..., None] * identity


def draw_ds_matrix(key, part):
    key_off, key_diag = jax.random.split(jax.random.fold_in(key, 23))
    array_shape = (TILES_X, TILES_Y, ATOM_DEV, NPROJ, NPROJ)
    uniform_off = jax.random.uniform(key_off, array_shape, jnp.float32, -0.1, 0.1)
    symmetric = 0.5 * (uniform_off + jnp.swapaxes(uniform_off, -1, -2))
    identity = jnp.eye(NPROJ, dtype=jnp.float32)
    diagonal = 1.0 + jax.random.uniform(key_diag, array_shape[:-1], jnp.float32, 0.0, 1.0)
    return symmetric * (1.0 - identity) + diagonal[..., None] * identity


def shard_levels(rng, dims, cuts, smallest, top_value):
    def one(position, shards_of):
        heights = jax.random.uniform(jax.random.fold_in(jax.random.fold_in(rng, 6), position), (shards_of,), jnp.float32, smallest / len(cuts), top_value / len(cuts))
        return jnp.repeat(jnp.exp(heights), dims[position] // shards_of).reshape((-1,) + (1,) * (len(dims) - position - 1))

    gain = one(*cuts[0])
    for cut in cuts[1:]:
        gain = gain * one(*cut)
    return gain


def noise(own_key, dims, scale, limit, shards=(), held_as=jnp.bfloat16):
    values = jax.random.normal(own_key, dims, jnp.float32) * scale
    if len(shards) > 0:
        values = shard_levels(own_key, dims, shards, -0.22, 0.18) * values
    return jnp.clip(values, min=-limit, max=limit).astype(held_as)


def setup_inputs(seed: int = 0) -> dict:
    key_list = jax.random.split(jax.random.key(seed), 7)
    wave_bands = noise(key_list[0], (BANDS, NX, NY, NZ), 1.0, 6.0, ((0, 4), (1, 4), (2, 2)), jnp.float32)
    potential = jnp.clip(-1.5 + 2.0 * jax.random.uniform(key_list[1], (NX, NY, NZ), jnp.float32) ** shard_levels(key_list[1], (NX, NY, NZ), ((0, 4), (1, 2), (2, 4)), -0.2, 0.2), -1.5, 0.5)
    atom_offsets = draw_atom_offsets(jax.random.fold_in(key_list[6], 71), 0)
    proj_counts = draw_proj_counts(jax.random.fold_in(key_list[6], 71), 0)
    dh_matrix = draw_dh_matrix(jax.random.fold_in(key_list[6], 71), 0)
    ds_matrix = draw_ds_matrix(jax.random.fold_in(key_list[6], 71), 0)
    return dict(wave_bands=wave_bands, potential=potential, atom_offsets=atom_offsets, proj_counts=proj_counts, dh_matrix=dh_matrix, ds_matrix=ds_matrix)


STENCIL = (-49.0 / 18.0, 1.5, -0.15, 1.0 / 90.0)
RELAXATION = 2.0 / 3.0
MASS_SHIFT = 0.25
AMPLITUDE = 0.15
PRECISE = lax.Precision.HIGHEST


def projector_table():
    box_steps = jnp.arange(12, dtype=jnp.float32) - 6.0
    filler = jnp.ones((12, 12, 12), jnp.float32)
    along_x = box_steps[:, None, None] * filler
    along_y = box_steps[None, :, None] * filler
    along_z = box_steps[None, None, :] * filler
    radius_sq = along_x * along_x + along_y * along_y + along_z * along_z
    radial_s = jnp.exp(-radius_sq / 8.0)
    radial_p = jnp.exp(-radius_sq / 9.68) / 2.2
    radial_d = jnp.exp(-radius_sq / 11.52) / 5.76
    angular = [radial_s, radial_p * along_x, radial_p * along_y, radial_p * along_z,
               radial_d * along_x * along_y, radial_d * along_y * along_z, radial_d * along_z * along_x,
               0.5 * radial_d * (along_x * along_x - along_y * along_y),
               radial_d * (3.0 * along_z * along_z - radius_sq) * 0.28867513]
    return AMPLITUDE * jnp.stack(angular).reshape(9, 1728)


def shift_z(field, reach):
    depth = field.shape[-1]
    zeros_rim = jnp.zeros(field.shape[:-1] + (abs(reach),), field.dtype)
    if reach > 0:
        return jnp.concatenate([zeros_rim, field[..., :depth - reach]], axis=-1)
    return jnp.concatenate([field[..., -reach:], zeros_rim], axis=-1)


def kinetic(field):
    laplacian = 3.0 * STENCIL[0] * field
    for reach in (1, 2, 3):
        weight = STENCIL[reach]
        laplacian = laplacian + weight * (jnp.roll(field, reach, 1) + jnp.roll(field, -reach, 1)
                                          + jnp.roll(field, reach, 2) + jnp.roll(field, -reach, 2)
                                          + shift_z(field, reach) + shift_z(field, -reach))
    return -0.5 * laplacian


def projector_terms(field, atom_offsets, proj_counts, dh_matrix, ds_matrix, projector_rows):
    nbands = field.shape[0]
    box_steps = jnp.arange(12, dtype=jnp.int32)
    first_tile = jnp.arange(TILES_X, dtype=jnp.int32)[:, None, None]
    second_tile = jnp.arange(TILES_Y, dtype=jnp.int32)[None, :, None]
    centre_x = (first_tile * CX + atom_offsets[..., 0]).reshape(-1)
    centre_y = (second_tile * CY + atom_offsets[..., 1]).reshape(-1)
    centre_z = atom_offsets[..., 2].reshape(-1)
    cells_x = (centre_x[:, None] - 6 + box_steps[None, :]) % NX
    cells_y = (centre_y[:, None] - 6 + box_steps[None, :]) % NY
    cells_z = centre_z[:, None] - 6 + box_steps[None, :]
    index_x = cells_x[:, :, None, None]
    index_y = cells_y[:, None, :, None]
    index_z = cells_z[:, None, None, :]
    box_values = field[:, index_x, index_y, index_z].reshape(nbands, -1, 1728)
    active = (jnp.arange(NPROJ, dtype=jnp.int32)[None, :] < proj_counts.reshape(-1)[:, None]).astype(jnp.float32)
    intersection = jnp.einsum("ik,bak->aib", projector_rows, box_values, precision=PRECISE) * active[:, :, None]
    dh_flat = dh_matrix.reshape(-1, NPROJ, NPROJ)
    ds_flat = ds_matrix.reshape(-1, NPROJ, NPROJ)
    coefficients = jnp.stack([jnp.einsum("aij,ajb->aib", dh_flat, intersection, precision=PRECISE),
                              jnp.einsum("aij,ajb->aib", ds_flat, intersection, precision=PRECISE)])
    coefficients = coefficients * active[None, :, :, None]
    spread = jnp.einsum("ik,haib->hbak", projector_rows, coefficients, precision=PRECISE)
    spread = spread.reshape(2, nbands, -1, 12, 12, 12)
    correction = jnp.zeros((2,) + field.shape, jnp.float32).at[:, :, index_x, index_y, index_z].add(spread)
    return correction[0], correction[1]


def hamiltonian(field, potential, atom_offsets, proj_counts, dh_matrix, ds_matrix, projector_rows):
    corr_h, corr_s = projector_terms(field, atom_offsets, proj_counts, dh_matrix, ds_matrix, projector_rows)
    return kinetic(field) + potential[None] * field + corr_h, field + corr_s


def level_apply(field, level):
    neighbours = (jnp.roll(field, 1, 1) + jnp.roll(field, -1, 1) + jnp.roll(field, 1, 2) + jnp.roll(field, -1, 2)
                  + shift_z(field, 1) + shift_z(field, -1))
    return -0.5 * (neighbours - 6.0 * field) / 4.0 ** level + MASS_SHIFT * field


def diagonal_of(level):
    return 3.0 / 4.0 ** level + MASS_SHIFT


def relax(field, source, level):
    return field + RELAXATION * (source - level_apply(field, level)) / diagonal_of(level)


def restrict(field):
    nbands, size_x, size_y, size_z = field.shape
    return field.reshape(nbands, size_x // 2, 2, size_y // 2, 2, size_z // 2, 2).mean(axis=(2, 4, 6))


def prolong(field):
    return jnp.repeat(jnp.repeat(jnp.repeat(field, 2, axis=1), 2, axis=2), 2, axis=3)


def precondition(source_zero):
    guess_zero = RELAXATION * source_zero / diagonal_of(0)
    source_one = restrict(source_zero - level_apply(guess_zero, 0))
    guess_one = RELAXATION * source_one / diagonal_of(1)
    source_two = restrict(source_one - level_apply(guess_one, 1))
    guess_two = RELAXATION * source_two / diagonal_of(2)
    for sweep_index in range(COARSE_SWEEPS):
        guess_two = relax(guess_two, source_two, 2)
    guess_one = relax(guess_one + prolong(guess_two), source_one, 1)
    return relax(guess_zero + prolong(guess_one), source_zero, 0)


def reference(wave_bands, potential, atom_offsets, proj_counts, dh_matrix, ds_matrix):
    projector_rows = projector_table()
    h_band, s_band = hamiltonian(wave_bands, potential, atom_offsets, proj_counts, dh_matrix, ds_matrix, projector_rows)
    band_energy = jnp.sum(wave_bands * h_band, axis=(1, 2, 3)) / jnp.sum(wave_bands * s_band, axis=(1, 2, 3))
    energy_grid = band_energy[:, None, None, None]
    residual = h_band - energy_grid * s_band
    direction = precondition(residual)
    h_dir, s_dir = hamiltonian(direction, potential, atom_offsets, proj_counts, dh_matrix, ds_matrix, projector_rows)
    change = h_dir - energy_grid * s_dir
    step_length = -jnp.sum(residual * change, axis=(1, 2, 3)) / jnp.sum(change * change, axis=(1, 2, 3))
    step_grid = step_length[:, None, None, None]
    return wave_bands + step_grid * direction, residual + step_grid * change, band_energy
```

```python
import functools

import jax
import jax.numpy as jnp
from jax import lax
from jax.experimental import pallas as pl
from jax.experimental.pallas import tpu as pltpu
from jax.sharding import PartitionSpec as P

NPROJ = 9
COARSE_SWEEPS = 2


STENCIL = (-49.0 / 18.0, 1.5, -0.15, 1.0 / 90.0)
RELAXATION = 2.0 / 3.0
MASS_SHIFT = 0.25
AMPLITUDE = 0.15
PRECISE = lax.Precision.HIGHEST


def extended(cells, sides, width):
    for axis, dim in sides:
        count = lax.axis_size(axis)
        head = lax.slice_in_dim(cells, 0, width, axis=dim)
        tail = lax.slice_in_dim(cells, cells.shape[dim] - width, cells.shape[dim], axis=dim)
        cells = jnp.concatenate(
            [
                lax.ppermute(tail, axis, [(i, (i + 1) % count) for i in range(count)]),
                cells,
                lax.ppermute(head, axis, [((i + 1) % count, i) for i in range(count)]),
            ],
            axis=dim,
        )
    return cells


def projector_table():
    box_steps = jnp.arange(12, dtype=jnp.float32) - 6.0
    filler = jnp.ones((12, 12, 12), jnp.float32)
    along_x = box_steps[:, None, None] * filler
    along_y = box_steps[None, :, None] * filler
    along_z = box_steps[None, None, :] * filler
    radius_sq = along_x * along_x + along_y * along_y + along_z * along_z
    radial_s = jnp.exp(-radius_sq / 8.0)
    radial_p = jnp.exp(-radius_sq / 9.68) / 2.2
    radial_d = jnp.exp(-radius_sq / 11.52) / 5.76
    angular = [
        radial_s,
        radial_p * along_x,
        radial_p * along_y,
        radial_p * along_z,
        radial_d * along_x * along_y,
        radial_d * along_y * along_z,
        radial_d * along_z * along_x,
        0.5 * radial_d * (along_x * along_x - along_y * along_y),
        radial_d * (3.0 * along_z * along_z - radius_sq) * 0.28867513,
    ]
    return AMPLITUDE * jnp.stack(angular).reshape(9, 1728)


def shift_z(field, reach):
    depth = field.shape[-1]
    zeros_rim = jnp.zeros(field.shape[:-1] + (abs(reach),), field.dtype)
    if reach > 0:
        return jnp.concatenate([zeros_rim, field[..., : depth - reach]], axis=-1)
    return jnp.concatenate([field[..., -reach:], zeros_rim], axis=-1)


def kinetic_padded(padded, width, tile_x, tile_y):
    center = padded[:, width : width + tile_x, width : width + tile_y]
    laplacian = 3.0 * STENCIL[0] * center
    for reach in (1, 2, 3):
        weight = STENCIL[reach]
        laplacian = laplacian + weight * (
            padded[:, width - reach : width - reach + tile_x, width : width + tile_y]
            + padded[:, width + reach : width + reach + tile_x, width : width + tile_y]
            + padded[:, width : width + tile_x, width - reach : width - reach + tile_y]
            + padded[:, width : width + tile_x, width + reach : width + reach + tile_y]
            + shift_z(center, reach)
            + shift_z(center, -reach)
        )
    return -0.5 * laplacian


def box_targets(places, tile_x, tile_y, depth):
    box_steps = jnp.arange(12, dtype=jnp.int32)
    tile_shift = jnp.arange(3, dtype=jnp.int32) - 1
    target_x = (
        tile_shift[:, None, None, None] * tile_x + places[:, :, :, 0][..., None] - 6 + box_steps
    )
    target_y = (
        tile_shift[None, :, None, None] * tile_y + places[:, :, :, 1][..., None] - 6 + box_steps
    )
    target_z = places[:, :, :, 2][..., None] - 6 + box_steps
    target_x = jnp.where((target_x >= 0) & (target_x < tile_x), target_x, tile_x + 12)
    target_y = jnp.where((target_y >= 0) & (target_y < tile_y), target_y, tile_y + 12)
    depth_cells = jnp.arange(depth, dtype=jnp.int32)
    window = (target_z[..., None] == depth_cells).astype(jnp.float32)
    return (target_x, target_y, window)


def own_intersection(widened, atom_offsets, window, projector_rows):
    nbands = widened.shape[0]
    box_steps = jnp.arange(12, dtype=jnp.int32)
    owned = atom_offsets[0, 0]
    index_x = (owned[:, 0:1] + box_steps[None, :])[:, :, None]
    index_y = (owned[:, 1:2] + box_steps[None, :])[:, None, :]
    columns = widened[:, index_x, index_y]
    box_values = jnp.einsum("bauvz,akz->bauvk", columns, window[1, 1], precision=PRECISE)
    box_values = box_values.reshape(nbands, -1, 1728)
    return jnp.einsum("ik,bak->aib", projector_rows, box_values, precision=PRECISE)


def projector_terms(
    intersection, proj_counts, targets, dh_matrix, ds_matrix, projector_rows, field_shape
):
    nbands, tile_x, tile_y, depth = field_shape
    active = (jnp.arange(NPROJ, dtype=jnp.int32)[None, :] < proj_counts[0, 0][:, None]).astype(
        jnp.float32
    )
    intersection = intersection * active[:, :, None]
    coefficients = jnp.stack(
        [
            jnp.einsum("aij,ajb->aib", dh_matrix[0, 0], intersection, precision=PRECISE),
            jnp.einsum("aij,ajb->aib", ds_matrix[0, 0], intersection, precision=PRECISE),
        ]
    )
    coefficients = coefficients * active[None, :, :, None]
    nearby = extended(coefficients[None, None], (("dx", 0), ("dy", 1)), 1)
    spread = jnp.einsum("ik,uvhaib->hbuvak", projector_rows, nearby, precision=PRECISE)
    spread = spread.reshape(2, nbands, 3, 3, -1, 144, 12)
    target_x, target_y, window = targets
    placed = jnp.einsum("hbuvaxk,uvakz->hbuvaxz", spread, window, precision=PRECISE)
    placed = placed.reshape(2, nbands, 3, 3, -1, 12, 12, depth)
    correction = jnp.zeros((2, nbands, tile_x, tile_y, depth), jnp.float32)
    correction = correction.at[:, :, target_x[..., :, None], target_y[..., None, :]].add(
        placed, mode="drop"
    )
    return (correction[0], correction[1])


def hamiltonian(
    field, full_potential, atom_offsets, proj_counts, targets, dh_matrix, ds_matrix, projector_rows
):
    tile_x, tile_y = (field.shape[1], field.shape[2])
    widened = extended(field, (("dx", 1), ("dy", 2)), 6)
    kinetic_part = kinetic_padded(widened, 6, tile_x, tile_y)
    intersection = own_intersection(widened, atom_offsets, targets[2], projector_rows)
    corr_h, corr_s = projector_terms(
        intersection, proj_counts, targets, dh_matrix, ds_matrix, projector_rows, field.shape
    )
    return (kinetic_part + full_potential[None] * field + corr_h, field + corr_s)


def domain_sums(values):
    return lax.psum(values, ("dx", "dy"))


def diagonal_of(level):
    return 3.0 / 4.0**level + MASS_SHIFT


def tile_apply(field, level):
    padded = extended(field, (("dx", 1), ("dy", 2)), 1)
    neighbours = (
        padded[:, :-2, 1:-1]
        + padded[:, 2:, 1:-1]
        + padded[:, 1:-1, :-2]
        + padded[:, 1:-1, 2:]
        + shift_z(field, 1)
        + shift_z(field, -1)
    )
    return -0.5 * (neighbours - 6.0 * field) / 4.0**level + MASS_SHIFT * field


def pair_table(depth):
    fine_cells = jnp.arange(depth, dtype=jnp.int32)[:, None] // 2
    coarse_cells = jnp.arange(depth // 2, dtype=jnp.int32)[None, :]
    return (fine_cells == coarse_cells).astype(jnp.float32)


def restrict(field):
    nbands, size_x, size_y, size_z = field.shape
    planar = field.reshape(nbands, size_x // 2, 2, size_y // 2, 2, size_z).mean(axis=(2, 4))
    return jnp.einsum("bxyz,zw->bxyw", planar, 0.5 * pair_table(size_z), precision=PRECISE)


def prolong(field):
    size_z = field.shape[3]
    widened = jnp.repeat(jnp.repeat(field, 2, axis=1), 2, axis=2)
    return jnp.einsum("bxyw,zw->bxyz", widened, pair_table(2 * size_z), precision=PRECISE)


def precondition(source_zero):
    guess_zero = RELAXATION * source_zero / diagonal_of(0)
    source_one = restrict(source_zero - tile_apply(guess_zero, 0))
    guess_one = RELAXATION * source_one / diagonal_of(1)
    source_two = restrict(source_one - tile_apply(guess_one, 1))
    guess_two = RELAXATION * source_two / diagonal_of(2)
    for sweep_index in range(COARSE_SWEEPS):
        guess_two = guess_two + RELAXATION * (source_two - tile_apply(guess_two, 2)) / diagonal_of(
            2
        )
    guess_one = guess_one + prolong(guess_two)
    guess_one = guess_one + RELAXATION * (source_one - tile_apply(guess_one, 1)) / diagonal_of(1)
    guess_zero = guess_zero + prolong(guess_one)
    return guess_zero + RELAXATION * (source_zero - tile_apply(guess_zero, 0)) / diagonal_of(0)


def distributed(wave_bands, potential, atom_offsets, proj_counts, dh_matrix, ds_matrix):
    projector_rows = projector_table()
    full_potential = lax.all_gather(potential, "band", axis=2, tiled=True)
    places = extended(atom_offsets, (("dx", 0), ("dy", 1)), 1)
    targets = box_targets(places, wave_bands.shape[1], wave_bands.shape[2], wave_bands.shape[3])
    h_band, s_band = hamiltonian(
        wave_bands,
        full_potential,
        atom_offsets,
        proj_counts,
        targets,
        dh_matrix,
        ds_matrix,
        projector_rows,
    )
    energy_sums = domain_sums(
        jnp.stack(
            [
                jnp.sum(wave_bands * h_band, axis=(1, 2, 3)),
                jnp.sum(wave_bands * s_band, axis=(1, 2, 3)),
            ]
        )
    )
    band_energy = energy_sums[0] / energy_sums[1]
    energy_grid = band_energy[:, None, None, None]
    residual = h_band - energy_grid * s_band
    direction = precondition(residual)
    h_dir, s_dir = hamiltonian(
        direction,
        full_potential,
        atom_offsets,
        proj_counts,
        targets,
        dh_matrix,
        ds_matrix,
        projector_rows,
    )
    change = h_dir - energy_grid * s_dir
    line_sums = domain_sums(
        jnp.stack(
            [jnp.sum(residual * change, axis=(1, 2, 3)), jnp.sum(change * change, axis=(1, 2, 3))]
        )
    )
    step_grid = (-line_sums[0] / line_sums[1])[:, None, None, None]
    return (wave_bands + step_grid * direction, residual + step_grid * change, band_energy)


BOX_LOW = 6
BOX_CELLS = 12
BAND_COPIES = 24
LANES = 128
SUBLANES = 8
RADIAL_WIDTHS = (8.0, 9.68, 11.52)
PLANE_FACTORS = (
    (0, 0, 0),
    (1, 1, 0),
    (1, 0, 1),
    (1, 0, 0),
    (2, 1, 1),
    (2, 0, 1),
    (2, 1, 0),
    (2, 2, 0),
    (2, 0, 0),
    (2, 0, 2),
)
D_SCALE = 0.28867513


class Sizes:
    def __init__(self, wave, potential, atoms, tiles_x, tiles_y, groups):
        self.tile_x, self.tile_y, self.depth = wave.shape[1:]
        self.atoms = atoms
        self.tiles_x, self.tiles_y, self.groups = tiles_x, tiles_y, groups
        self.grid_x, self.grid_y = tiles_x * self.tile_x, tiles_y * self.tile_y
        self.cells = self.grid_x * self.grid_y
        self.chunk = potential.shape[2]
        self.all_atoms = tiles_x * tiles_y * atoms
        self.wave_rows = self.tile_x * self.tile_y
        self.pot_rows = self.wave_rows // groups
        self.param_rows = -(-3 * atoms // SUBLANES) * SUBLANES
        self.rows = self.wave_rows + self.pot_rows + self.param_rows
        self.factor_rows = len(PLANE_FACTORS) * self.all_atoms
        self.factor_lanes = -(-self.factor_rows // LANES) * LANES

    def fits(self, vmem_bytes):
        whole = 4 * self.cells * self.depth
        tables = 8 * self.cells * self.factor_lanes
        return (
            self.depth == LANES
            and self.chunk * self.groups == LANES
            and self.tile_x % max(self.groups, 4) == 0
            and self.tile_y % 16 == 0
            and self.grid_x >= BOX_CELLS
            and self.grid_y >= 2 * BOX_CELLS
            and self.cells % LANES == 0
            and self.all_atoms % 16 == 0
            and LANES % self.all_atoms == 0
            and BAND_COPIES * whole + 2 * tables <= vmem_bytes
        )


def bcast_lane(shape):
    return lax.broadcasted_iota(jnp.int32, shape, len(shape) - 1)


def split(value):
    high = value.astype(jnp.bfloat16)
    return high, (value - high.astype(jnp.float32)).astype(jnp.bfloat16)


def dot3(left, right):
    dot = lambda a, b: jnp.dot(a, b, preferred_element_type=jnp.float32)
    return dot(left[0], right[0]) + (dot(left[0], right[1]) + dot(left[1], right[0]))


def pack_kernel(sz, wave_ref, pot_ref, offs_ref, counts_ref, dh_ref, ds_ref, out_ref):
    out_ref[: sz.wave_rows, :] = wave_ref[0].reshape(sz.wave_rows, sz.depth)
    per = sz.tile_x // sz.groups
    pieces = [
        pot_ref[g * per : (g + 1) * per].reshape(sz.pot_rows, sz.chunk)
        for g in range(sz.groups)
    ]
    packed = jnp.concatenate(pieces, axis=1)
    group = lax.axis_index("band")
    out_ref[sz.wave_rows : sz.wave_rows + sz.pot_rows, :] = pltpu.roll(
        packed, group * sz.chunk, 1
    )
    base = sz.wave_rows + sz.pot_rows
    out_ref[base:, :] = jnp.zeros((sz.param_rows, LANES), jnp.float32)
    for j in range(NPROJ):
        lanes = slice(j * NPROJ, (j + 1) * NPROJ)
        for a in range(sz.atoms):
            out_ref[base + a : base + a + 1, lanes] = dh_ref[0, 0, a, j : j + 1, :]
            out_ref[base + sz.atoms + a : base + sz.atoms + a + 1, lanes] = ds_ref[
                0, 0, a, j : j + 1, :
            ]
    lane = bcast_lane((1, LANES))
    for a in range(sz.atoms):
        row = jnp.zeros((1, LANES), jnp.float32)
        for k in range(3):
            row = jnp.where(lane == k, offs_ref[0, 0, a, k].astype(jnp.float32), row)
        row = jnp.where(lane == 3, counts_ref[0, 0, a].astype(jnp.float32), row)
        at = base + 2 * sz.atoms + a
        out_ref[at : at + 1, :] = row


def wrapped(cell, centre, count):
    offset = cell - centre + float(BOX_LOW)
    offset = jnp.where(offset < 0.0, offset + float(count), offset)
    offset = jnp.where(offset >= float(count), offset - float(count), offset)
    inside = offset < float(BOX_CELLS)
    return offset - float(BOX_LOW), inside


def fill_rims(ref, width, count_x, count_y):
    ref[:, 0:SUBLANES, :] = ref[:, count_y : count_y + SUBLANES, :]
    ref[:, count_y + SUBLANES : count_y + 2 * SUBLANES, :] = ref[:, SUBLANES : 2 * SUBLANES, :]
    ref[0:width] = ref[count_x : count_x + width]
    ref[count_x + width : count_x + 2 * width] = ref[width : 2 * width]


def shifted_pair(value, reach):
    lane = bcast_lane((1, LANES))
    below = jnp.where(lane >= reach, pltpu.roll(value, reach, 1), 0.0)
    above = jnp.where(lane < LANES - reach, pltpu.roll(value, LANES - reach, 1), 0.0)
    return below + above


def kinetic_row(ref, width, x, count_y):
    rows = pl.ds(SUBLANES, count_y)
    center = ref[x + width, rows, :]
    total = (-1.5 * STENCIL[0]) * center
    for reach in (1, 2, 3):
        around = (
            ref[x + width - reach, rows, :]
            + ref[x + width + reach, rows, :]
            + ref[x + width, pl.ds(SUBLANES - reach, count_y), :]
            + ref[x + width, pl.ds(SUBLANES + reach, count_y), :]
            + shifted_pair(center, reach)
        )
        total = total + (-0.5 * STENCIL[reach]) * around
    return total


def neighbour_row(ref, x, count_y, step):
    rows = pl.ds(SUBLANES, count_y)
    center = ref[x + 1, rows, :]
    around = (
        ref[x, rows, :]
        + ref[x + 2, rows, :]
        + ref[x + 1, pl.ds(SUBLANES - 1, count_y), :]
        + ref[x + 1, pl.ds(SUBLANES + 1, count_y), :]
        + shifted_pair(center, step)
    )
    return around, center


def loop_x(count, body, unroll=2):
    def step(x, carry):
        body(x)
        return carry

    lax.fori_loop(0, count, step, 0, unroll=unroll)


def plane_weights(sz, meta, w_ref, wt_ref, wx_ref, wy_ref):
    atoms = sz.all_atoms
    widths = [-1.0 / w for w in RADIAL_WIDTHS]
    columns = [meta[:, k : k + 1] for k in range(2)]
    for tile in range(sz.cells // LANES):
        cell = bcast_lane((1, LANES)) + tile * LANES
        cell_x, cell_y = cell // sz.grid_y, cell % sz.grid_y
        rx, inside_x = wrapped(cell_x.astype(jnp.float32), columns[0], sz.grid_x)
        ry, inside_y = wrapped(cell_y.astype(jnp.float32), columns[1], sz.grid_y)
        square = rx * rx + ry * ry
        inside = jnp.logical_and(inside_x, inside_y)
        radial = [jnp.where(inside, jnp.exp(square * w), 0.0) for w in widths]
        powers_x, powers_y = [None, rx, rx * rx], [None, ry, ry * ry]
        for index, (kind, px, py) in enumerate(PLANE_FACTORS):
            value = radial[kind]
            value = value if px == 0 else value * powers_x[px]
            value = value if py == 0 else value * powers_y[py]
            high, low = split(value)
            rows, lanes = slice(index * atoms, (index + 1) * atoms), slice(tile * LANES, (tile + 1) * LANES)
            w_ref[0, rows, lanes] = high
            w_ref[1, rows, lanes] = low
    turned = jnp.concatenate([meta] * (LANES // atoms), axis=0).T
    for axis, count, ref in ((0, sz.grid_x, wx_ref), (1, sz.grid_y, wy_ref)):
        centre = turned[axis : axis + 1, :]
        cell = lax.broadcasted_iota(jnp.int32, (count, LANES), 0).astype(jnp.float32)
        offset, inside = wrapped(cell, centre, count)
        radial = [jnp.where(inside, jnp.exp(offset * offset * w), 0.0) for w in widths]
        powers = [1.0, offset, offset * offset]
        for tile in range(sz.factor_lanes // LANES):
            factor = bcast_lane((1, LANES)) // atoms + tile * (LANES // atoms)
            value = jnp.zeros((count, LANES), jnp.float32)
            for index, (kind, *power) in enumerate(PLANE_FACTORS):
                if index * atoms // LANES == tile:
                    value = jnp.where(factor == index, radial[kind] * powers[power[axis]], value)
            ref[:, tile * LANES : (tile + 1) * LANES] = value

    def plane(x):
        high, low = split(wx_ref[pl.ds(x, 1), :] * wy_ref[...])
        rows = pl.ds(pl.multiple_of(x * sz.grid_y, 16), sz.grid_y)
        wt_ref[0, rows, :] = high
        wt_ref[1, rows, :] = low

    loop_x(sz.grid_x, plane)


def depth_weights(sz, meta, wz_ref):
    cell = bcast_lane((1, LANES)).astype(jnp.float32)
    offset = cell - meta[:, 2:3]
    inside = jnp.logical_and(offset >= -float(BOX_LOW), offset < float(BOX_CELLS - BOX_LOW))
    radial = [
        jnp.where(inside, (AMPLITUDE * scale) * jnp.exp(offset * offset * (-1.0 / w)), 0.0)
        for scale, w in zip((1.0, 1.0 / 2.2, 1.0 / 5.76), RADIAL_WIDTHS)
    ]
    wz_ref[0] = radial[0]
    wz_ref[1] = radial[1]
    wz_ref[2] = radial[1] * offset
    wz_ref[3] = radial[2]
    wz_ref[4] = radial[2] * offset
    wz_ref[5] = radial[2] * (offset * offset)


def intersections(sz, w_ref, field, wz_ref, active):
    sums = dot3((w_ref[0], w_ref[1]), field)
    u = [sums[c * sz.all_atoms : (c + 1) * sz.all_atoms] for c in range(len(PLANE_FACTORS))]
    wide = u[7] + u[9]
    products = [
        u[0] * wz_ref[0],
        u[1] * wz_ref[1],
        u[2] * wz_ref[1],
        u[3] * wz_ref[2],
        u[4] * wz_ref[3],
        u[5] * wz_ref[4],
        u[6] * wz_ref[4],
        (0.5 * (u[7] - u[9])) * wz_ref[3],
        D_SCALE * (2.0 * u[8] * wz_ref[5] - wide * wz_ref[3]),
    ]
    return [jnp.sum(p, axis=1, keepdims=True) * active[i] for i, p in enumerate(products)]


def active_columns(meta):
    return [(meta[:, 3:4] > float(i)).astype(jnp.float32) for i in range(NPROJ)]


def spread_lanes(columns):
    lane = bcast_lane((1, LANES))
    inner = jnp.zeros((columns[0].shape[0], LANES), jnp.float32)
    outer = inner
    for k in range(NPROJ):
        inner = jnp.where(jnp.logical_and(lane % NPROJ == k, lane < NPROJ * NPROJ), columns[k], inner)
        outer = jnp.where(lane // NPROJ == k, columns[k], outer)
    return inner, outer


def correction(sz, matrix, inner, active, wz_ref, wt_ref, out_ref):
    lane = bcast_lane((1, LANES))
    terms = matrix * inner
    coef = [
        jnp.sum(jnp.where(lane // NPROJ == i, terms, 0.0), axis=1, keepdims=True) * active[i]
        for i in range(NPROJ)
    ]
    tilt = (0.5 * coef[7]) * wz_ref[3]
    ring = (D_SCALE * coef[8]) * wz_ref[3]
    blocks = [
        coef[0] * wz_ref[0],
        coef[1] * wz_ref[1],
        coef[2] * wz_ref[1],
        coef[3] * wz_ref[2],
        coef[4] * wz_ref[3],
        coef[5] * wz_ref[4],
        coef[6] * wz_ref[4],
        tilt - ring,
        (2.0 * D_SCALE * coef[8]) * wz_ref[5],
        -(tilt + ring),
    ]
    spare = sz.factor_lanes - sz.factor_rows
    if spare:
        blocks.append(jnp.zeros((spare, LANES), jnp.float32))
    right = split(jnp.concatenate(blocks, axis=0))
    out_ref[...] = dot3((wt_ref[0], wt_ref[1]), right)


def first_kernel(sz, *refs):
    blocks = refs[: sz.tiles_x * sz.tiles_y]
    (psi, kin, w_ref, wt_ref, wz_ref, par_ref, sums_ref, parts_ref, wx_ref, wy_ref) = refs[len(blocks) :]
    here_x, here_y = lax.axis_index("dx"), lax.axis_index("dy")
    base = sz.wave_rows + sz.pot_rows
    for index, block in enumerate(blocks):
        shift_y, shift_x = divmod(index, sz.tiles_x)
        tile_x = lax.rem(here_x + shift_x, sz.tiles_x)
        tile_y = lax.rem(here_y + shift_y, sz.tiles_y)
        at_y = pl.multiple_of(tile_y * sz.tile_y, 16)
        for x in range(sz.tile_x):
            value = block[x * sz.tile_y : (x + 1) * sz.tile_y, :]
            cell_x = tile_x * sz.tile_x + x
            psi[cell_x + 3, pl.ds(at_y + SUBLANES, sz.tile_y), :] = value
            rows = pl.ds(pl.multiple_of(cell_x * sz.grid_y + at_y, 16), sz.tile_y)
            high, low = split(value)
            parts_ref[0, rows, :] = high
            parts_ref[1, rows, :] = low
        tile = tile_x * sz.tiles_y + tile_y
        for k in range(3):
            par_ref[k, pl.ds(tile * sz.atoms, sz.atoms), :] = block[
                base + k * sz.atoms : base + (k + 1) * sz.atoms, :
            ]
    fill_rims(psi, 3, sz.grid_x, sz.grid_y)
    owners = lax.broadcasted_iota(jnp.int32, (sz.all_atoms, LANES), 0) // sz.atoms
    lane = bcast_lane((sz.all_atoms, LANES))
    meta = par_ref[2]
    meta = meta + jnp.where(lane == 0, (owners // sz.tiles_y * sz.tile_x).astype(jnp.float32), 0.0)
    meta = meta + jnp.where(lane == 1, (owners % sz.tiles_y * sz.tile_y).astype(jnp.float32), 0.0)
    par_ref[2] = meta
    plane_weights(sz, meta, w_ref, wt_ref, wx_ref, wy_ref)
    depth_weights(sz, meta, wz_ref)
    columns = intersections(sz, w_ref, (parts_ref[0], parts_ref[1]), wz_ref, active_columns(meta))
    inner, outer = spread_lanes(columns)
    par_ref[3] = inner
    pair = inner * outer

    def plane(x, carry):
        energy, norm = carry
        center = psi[x + 3, pl.ds(SUBLANES, sz.grid_y), :]
        value = kinetic_row(psi, 3, x, sz.grid_y)
        kin[x] = value
        return energy + value * center, norm + center * center

    zero = jnp.zeros((sz.grid_y, LANES), jnp.float32)
    energy, norm = lax.fori_loop(0, sz.grid_x, plane, (zero, zero), unroll=2)
    fold = lambda v: jnp.sum(v, axis=0, keepdims=True)
    sums_ref[0:1, :] = fold(energy) + fold(par_ref[0] * pair)
    sums_ref[1:2, :] = fold(norm) + fold(par_ref[1] * pair)


def half_rows(ref, value, count):
    ref[0:count, :] = value
    return ref[pl.ds(0, count // 2, stride=2), :] + ref[pl.ds(1, count // 2, stride=2), :]


def pair_lanes(value, step):
    lane = bcast_lane((1, LANES))
    other = jnp.where(
        (lane // step) % 2 == 1, pltpu.roll(value, step, 1), pltpu.roll(value, LANES - step, 1)
    )
    return value + other


def level_numbers(level):
    return 0.5 / 4.0**level, RELAXATION / diagonal_of(level)


def restrict_into(sz_x, sz_y, level, source, target, rows_ref):
    spread, guess = level_numbers(level)

    def plane(x):
        total = None
        for part in range(2):
            around, center = neighbour_row(source, 2 * x + part, sz_y, 2**level)
            value = (1.0 - RELAXATION) * center + (spread * guess) * around
            total = value if total is None else total + value
        target[x + 1, pl.ds(SUBLANES, sz_y // 2), :] = 0.125 * pair_lanes(
            half_rows(rows_ref, total, sz_y), 2**level
        )

    loop_x(sz_x // 2, plane)
    fill_rims(target, 1, sz_x // 2, sz_y // 2)


def relax_rows(sz_x, sz_y, level, guess_ref, source, emit):
    spread, guess = level_numbers(level)

    def plane(x):
        around, center = neighbour_row(guess_ref, x, sz_y, 2**level)
        right = source[x + 1, pl.ds(SUBLANES, sz_y), :]
        emit(x, (1.0 - RELAXATION) * center + guess * right + (guess * spread) * around)

    loop_x(sz_x, plane)


def prolong_into(sz_x, sz_y, level, coarse, source, target):
    guess = level_numbers(level)[1]

    def plane(x):
        value = coarse[x]
        for part in range(2):
            at = 2 * x + part + 1
            target[at, pl.ds(SUBLANES, sz_y // 2, stride=2), :] = value
            target[at, pl.ds(SUBLANES + 1, sz_y // 2, stride=2), :] = value
            rows = pl.ds(SUBLANES, sz_y)
            target[at, rows, :] = target[at, rows, :] + guess * source[at, rows, :]

    loop_x(sz_x // 2, plane)
    fill_rims(target, 1, sz_x, sz_y)


def second_kernel(sz, *refs):
    pots = refs[: sz.groups * sz.tiles_y]
    (psi, kin, w_ref, wt_ref, wz_ref, par_ref, sums_ref, bands_ref, resid_ref, energy_ref) = refs[len(pots) : len(pots) + 10]
    (pot, corr, res, zfield, direct, change, b1, z1, x1, b2, x2, rows_ref, parts_ref) = refs[len(pots) + 10 :]
    nx, ny = sz.grid_x, sz.grid_y
    here_x, here_y = lax.axis_index("dx"), lax.axis_index("dy")
    here_group = lax.axis_index("band")
    per = sz.tile_x // sz.groups
    slot = bcast_lane((1, LANES)) // sz.chunk
    for shift_y in range(sz.tiles_y):
        tile_y = lax.rem(here_y + shift_y, sz.tiles_y)
        at_y = pl.multiple_of(tile_y * sz.tile_y, 16)
        for shift_x in range(sz.tiles_x):
            tile_x = lax.rem(here_x + shift_x, sz.tiles_x)
            for g in range(sz.groups):
                value = None
                for shift_b in range(sz.groups):
                    source = lax.rem(here_group + shift_b, sz.groups)
                    piece = pots[shift_y * sz.groups + shift_b][
                        shift_x * sz.pot_rows : (shift_x + 1) * sz.pot_rows, :
                    ]
                    chosen = slot == lax.rem(source + g, sz.groups)
                    value = piece if value is None else jnp.where(chosen, piece, value)
                if g:
                    value = pltpu.roll(value, LANES - g * sz.chunk, 1)
                for k in range(per):
                    pot[tile_x * sz.tile_x + g * per + k, pl.ds(at_y, sz.tile_y), :] = value[
                        k * sz.tile_y : (k + 1) * sz.tile_y
                    ]

    def weigh(x, total):
        center = psi[x + 3, pl.ds(SUBLANES, ny), :]
        return total + pot[x] * (center * center)

    total = lax.fori_loop(0, nx, weigh, jnp.zeros((ny, LANES), jnp.float32), unroll=2)
    energy = (jnp.sum(total) + jnp.sum(sums_ref[0:1, :])) / jnp.sum(sums_ref[1:2, :])
    energy_ref[0] = energy
    meta = par_ref[2]
    active = active_columns(meta)
    matrix = par_ref[0] - energy * par_ref[1]
    correction(sz, matrix, par_ref[3], active, wz_ref, wt_ref, corr)

    def residual(x):
        center = psi[x + 3, pl.ds(SUBLANES, ny), :]
        rows = pl.ds(pl.multiple_of(x * ny, 16), ny)
        res[x + 1, pl.ds(SUBLANES, ny), :] = kin[x] + (pot[x] - energy) * center + corr[rows, :]

    loop_x(nx, residual)
    fill_rims(res, 1, nx, ny)
    restrict_into(nx, ny, 0, res, b1, rows_ref)
    restrict_into(nx // 2, ny // 2, 1, b1, b2, rows_ref)
    guess = level_numbers(2)[1]
    x2[...] = guess * b2[...]
    quarter_x, quarter_y = nx // 4, ny // 4
    for sweep in range(COARSE_SWEEPS):
        planes = []
        spread = level_numbers(2)[0]
        for x in range(quarter_x):
            around, center = neighbour_row(x2, x, quarter_y, 4)
            right = b2[x + 1, pl.ds(SUBLANES, quarter_y), :]
            planes.append((1.0 - RELAXATION) * center + guess * right + (guess * spread) * around)
        for x in range(quarter_x):
            x2[x + 1, pl.ds(SUBLANES, quarter_y), :] = planes[x]
        fill_rims(x2, 1, quarter_x, quarter_y)

    class Planes:
        def __init__(self, ref, rows):
            self.ref, self.rows = ref, rows

        def __getitem__(self, x):
            return self.ref[x + 1, pl.ds(SUBLANES, self.rows), :]

    prolong_into(nx // 2, ny // 2, 1, Planes(x2, quarter_y), b1, z1)

    def emit_one(x, value):
        x1[x] = value

    relax_rows(nx // 2, ny // 2, 1, z1, b1, emit_one)
    prolong_into(nx, ny, 0, x1, res, zfield)

    def emit_zero(x, value):
        direct[x + 3, pl.ds(SUBLANES, ny), :] = value
        rows = pl.ds(pl.multiple_of(x * ny, 16), ny)
        high, low = split(value)
        parts_ref[0, rows, :] = high
        parts_ref[1, rows, :] = low

    relax_rows(nx, ny, 0, zfield, res, emit_zero)
    fill_rims(direct, 3, nx, ny)
    columns = intersections(sz, w_ref, (parts_ref[0], parts_ref[1]), wz_ref, active)
    correction(sz, matrix, spread_lanes(columns)[0], active, wz_ref, wt_ref, corr)

    def line(x, carry):
        over, under = carry
        center = direct[x + 3, pl.ds(SUBLANES, ny), :]
        rows = pl.ds(pl.multiple_of(x * ny, 16), ny)
        value = kinetic_row(direct, 3, x, ny) + (pot[x] - energy) * center + corr[rows, :]
        change[x] = value
        return over + value * res[x + 1, pl.ds(SUBLANES, ny), :], under + value * value

    zero = jnp.zeros((ny, LANES), jnp.float32)
    over, under = lax.fori_loop(0, nx, line, (zero, zero), unroll=2)
    step = -jnp.sum(over) / jnp.sum(under)
    at_x, at_y = here_x * sz.tile_x, pl.multiple_of(here_y * sz.tile_y, 16)
    for x in range(sz.tile_x):
        cell = at_x + x
        inner = pl.ds(at_y + SUBLANES, sz.tile_y)
        bands_ref[0, x] = psi[cell + 3, inner, :] + step * direct[cell + 3, inner, :]
        resid_ref[0, x] = res[cell + 1, inner, :] + step * change[cell, pl.ds(at_y, sz.tile_y), :]


def from_shift(value, axis, shift):
    count = lax.axis_size(axis)
    return lax.ppermute(value, axis, [((i + shift) % count, i) for i in range(count)])


def replicated(sz, wave_bands, potential, atom_offsets, proj_counts, dh_matrix, ds_matrix):
    vmem = pl.BlockSpec(memory_space=pltpu.VMEM)
    smem = pl.BlockSpec(memory_space=pltpu.SMEM)
    shape = lambda *dims: jax.ShapeDtypeStruct(dims, jnp.float32)
    half = lambda *dims: jax.ShapeDtypeStruct(dims, jnp.bfloat16)
    own = pl.pallas_call(
        functools.partial(pack_kernel, sz),
        out_shape=shape(sz.rows, LANES),
        in_specs=[vmem, vmem, smem, smem, vmem, vmem],
        out_specs=vmem,
        name="pack",
    )(wave_bands, potential, atom_offsets, proj_counts, dh_matrix, ds_matrix)
    line = [own] + [from_shift(own, "dx", s) for s in range(1, sz.tiles_x)]
    blocks = list(line)
    for s in range(1, sz.tiles_y):
        blocks += [from_shift(block, "dy", s) for block in line]
    chunk = jnp.concatenate(
        [block[sz.wave_rows : sz.wave_rows + sz.pot_rows] for block in line], axis=0
    )
    chunks = [chunk] + [from_shift(chunk, "band", s) for s in range(1, sz.groups)]
    pots = list(chunks)
    for s in range(1, sz.tiles_y):
        pots += [from_shift(piece, "dy", s) for piece in chunks]
    nx, ny = sz.grid_x, sz.grid_y
    padded = lambda x, y, width: (x + 2 * width, y + 2 * SUBLANES, LANES)
    made = pl.pallas_call(
        functools.partial(first_kernel, sz),
        out_shape=(
            shape(*padded(nx, ny, 3)),
            shape(nx, ny, LANES),
            half(2, sz.factor_rows, sz.cells),
            half(2, sz.cells, sz.factor_lanes),
            shape(6, sz.all_atoms, LANES),
            shape(4, sz.all_atoms, LANES),
            shape(2, LANES),
        ),
        in_specs=[vmem] * len(blocks),
        out_specs=(vmem,) * 7,
        scratch_shapes=[
            pltpu.VMEM((2, sz.cells, LANES), jnp.bfloat16),
            pltpu.VMEM((nx, sz.factor_lanes), jnp.float32),
            pltpu.VMEM((ny, sz.factor_lanes), jnp.float32),
        ],
        name="first",
    )(*blocks)
    scratch = lambda *dims: pltpu.VMEM(dims, jnp.float32)
    return pl.pallas_call(
        functools.partial(second_kernel, sz),
        out_shape=(
            jax.ShapeDtypeStruct(wave_bands.shape, jnp.float32),
            jax.ShapeDtypeStruct(wave_bands.shape, jnp.float32),
            shape(1),
        ),
        in_specs=[vmem] * (len(pots) + len(made)),
        out_specs=(vmem, vmem, smem),
        scratch_shapes=[
            scratch(nx, ny, LANES),
            scratch(sz.cells, LANES),
            scratch(*padded(nx, ny, 1)),
            scratch(*padded(nx, ny, 1)),
            scratch(*padded(nx, ny, 3)),
            scratch(nx, ny, LANES),
            scratch(*padded(nx // 2, ny // 2, 1)),
            scratch(*padded(nx // 2, ny // 2, 1)),
            scratch(nx // 2, ny // 2, LANES),
            scratch(*padded(nx // 4, ny // 4, 1)),
            scratch(*padded(nx // 4, ny // 4, 1)),
            scratch(ny, LANES),
            pltpu.VMEM((2, sz.cells, LANES), jnp.bfloat16),
        ],
        name="second",
    )(*pots, *made)


VMEM_BUDGET = 48 * 1024 * 1024


def on_device(wave_bands, potential, atom_offsets, proj_counts, dh_matrix, ds_matrix):
    sz = Sizes(
        wave_bands,
        potential,
        proj_counts.shape[2],
        lax.axis_size("dx"),
        lax.axis_size("dy"),
        lax.axis_size("band"),
    )
    step = functools.partial(replicated, sz) if sz.fits(VMEM_BUDGET) else distributed
    return step(wave_bands, potential, atom_offsets, proj_counts, dh_matrix, ds_matrix)


def solution(mesh):
    return jax.shard_map(
        on_device,
        mesh=mesh,
        in_specs=(
            P("band", "dx", "dy", None),
            P("dx", "dy", "band"),
            P("dx", "dy", None, None),
            P("dx", "dy", None),
            P("dx", "dy", None, None, None),
            P("dx", "dy", None, None, None),
        ),
        out_specs=(P("band", "dx", "dy", None), P("band", "dx", "dy", None), P("band")),
        check_vma=False,
    )
```

```python
import functools

import jax
import jax.numpy as jnp
from jax import lax
from jax.experimental import pallas as pl
from jax.experimental.pallas import tpu as pltpu
from jax.sharding import PartitionSpec as P

NPROJ = 9
COARSE_SWEEPS = 2


STENCIL = (-49.0 / 18.0, 1.5, -0.15, 1.0 / 90.0)
RELAXATION = 2.0 / 3.0
MASS_SHIFT = 0.25
AMPLITUDE = 0.15
PRECISE = lax.Precision.HIGHEST


def extended(cells, sides, width):
    for axis, dim in sides:
        count = lax.axis_size(axis)
        head = lax.slice_in_dim(cells, 0, width, axis=dim)
        tail = lax.slice_in_dim(cells, cells.shape[dim] - width, cells.shape[dim], axis=dim)
        cells = jnp.concatenate(
            [
                lax.ppermute(tail, axis, [(i, (i + 1) % count) for i in range(count)]),
                cells,
                lax.ppermute(head, axis, [((i + 1) % count, i) for i in range(count)]),
            ],
            axis=dim,
        )
    return cells


def projector_table():
    box_steps = jnp.arange(12, dtype=jnp.float32) - 6.0
    filler = jnp.ones((12, 12, 12), jnp.float32)
    along_x = box_steps[:, None, None] * filler
    along_y = box_steps[None, :, None] * filler
    along_z = box_steps[None, None, :] * filler
    radius_sq = along_x * along_x + along_y * along_y + along_z * along_z
    radial_s = jnp.exp(-radius_sq / 8.0)
    radial_p = jnp.exp(-radius_sq / 9.68) / 2.2
    radial_d = jnp.exp(-radius_sq / 11.52) / 5.76
    angular = [
        radial_s,
        radial_p * along_x,
        radial_p * along_y,
        radial_p * along_z,
        radial_d * along_x * along_y,
        radial_d * along_y * along_z,
        radial_d * along_z * along_x,
        0.5 * radial_d * (along_x * along_x - along_y * along_y),
        radial_d * (3.0 * along_z * along_z - radius_sq) * 0.28867513,
    ]
    return AMPLITUDE * jnp.stack(angular).reshape(9, 1728)


def shift_z(field, reach):
    depth = field.shape[-1]
    zeros_rim = jnp.zeros(field.shape[:-1] + (abs(reach),), field.dtype)
    if reach > 0:
        return jnp.concatenate([zeros_rim, field[..., : depth - reach]], axis=-1)
    return jnp.concatenate([field[..., -reach:], zeros_rim], axis=-1)


def kinetic_padded(padded, width, tile_x, tile_y):
    center = padded[:, width : width + tile_x, width : width + tile_y]
    laplacian = 3.0 * STENCIL[0] * center
    for reach in (1, 2, 3):
        weight = STENCIL[reach]
        laplacian = laplacian + weight * (
            padded[:, width - reach : width - reach + tile_x, width : width + tile_y]
            + padded[:, width + reach : width + reach + tile_x, width : width + tile_y]
            + padded[:, width : width + tile_x, width - reach : width - reach + tile_y]
            + padded[:, width : width + tile_x, width + reach : width + reach + tile_y]
            + shift_z(center, reach)
            + shift_z(center, -reach)
        )
    return -0.5 * laplacian


def box_targets(places, tile_x, tile_y, depth):
    box_steps = jnp.arange(12, dtype=jnp.int32)
    tile_shift = jnp.arange(3, dtype=jnp.int32) - 1
    target_x = (
        tile_shift[:, None, None, None] * tile_x + places[:, :, :, 0][..., None] - 6 + box_steps
    )
    target_y = (
        tile_shift[None, :, None, None] * tile_y + places[:, :, :, 1][..., None] - 6 + box_steps
    )
    target_z = places[:, :, :, 2][..., None] - 6 + box_steps
    target_x = jnp.where((target_x >= 0) & (target_x < tile_x), target_x, tile_x + 12)
    target_y = jnp.where((target_y >= 0) & (target_y < tile_y), target_y, tile_y + 12)
    depth_cells = jnp.arange(depth, dtype=jnp.int32)
    window = (target_z[..., None] == depth_cells).astype(jnp.float32)
    return (target_x, target_y, window)


def own_intersection(widened, atom_offsets, window, projector_rows):
    nbands = widened.shape[0]
    box_steps = jnp.arange(12, dtype=jnp.int32)
    owned = atom_offsets[0, 0]
    index_x = (owned[:, 0:1] + box_steps[None, :])[:, :, None]
    index_y = (owned[:, 1:2] + box_steps[None, :])[:, None, :]
    columns = widened[:, index_x, index_y]
    box_values = jnp.einsum("bauvz,akz->bauvk", columns, window[1, 1], precision=PRECISE)
    box_values = box_values.reshape(nbands, -1, 1728)
    return jnp.einsum("ik,bak->aib", projector_rows, box_values, precision=PRECISE)


def projector_terms(
    intersection, proj_counts, targets, dh_matrix, ds_matrix, projector_rows, field_shape
):
    nbands, tile_x, tile_y, depth = field_shape
    active = (jnp.arange(NPROJ, dtype=jnp.int32)[None, :] < proj_counts[0, 0][:, None]).astype(
        jnp.float32
    )
    intersection = intersection * active[:, :, None]
    coefficients = jnp.stack(
        [
            jnp.einsum("aij,ajb->aib", dh_matrix[0, 0], intersection, precision=PRECISE),
            jnp.einsum("aij,ajb->aib", ds_matrix[0, 0], intersection, precision=PRECISE),
        ]
    )
    coefficients = coefficients * active[None, :, :, None]
    nearby = extended(coefficients[None, None], (("dx", 0), ("dy", 1)), 1)
    spread = jnp.einsum("ik,uvhaib->hbuvak", projector_rows, nearby, precision=PRECISE)
    spread = spread.reshape(2, nbands, 3, 3, -1, 144, 12)
    target_x, target_y, window = targets
    placed = jnp.einsum("hbuvaxk,uvakz->hbuvaxz", spread, window, precision=PRECISE)
    placed = placed.reshape(2, nbands, 3, 3, -1, 12, 12, depth)
    correction = jnp.zeros((2, nbands, tile_x, tile_y, depth), jnp.float32)
    correction = correction.at[:, :, target_x[..., :, None], target_y[..., None, :]].add(
        placed, mode="drop"
    )
    return (correction[0], correction[1])


def hamiltonian(
    field, full_potential, atom_offsets, proj_counts, targets, dh_matrix, ds_matrix, projector_rows
):
    tile_x, tile_y = (field.shape[1], field.shape[2])
    widened = extended(field, (("dx", 1), ("dy", 2)), 6)
    kinetic_part = kinetic_padded(widened, 6, tile_x, tile_y)
    intersection = own_intersection(widened, atom_offsets, targets[2], projector_rows)
    corr_h, corr_s = projector_terms(
        intersection, proj_counts, targets, dh_matrix, ds_matrix, projector_rows, field.shape
    )
    return (kinetic_part + full_potential[None] * field + corr_h, field + corr_s)


def domain_sums(values):
    return lax.psum(values, ("dx", "dy"))


def diagonal_of(level):
    return 3.0 / 4.0**level + MASS_SHIFT


def tile_apply(field, level):
    padded = extended(field, (("dx", 1), ("dy", 2)), 1)
    neighbours = (
        padded[:, :-2, 1:-1]
        + padded[:, 2:, 1:-1]
        + padded[:, 1:-1, :-2]
        + padded[:, 1:-1, 2:]
        + shift_z(field, 1)
        + shift_z(field, -1)
    )
    return -0.5 * (neighbours - 6.0 * field) / 4.0**level + MASS_SHIFT * field


def pair_table(depth):
    fine_cells = jnp.arange(depth, dtype=jnp.int32)[:, None] // 2
    coarse_cells = jnp.arange(depth // 2, dtype=jnp.int32)[None, :]
    return (fine_cells == coarse_cells).astype(jnp.float32)


def restrict(field):
    nbands, size_x, size_y, size_z = field.shape
    planar = field.reshape(nbands, size_x // 2, 2, size_y // 2, 2, size_z).mean(axis=(2, 4))
    return jnp.einsum("bxyz,zw->bxyw", planar, 0.5 * pair_table(size_z), precision=PRECISE)


def prolong(field):
    size_z = field.shape[3]
    widened = jnp.repeat(jnp.repeat(field, 2, axis=1), 2, axis=2)
    return jnp.einsum("bxyw,zw->bxyz", widened, pair_table(2 * size_z), precision=PRECISE)


def precondition(source_zero):
    guess_zero = RELAXATION * source_zero / diagonal_of(0)
    source_one = restrict(source_zero - tile_apply(guess_zero, 0))
    guess_one = RELAXATION * source_one / diagonal_of(1)
    source_two = restrict(source_one - tile_apply(guess_one, 1))
    guess_two = RELAXATION * source_two / diagonal_of(2)
    for sweep_index in range(COARSE_SWEEPS):
        guess_two = guess_two + RELAXATION * (source_two - tile_apply(guess_two, 2)) / diagonal_of(
            2
        )
    guess_one = guess_one + prolong(guess_two)
    guess_one = guess_one + RELAXATION * (source_one - tile_apply(guess_one, 1)) / diagonal_of(1)
    guess_zero = guess_zero + prolong(guess_one)
    return guess_zero + RELAXATION * (source_zero - tile_apply(guess_zero, 0)) / diagonal_of(0)


def distributed(wave_bands, potential, atom_offsets, proj_counts, dh_matrix, ds_matrix):
    projector_rows = projector_table()
    full_potential = lax.all_gather(potential, "band", axis=2, tiled=True)
    places = extended(atom_offsets, (("dx", 0), ("dy", 1)), 1)
    targets = box_targets(places, wave_bands.shape[1], wave_bands.shape[2], wave_bands.shape[3])
    h_band, s_band = hamiltonian(
        wave_bands,
        full_potential,
        atom_offsets,
        proj_counts,
        targets,
        dh_matrix,
        ds_matrix,
        projector_rows,
    )
    energy_sums = domain_sums(
        jnp.stack(
            [
                jnp.sum(wave_bands * h_band, axis=(1, 2, 3)),
                jnp.sum(wave_bands * s_band, axis=(1, 2, 3)),
            ]
        )
    )
    band_energy = energy_sums[0] / energy_sums[1]
    energy_grid = band_energy[:, None, None, None]
    residual = h_band - energy_grid * s_band
    direction = precondition(residual)
    h_dir, s_dir = hamiltonian(
        direction,
        full_potential,
        atom_offsets,
        proj_counts,
        targets,
        dh_matrix,
        ds_matrix,
        projector_rows,
    )
    change = h_dir - energy_grid * s_dir
    line_sums = domain_sums(
        jnp.stack(
            [jnp.sum(residual * change, axis=(1, 2, 3)), jnp.sum(change * change, axis=(1, 2, 3))]
        )
    )
    step_grid = (-line_sums[0] / line_sums[1])[:, None, None, None]
    return (wave_bands + step_grid * direction, residual + step_grid * change, band_energy)


BOX_LOW = 6
BOX_CELLS = 12
LANES = 128
SUBLANES = 8
RADIAL_WIDTHS = (8.0, 9.68, 11.52)
PLANE_FACTORS = (
    (0, 0, 0),
    (1, 1, 0),
    (1, 0, 1),
    (1, 0, 0),
    (2, 1, 1),
    (2, 0, 1),
    (2, 1, 0),
    (2, 2, 0),
    (2, 0, 0),
    (2, 0, 2),
)
D_SCALE = 0.28867513
DEPTH_SCALE = 180.0
BLOCK = 8
VMEM_BUDGET = 40 * 1024 * 1024
VMEM_GRANT = 24 * 1024 * 1024


class Sizes:
    def __init__(self, wave, potential, atoms, tiles_x, tiles_y, groups):
        self.tile_x, self.tile_y, self.depth = wave.shape[1:]
        self.atoms = atoms
        self.tiles_x, self.tiles_y, self.groups = tiles_x, tiles_y, groups
        self.grid_x, self.grid_y = tiles_x * self.tile_x, tiles_y * self.tile_y
        self.cells = self.grid_x * self.grid_y
        self.chunk = potential.shape[2]
        self.all_atoms = tiles_x * tiles_y * atoms
        self.wave_rows = self.tile_x * self.tile_y
        self.pot_rows = self.wave_rows // groups
        self.param_rows = -(-2 * atoms // SUBLANES) * SUBLANES
        self.rows = self.wave_rows + self.pot_rows + self.param_rows
        self.factors = len(PLANE_FACTORS) * self.all_atoms

    def fits(self, vmem_bytes):
        return (
            self.depth == LANES
            and self.chunk * self.groups == LANES
            and self.tile_x % max(self.groups, BLOCK) == 0
            and self.tile_y % 16 == 0
            and self.grid_x >= 2 * BLOCK
            and self.grid_y >= 32
            and self.all_atoms % 16 == 0
            and LANES % self.all_atoms == 0
            and self.cells * (60 * LANES + 8 * self.factors) <= vmem_bytes
        )


def lanes_of(rows=1):
    return lax.broadcasted_iota(jnp.int32, (rows, LANES), 1)


def split(value):
    high = value.astype(jnp.bfloat16)
    return high, (value - high.astype(jnp.float32)).astype(jnp.bfloat16)


def halves(value):
    return value[:, :LANES] + value[:, LANES:]


def dot(left, right):
    return jnp.dot(left, right, preferred_element_type=jnp.float32)


META_LANE = 96


def pack_kernel(sz, wave_ref, pot_ref, offs_ref, counts_ref, dh_ref, ds_ref, out_ref, *scratch):
    pot, offs, counts, dh, ds, sems = scratch
    base = sz.wave_rows + sz.pot_rows
    pairs = [
        (pot_ref, pot),
        (offs_ref, offs),
        (counts_ref, counts),
        (dh_ref, dh),
        (ds_ref, ds),
        (wave_ref, out_ref.at[pl.ds(0, sz.wave_rows)]),
    ]
    copies = [pltpu.make_async_copy(a, b, sems.at[i]) for i, (a, b) in enumerate(pairs)]
    for copy in copies:
        copy.start()
    out_ref[base:, :] = jnp.zeros((sz.param_rows, LANES), jnp.float32)
    copies[0].wait()
    per = sz.tile_x // sz.groups
    pieces = [
        pot[g * per : (g + 1) * per].reshape(sz.pot_rows, sz.chunk) for g in range(sz.groups)
    ]
    out_ref[sz.wave_rows : base, :] = pltpu.roll(
        jnp.concatenate(pieces, axis=1), lax.axis_index("band") * sz.chunk, 1
    )
    copies[3].wait()
    copies[4].wait()
    for j in range(NPROJ):
        lanes = slice(j * NPROJ, (j + 1) * NPROJ)
        out_ref[base : base + sz.atoms, lanes] = dh[0, 0, j]
        out_ref[base + sz.atoms : base + 2 * sz.atoms, lanes] = ds[0, 0, j]
    copies[1].wait()
    copies[2].wait()
    lane = lanes_of(1)
    for a in range(sz.atoms):
        row = jnp.where(lane == META_LANE + 3, counts[0, 0, a].astype(jnp.float32), 0.0)
        for k in range(3):
            row = jnp.where(lane == META_LANE + k, offs[0, k, 0, a].astype(jnp.float32), row)
        out_ref[base + a : base + a + 1, META_LANE : META_LANE + 4] = row[:, META_LANE : META_LANE + 4]
    copies[5].wait()


def wrapped(cell, centre, count):
    offset = cell - centre + float(BOX_LOW)
    offset = jnp.where(offset < 0.0, offset + float(count), offset)
    offset = jnp.where(offset >= float(count), offset - float(count), offset)
    inside = offset < float(BOX_CELLS)
    return offset - float(BOX_LOW), inside


def fill_rims(ref, width, count_x, count_y):
    ref[:, 0:SUBLANES, :] = ref[:, count_y : count_y + SUBLANES, :]
    ref[:, count_y + SUBLANES : count_y + 2 * SUBLANES, :] = ref[:, SUBLANES : 2 * SUBLANES, :]
    ref[0:width] = ref[count_x : count_x + width]
    ref[count_x + width : count_x + 2 * width] = ref[width : 2 * width]


def shifted_pair(value, reach):
    lane = lanes_of(1)
    below = jnp.where(lane >= reach, pltpu.roll(value, reach, 1), 0.0)
    above = jnp.where(lane < LANES - reach, pltpu.roll(value, LANES - reach, 1), 0.0)
    return below + above


def planar_kinetic(ref, x0, y0, rows, count):
    at = lambda x, y: ref[x0 + x + 3, pl.ds(SUBLANES + y0 + y, rows), :]
    planes = [at(x, 0) for x in range(-3, count + 3)]
    found = []
    for x in range(count):
        total = (-1.5 * STENCIL[0]) * planes[x + 3]
        for reach in (1, 2, 3):
            around = (planes[x + 3 - reach] + planes[x + 3 + reach]) + (at(x, -reach) + at(x, reach))
            total = total + (-0.5 * STENCIL[reach]) * around
        found.append((planes[x + 3], total))
    return found


def depth_matrix():
    row = lax.broadcasted_iota(jnp.int32, (2 * LANES, LANES), 0) % LANES
    reach = jnp.abs(row - lax.broadcasted_iota(jnp.int32, (2 * LANES, LANES), 1))
    value = jnp.zeros((2 * LANES, LANES), jnp.float32)
    for k in (1, 2, 3):
        value = jnp.where(reach == k, -0.5 * STENCIL[k] * DEPTH_SCALE, value)
    return value.astype(jnp.bfloat16)


def neighbour_block(ref, x0, y0, rows, count, step):
    at = lambda x, y: ref[x0 + x + 1, pl.ds(SUBLANES + y0 + y, rows), :]
    planes = [at(x, 0) for x in range(-1, count + 1)]
    found = []
    for x in range(count):
        center = planes[x + 1]
        around = (planes[x] + planes[x + 2]) + (at(x, -1) + at(x, 1)) + shifted_pair(center, step)
        found.append((center, around))
    return found


def over_blocks(count, body):
    if count <= 2 * BLOCK:
        for x0 in range(0, count, BLOCK):
            body(x0)
        return

    def step(index, carry):
        body(index * BLOCK)
        return carry

    lax.fori_loop(0, count // BLOCK, step, 0)


def plane_weights(sz, meta, w_ref, a_ref, wx_ref, wy_ref):
    atoms = sz.all_atoms
    widths = [-1.0 / w for w in RADIAL_WIDTHS]
    for tile in range(sz.cells // LANES):
        cell = lanes_of(1) + tile * LANES
        cell_x = (cell // sz.grid_y).astype(jnp.float32)
        cell_y = (cell % sz.grid_y).astype(jnp.float32)
        for start in range(0, atoms, 16):
            rx, inside_x = wrapped(cell_x, meta[start : start + 16, 0:1], sz.grid_x)
            ry, inside_y = wrapped(cell_y, meta[start : start + 16, 1:2], sz.grid_y)
            square = rx * rx + ry * ry
            inside = jnp.logical_and(inside_x, inside_y)
            radial = [jnp.where(inside, jnp.exp(square * w), 0.0) for w in widths]
            powers_x, powers_y = [None, rx, rx * rx], [None, ry, ry * ry]
            for index, (kind, px, py) in enumerate(PLANE_FACTORS):
                value = radial[kind]
                value = value if px == 0 else value * powers_x[px]
                value = value if py == 0 else value * powers_y[py]
                high, low = split(value)
                at = index * atoms + start
                lanes = slice(tile * LANES, (tile + 1) * LANES)
                w_ref[at : at + 16, lanes] = high
                w_ref[sz.factors + at : sz.factors + at + 16, lanes] = low
    turned = jnp.concatenate([meta] * (LANES // atoms), axis=0).T
    tiles = 2 * sz.factors // LANES
    for axis, count, ref in ((0, sz.grid_x, wx_ref), (1, sz.grid_y, wy_ref)):
        centre = turned[axis : axis + 1, :]
        cell = lax.broadcasted_iota(jnp.int32, (count, LANES), 0).astype(jnp.float32)
        offset, inside = wrapped(cell, centre, count)
        radial = [jnp.where(inside, jnp.exp(offset * offset * w), 0.0) for w in widths]
        powers = [1.0, offset, offset * offset]
        for tile in range(tiles):
            place = lanes_of(1) // atoms + tile * (LANES // atoms)
            value = None
            for slot in range(LANES // atoms):
                index = tile * (LANES // atoms) + slot
                kind, *power = PLANE_FACTORS[index % len(PLANE_FACTORS)]
                term = radial[kind] if power[axis] == 0 else radial[kind] * powers[power[axis]]
                value = term if value is None else jnp.where(place == index, term, value)
            ref[tile] = value

    def planes(x):
        rows = pl.ds(pl.multiple_of(x * sz.grid_y, 16), sz.grid_y)
        for tile in range(tiles):
            lanes = slice(tile * LANES, (tile + 1) * LANES)
            value = wx_ref[tile, pl.ds(x, 1), :] * wy_ref[tile]
            high = value.astype(jnp.bfloat16)
            if (tile + 1) * LANES > sz.factors:
                low = value - high.astype(jnp.float32)
                if tile * LANES < sz.factors:
                    low = jnp.where(lanes_of(1) + tile * LANES < sz.factors, value, low)
                high = low.astype(jnp.bfloat16)
            a_ref[rows, lanes] = high

    lax.fori_loop(0, sz.grid_x, lambda x, c: (planes(x), c)[1], 0, unroll=4)


def depth_weights(sz, meta, wz_ref):
    offset = lanes_of(1).astype(jnp.float32) - meta[:, 2:3]
    inside = jnp.logical_and(offset >= -float(BOX_LOW), offset < float(BOX_CELLS - BOX_LOW))
    radial = [
        jnp.where(inside, (AMPLITUDE * scale) * jnp.exp(offset * offset * (-1.0 / w)), 0.0)
        for scale, w in zip((1.0, 1.0 / 2.2, 1.0 / 5.76), RADIAL_WIDTHS)
    ]
    wz_ref[0] = radial[0]
    wz_ref[1] = radial[1]
    wz_ref[2] = radial[1] * offset
    wz_ref[3] = radial[2]
    wz_ref[4] = radial[2] * offset
    wz_ref[5] = radial[2] * (offset * offset)


def intersections(sz, w_ref, parts, wz_ref, active):
    sums = dot(w_ref[...], parts)
    sums = halves(sums[: sz.factors]) + sums[sz.factors :, :LANES]
    u = [sums[c * sz.all_atoms : (c + 1) * sz.all_atoms] for c in range(len(PLANE_FACTORS))]
    products = [
        u[0] * wz_ref[0],
        u[1] * wz_ref[1],
        u[2] * wz_ref[1],
        u[3] * wz_ref[2],
        u[4] * wz_ref[3],
        u[5] * wz_ref[4],
        u[6] * wz_ref[4],
        (0.5 * (u[7] - u[9])) * wz_ref[3],
        D_SCALE * (2.0 * u[8] * wz_ref[5] - (u[7] + u[9]) * wz_ref[3]),
    ]
    return [jnp.sum(p, axis=1, keepdims=True) * active[i] for i, p in enumerate(products)]


def active_columns(meta):
    return [(meta[:, 3:4] > float(i)).astype(jnp.float32) for i in range(NPROJ)]


def inner_lanes(columns):
    lane = lanes_of(1)
    inner = jnp.zeros((columns[0].shape[0], LANES), jnp.float32)
    for k in range(NPROJ):
        inner = jnp.where(jnp.logical_and(lane % NPROJ == k, lane < NPROJ * NPROJ), columns[k], inner)
    return inner


def outer_lanes(columns):
    lane = lanes_of(1)
    outer = jnp.zeros((columns[0].shape[0], LANES), jnp.float32)
    for k in range(NPROJ):
        outer = jnp.where(lane // NPROJ == k, columns[k], outer)
    return outer


def projector_sources(sz, matrix, inner, active, wz_ref, q_ref):
    lane = lanes_of(1)
    terms = DEPTH_SCALE * (matrix * inner)
    coef = [
        jnp.sum(jnp.where(lane // NPROJ == i, terms, 0.0), axis=1, keepdims=True) * active[i]
        for i in range(NPROJ)
    ]
    tilt = (0.5 * coef[7]) * wz_ref[3]
    ring = (D_SCALE * coef[8]) * wz_ref[3]
    blocks = [
        coef[0] * wz_ref[0],
        coef[1] * wz_ref[1],
        coef[2] * wz_ref[1],
        coef[3] * wz_ref[2],
        coef[4] * wz_ref[3],
        coef[5] * wz_ref[4],
        coef[6] * wz_ref[4],
        tilt - ring,
        (2.0 * D_SCALE * coef[8]) * wz_ref[5],
        -(tilt + ring),
    ]
    for index, block in enumerate(blocks):
        at = index * sz.all_atoms
        high, low = split(block)
        q_ref[at : at + sz.all_atoms, :LANES] = high
        q_ref[at : at + sz.all_atoms, LANES:] = low
        q_ref[sz.factors + at : sz.factors + at + sz.all_atoms, :LANES] = high


def build_kernel(sz, *refs):
    blocks, rest = refs[: sz.tiles_x * sz.tiles_y], refs[sz.tiles_x * sz.tiles_y :]
    (psi, parts, w_ref, a_ref, wz_ref, par_ref, wx_ref, wy_ref) = rest
    here_x, here_y = lax.axis_index("dx"), lax.axis_index("dy")
    base = sz.wave_rows + sz.pot_rows
    for index, block in enumerate(blocks):
        shift_y, shift_x = divmod(index, sz.tiles_x)
        tile_x = lax.rem(here_x + shift_x, sz.tiles_x)
        tile_y = lax.rem(here_y + shift_y, sz.tiles_y)
        at_y = pl.multiple_of(tile_y * sz.tile_y, 16)
        for x in range(sz.tile_x):
            value = block[x * sz.tile_y : (x + 1) * sz.tile_y, :]
            cell_x = tile_x * sz.tile_x + x
            psi[cell_x + 3, pl.ds(at_y + SUBLANES, sz.tile_y), :] = value
            rows = pl.ds(pl.multiple_of(cell_x * sz.grid_y + at_y, 16), sz.tile_y)
            high, low = split(value)
            parts[rows, :LANES] = high
            parts[rows, LANES:] = low
        tile = tile_x * sz.tiles_y + tile_y
        for k in range(2):
            par_ref[k, pl.ds(tile * sz.atoms, sz.atoms), :] = block[
                base + k * sz.atoms : base + (k + 1) * sz.atoms, :
            ]
    fill_rims(psi, 3, sz.grid_x, sz.grid_y)
    owners = lax.broadcasted_iota(jnp.int32, (sz.all_atoms, LANES), 0) // sz.atoms
    lane = lanes_of(sz.all_atoms)
    meta = pltpu.roll(par_ref[0], LANES - META_LANE, 1)
    meta = meta + jnp.where(lane == 0, (owners // sz.tiles_y * sz.tile_x).astype(jnp.float32), 0.0)
    meta = meta + jnp.where(lane == 1, (owners % sz.tiles_y * sz.tile_y).astype(jnp.float32), 0.0)
    par_ref[2] = meta
    depth_weights(sz, meta, wz_ref)
    plane_weights(sz, meta, w_ref, a_ref, wx_ref, wy_ref)


def energy_kernel(sz, psi, parts, w_ref, wz_ref, par_ref, kin, inner_ref, sums_ref):
    kin[...] = dot(parts[...], depth_matrix()).reshape(kin.shape)
    columns = intersections(sz, w_ref, parts[...], wz_ref, active_columns(par_ref[2]))
    inner = inner_lanes(columns)
    inner_ref[...] = inner
    pair = inner * outer_lanes(columns)

    def block(index, carry):
        x0, (energy, norm) = index * BLOCK, carry
        for y0 in range(0, sz.grid_y, SUBLANES):
            for x, (center, value) in enumerate(planar_kinetic(psi, x0, y0, SUBLANES, BLOCK)):
                rows = pl.ds(y0, SUBLANES)
                value = value + (1.0 / DEPTH_SCALE) * kin[x0 + x, rows, :]
                kin[x0 + x, rows, :] = value
                energy, norm = energy + value * center, norm + center * center
        return energy, norm

    zero = jnp.zeros((SUBLANES, LANES), jnp.float32)
    energy, norm = lax.fori_loop(0, sz.grid_x // BLOCK, block, (zero, zero))
    fold = lambda v: jnp.sum(v, axis=0, keepdims=True)
    sums_ref[0:1, :] = fold(energy) + fold(par_ref[0] * pair)
    sums_ref[1:2, :] = fold(norm) + fold(par_ref[1] * pair)


def pair_lanes(value, step):
    lane = lanes_of(1)
    other = jnp.where(
        (lane // step) % 2 == 1, pltpu.roll(value, step, 1), pltpu.roll(value, LANES - step, 1)
    )
    return value + other


def level_numbers(level):
    return 0.5 / 4.0**level, RELAXATION / diagonal_of(level)


def restrict_into(count_x, count_y, level, source, target, rows_ref):
    spread, guess = level_numbers(level)
    rows = 2 * SUBLANES

    def body(x0):
        for y0 in range(0, count_y, rows):
            found = neighbour_block(source, x0, y0, rows, BLOCK, 2**level)
            values = [(1.0 - RELAXATION) * c + (spread * guess) * n for c, n in found]
            for x in range(BLOCK // 2):
                slot = y0 // rows * (BLOCK // 2) + x
                rows_ref[slot] = values[2 * x] + values[2 * x + 1]
                total = (
                    rows_ref[slot, pl.ds(0, SUBLANES, stride=2), :]
                    + rows_ref[slot, pl.ds(1, SUBLANES, stride=2), :]
                )
                target[x0 // 2 + x + 1, pl.ds(SUBLANES + y0 // 2, SUBLANES), :] = 0.125 * pair_lanes(
                    total, 2**level
                )

    over_blocks(count_x, body)
    fill_rims(target, 1, count_x // 2, count_y // 2)


def relax_rows(count_x, count_y, level, guess_ref, source, emit):
    spread, guess = level_numbers(level)
    rows = min(2 * SUBLANES, count_y)

    def body(x0):
        for y0 in range(0, count_y, rows):
            found = neighbour_block(guess_ref, x0, y0, rows, BLOCK, 2**level)
            for x, (center, around) in enumerate(found):
                right = source[x0 + x + 1, pl.ds(SUBLANES + y0, rows), :]
                value = (1.0 - RELAXATION) * center + guess * right + (guess * spread) * around
                emit(x0 + x, y0, rows, value)

    over_blocks(count_x, body)


def prolong_into(count_x, count_y, level, coarse, source, target):
    guess = level_numbers(level)[1]

    def body(x0):
        for y0 in range(0, count_y, 2 * SUBLANES):
            for half in range(BLOCK // 2):
                value = coarse(x0 // 2 + half, y0 // 2)
                for part in range(2):
                    at = x0 + 2 * half + part + 1
                    for row in range(2):
                        rows = pl.ds(SUBLANES + y0 + row, SUBLANES, stride=2)
                        target[at, rows, :] = value + guess * source[at, rows, :]

    over_blocks(count_x, body)
    fill_rims(target, 1, count_x, count_y)


def step_kernel(sz, *refs):
    pots, refs = refs[: sz.groups * sz.tiles_y], refs[sz.groups * sz.tiles_y :]
    (psi, kin, w_ref, a_ref, wz_ref, par_ref, inner_ref, sums_ref), refs = refs[:8], refs[8:]
    (bands_ref, resid_ref, energy_ref), refs = refs[:3], refs[3:]
    (pot, corr, res, zfield, direct, change, b1, z1, x1, b2, x2, rows_ref, parts, q_ref) = refs
    nx, ny = sz.grid_x, sz.grid_y
    here_x, here_y = lax.axis_index("dx"), lax.axis_index("dy")
    here_group = lax.axis_index("band")
    per = sz.tile_x // sz.groups
    slot = lanes_of(1) // sz.chunk
    total = jnp.zeros((sz.tile_y, LANES), jnp.float32)
    for shift_y in range(sz.tiles_y):
        tile_y = lax.rem(here_y + shift_y, sz.tiles_y)
        at_y = pl.multiple_of(tile_y * sz.tile_y, 16)
        for shift_x in range(sz.tiles_x):
            tile_x = lax.rem(here_x + shift_x, sz.tiles_x)
            for g in range(sz.groups):
                value = None
                for shift_b in range(sz.groups):
                    source = lax.rem(here_group + shift_b, sz.groups)
                    piece = pots[shift_y * sz.groups + shift_b][
                        shift_x * sz.pot_rows : (shift_x + 1) * sz.pot_rows, :
                    ]
                    chosen = slot == lax.rem(source + g, sz.groups)
                    value = piece if value is None else jnp.where(chosen, piece, value)
                if g:
                    value = pltpu.roll(value, LANES - g * sz.chunk, 1)
                for k in range(per):
                    cell_x = tile_x * sz.tile_x + g * per + k
                    plane = value[k * sz.tile_y : (k + 1) * sz.tile_y]
                    pot[cell_x, pl.ds(at_y, sz.tile_y), :] = plane
                    center = psi[cell_x + 3, pl.ds(at_y + SUBLANES, sz.tile_y), :]
                    total = total + plane * (center * center)
    energy = (jnp.sum(total) + jnp.sum(sums_ref[0:1, :])) / jnp.sum(sums_ref[1:2, :])
    energy_ref[0] = energy
    active = active_columns(par_ref[2])
    matrix = par_ref[0] - energy * par_ref[1]
    q_ref[sz.factors :, LANES:] = jnp.zeros((sz.factors, LANES), jnp.bfloat16)
    projector_sources(sz, matrix, inner_ref[...], active, wz_ref, q_ref)
    corr[...] = halves(dot(a_ref[...], q_ref[...]))

    def residual(x0):
        for x in range(BLOCK):
            rows = pl.ds(pl.multiple_of((x0 + x) * ny, 16), ny)
            center = psi[x0 + x + 3, pl.ds(SUBLANES, ny), :]
            value = kin[x0 + x] + (pot[x0 + x] - energy) * center
            res[x0 + x + 1, pl.ds(SUBLANES, ny), :] = value + (1.0 / DEPTH_SCALE) * corr[rows, :]

    over_blocks(nx, residual)
    fill_rims(res, 1, nx, ny)
    restrict_into(nx, ny, 0, res, b1, rows_ref)
    restrict_into(nx // 2, ny // 2, 1, b1, b2, rows_ref)
    quarter_x, quarter_y = nx // 4, ny // 4
    x2[...] = level_numbers(2)[1] * b2[...]
    for sweep in range(COARSE_SWEEPS):
        planes = []
        relax_rows(quarter_x, quarter_y, 2, x2, b2, lambda *piece: planes.append(piece))
        for x, y0, rows, value in planes:
            x2[x + 1, pl.ds(SUBLANES + y0, rows), :] = value
        fill_rims(x2, 1, quarter_x, quarter_y)
    coarse_two = lambda x, y: x2[x + 1, pl.ds(SUBLANES + y, SUBLANES), :]
    prolong_into(nx // 2, ny // 2, 1, coarse_two, b1, z1)

    def emit_one(x, y0, rows, value):
        x1[x, pl.ds(y0, rows), :] = value

    relax_rows(nx // 2, ny // 2, 1, z1, b1, emit_one)
    prolong_into(nx, ny, 0, lambda x, y: x1[x, pl.ds(y, SUBLANES), :], res, zfield)

    def emit_zero(x, y0, rows, value):
        direct[x + 3, pl.ds(SUBLANES + y0, rows), :] = value
        cells = pl.ds(pl.multiple_of(x * ny + y0, 16), rows)
        high, low = split(value)
        parts[cells, :LANES] = high
        parts[cells, LANES:] = low

    relax_rows(nx, ny, 0, zfield, res, emit_zero)
    fill_rims(direct, 3, nx, ny)
    columns = intersections(sz, w_ref, parts[...], wz_ref, active)
    projector_sources(sz, matrix, inner_lanes(columns), active, wz_ref, q_ref)
    corr[...] = halves(dot(a_ref[...], q_ref[...])) + dot(parts[...], depth_matrix())

    def line(index, carry):
        x0, (over, under) = index * BLOCK, carry
        for y0 in range(0, ny, SUBLANES):
            rows = pl.ds(y0, SUBLANES)
            for x, (center, value) in enumerate(planar_kinetic(direct, x0, y0, SUBLANES, BLOCK)):
                cells = pl.ds(pl.multiple_of((x0 + x) * ny + y0, SUBLANES), SUBLANES)
                value = value + (pot[x0 + x, rows, :] - energy) * center
                value = value + (1.0 / DEPTH_SCALE) * corr[cells, :]
                change[x0 + x, rows, :] = value
                over = over + value * res[x0 + x + 1, pl.ds(SUBLANES + y0, SUBLANES), :]
                under = under + value * value
        return over, under

    zero = jnp.zeros((SUBLANES, LANES), jnp.float32)
    over, under = lax.fori_loop(0, nx // BLOCK, line, (zero, zero))
    step = -jnp.sum(over) / jnp.sum(under)
    at_x, at_y = here_x * sz.tile_x, pl.multiple_of(here_y * sz.tile_y, 16)
    for x in range(sz.tile_x):
        cell = at_x + x
        inner = pl.ds(at_y + SUBLANES, sz.tile_y)
        bands_ref[0, x] = psi[cell + 3, inner, :] + step * direct[cell + 3, inner, :]
        resid_ref[0, x] = res[cell + 1, inner, :] + step * change[cell, pl.ds(at_y, sz.tile_y), :]


def from_shift(value, axis, shift):
    count = lax.axis_size(axis)
    return lax.ppermute(value, axis, [((i + shift) % count, i) for i in range(count)])


def replicated(sz, wave_bands, potential, atom_offsets, proj_counts, dh_matrix, ds_matrix):
    vmem = pl.BlockSpec(memory_space=pltpu.VMEM)
    smem = pl.BlockSpec(memory_space=pltpu.SMEM)
    hbm = pl.BlockSpec(memory_space=pltpu.HBM)
    shape = lambda *dims: jax.ShapeDtypeStruct(dims, jnp.float32)
    half = lambda *dims: jax.ShapeDtypeStruct(dims, jnp.bfloat16)
    scratch = lambda *dims: pltpu.VMEM(dims, jnp.float32)
    grant = pltpu.CompilerParams(vmem_limit_bytes=VMEM_GRANT)
    cost = lambda flops: pl.CostEstimate(flops=flops, transcendentals=0, bytes_accessed=0)
    inputs = (
        wave_bands.reshape(sz.wave_rows, LANES),
        potential,
        atom_offsets.transpose(0, 3, 1, 2),
        proj_counts,
        dh_matrix.transpose(0, 1, 3, 2, 4),
        ds_matrix.transpose(0, 1, 3, 2, 4),
    )
    own = pl.pallas_call(
        functools.partial(pack_kernel, sz),
        out_shape=shape(sz.rows, LANES),
        in_specs=[hbm] * 6,
        out_specs=vmem,
        scratch_shapes=[
            scratch(*inputs[1].shape),
            pltpu.SMEM(inputs[2].shape, jnp.int32),
            pltpu.SMEM(inputs[3].shape, jnp.int32),
            scratch(*inputs[4].shape),
            scratch(*inputs[5].shape),
            pltpu.SemaphoreType.DMA((6,)),
        ],
        compiler_params=grant,
        name="pack",
    )(*(pltpu.with_memory_space_constraint(value, pltpu.HBM) for value in inputs))
    line = [own] + [from_shift(own, "dx", s) for s in range(1, sz.tiles_x)]
    blocks = list(line)
    for s in range(1, sz.tiles_y):
        blocks += [from_shift(block, "dy", s) for block in line]
    chunk = jnp.concatenate(
        [block[sz.wave_rows : sz.wave_rows + sz.pot_rows] for block in line], axis=0
    )
    chunks = [chunk] + [from_shift(chunk, "band", s) for s in range(1, sz.groups)]
    pots = list(chunks)
    for s in range(1, sz.tiles_y):
        pots += [from_shift(piece, "dy", s) for piece in chunks]
    nx, ny = sz.grid_x, sz.grid_y
    padded = lambda x, y, width: (x + 2 * width, y + 2 * SUBLANES, LANES)
    psi, parts, w, a, wz, par = pl.pallas_call(
        functools.partial(build_kernel, sz),
        out_shape=(
            shape(*padded(nx, ny, 3)),
            half(sz.cells, 2 * LANES),
            half(2 * sz.factors, sz.cells),
            half(sz.cells, 2 * sz.factors),
            shape(6, sz.all_atoms, LANES),
            shape(3, sz.all_atoms, LANES),
        ),
        in_specs=[vmem] * len(blocks),
        out_specs=(vmem,) * 6,
        scratch_shapes=[scratch(2 * sz.factors // LANES, n, LANES) for n in (nx, ny)],
        compiler_params=grant,
        cost_estimate=cost(2_000_000_000),
        name="build",
    )(*blocks)
    kin, inner, sums = pl.pallas_call(
        functools.partial(energy_kernel, sz),
        out_shape=(shape(nx, ny, LANES), shape(sz.all_atoms, LANES), shape(2, LANES)),
        in_specs=[vmem] * 5,
        out_specs=(vmem,) * 3,
        compiler_params=grant,
        cost_estimate=cost(2_000_000_000),
        name="energy",
    )(psi, parts, w, wz, par)
    return pl.pallas_call(
        functools.partial(step_kernel, sz),
        out_shape=(
            jax.ShapeDtypeStruct(wave_bands.shape, jnp.float32),
            jax.ShapeDtypeStruct(wave_bands.shape, jnp.float32),
            shape(1),
        ),
        in_specs=[vmem] * (len(pots) + 8),
        out_specs=(vmem, vmem, smem),
        scratch_shapes=[
            scratch(nx, ny, LANES),
            scratch(sz.cells, LANES),
            scratch(*padded(nx, ny, 1)),
            scratch(*padded(nx, ny, 1)),
            scratch(*padded(nx, ny, 3)),
            scratch(nx, ny, LANES),
            scratch(*padded(nx // 2, ny // 2, 1)),
            scratch(*padded(nx // 2, ny // 2, 1)),
            scratch(nx // 2, ny // 2, LANES),
            scratch(*padded(nx // 4, ny // 4, 1)),
            scratch(*padded(nx // 4, ny // 4, 1)),
            scratch(ny // 2 // SUBLANES * (BLOCK // 2), 2 * SUBLANES, LANES),
            pltpu.VMEM((sz.cells, 2 * LANES), jnp.bfloat16),
            pltpu.VMEM((2 * sz.factors, 2 * LANES), jnp.bfloat16),
        ],
        compiler_params=grant,
        cost_estimate=cost(4_000_000_000),
        name="step",
    )(*pots, psi, kin, w, a, wz, par, inner, sums)


def on_device(wave_bands, potential, atom_offsets, proj_counts, dh_matrix, ds_matrix):
    sz = Sizes(
        wave_bands,
        potential,
        proj_counts.shape[2],
        lax.axis_size("dx"),
        lax.axis_size("dy"),
        lax.axis_size("band"),
    )
    step = functools.partial(replicated, sz) if sz.fits(VMEM_BUDGET) else distributed
    return step(wave_bands, potential, atom_offsets, proj_counts, dh_matrix, ds_matrix)


def solution(mesh):
    return jax.shard_map(
        on_device,
        mesh=mesh,
        in_specs=(
            P("band", "dx", "dy", None),
            P("dx", "dy", "band"),
            P("dx", "dy", None, None),
            P("dx", "dy", None),
            P("dx", "dy", None, None, None),
            P("dx", "dy", None, None, None),
        ),
        out_specs=(P("band", "dx", "dy", None), P("band", "dx", "dy", None), P("band")),
        check_vma=False,
    )
```

```python
import functools

import jax
import jax.numpy as jnp
from jax import lax
from jax.experimental import pallas as pl
from jax.experimental.pallas import tpu as pltpu
from jax.sharding import PartitionSpec as P

NPROJ = 9
COARSE_SWEEPS = 2


STENCIL = (-49.0 / 18.0, 1.5, -0.15, 1.0 / 90.0)
RELAXATION = 2.0 / 3.0
MASS_SHIFT = 0.25
AMPLITUDE = 0.15
PRECISE = lax.Precision.HIGHEST


def extended(cells, sides, width):
    for axis, dim in sides:
        count = lax.axis_size(axis)
        head = lax.slice_in_dim(cells, 0, width, axis=dim)
        tail = lax.slice_in_dim(cells, cells.shape[dim] - width, cells.shape[dim], axis=dim)
        cells = jnp.concatenate(
            [
                lax.ppermute(tail, axis, [(i, (i + 1) % count) for i in range(count)]),
                cells,
                lax.ppermute(head, axis, [((i + 1) % count, i) for i in range(count)]),
            ],
            axis=dim,
        )
    return cells


def projector_table():
    box_steps = jnp.arange(12, dtype=jnp.float32) - 6.0
    filler = jnp.ones((12, 12, 12), jnp.float32)
    along_x = box_steps[:, None, None] * filler
    along_y = box_steps[None, :, None] * filler
    along_z = box_steps[None, None, :] * filler
    radius_sq = along_x * along_x + along_y * along_y + along_z * along_z
    radial_s = jnp.exp(-radius_sq / 8.0)
    radial_p = jnp.exp(-radius_sq / 9.68) / 2.2
    radial_d = jnp.exp(-radius_sq / 11.52) / 5.76
    angular = [
        radial_s,
        radial_p * along_x,
        radial_p * along_y,
        radial_p * along_z,
        radial_d * along_x * along_y,
        radial_d * along_y * along_z,
        radial_d * along_z * along_x,
        0.5 * radial_d * (along_x * along_x - along_y * along_y),
        radial_d * (3.0 * along_z * along_z - radius_sq) * 0.28867513,
    ]
    return AMPLITUDE * jnp.stack(angular).reshape(9, 1728)


def shift_z(field, reach):
    depth = field.shape[-1]
    zeros_rim = jnp.zeros(field.shape[:-1] + (abs(reach),), field.dtype)
    if reach > 0:
        return jnp.concatenate([zeros_rim, field[..., : depth - reach]], axis=-1)
    return jnp.concatenate([field[..., -reach:], zeros_rim], axis=-1)


def kinetic_padded(padded, width, tile_x, tile_y):
    center = padded[:, width : width + tile_x, width : width + tile_y]
    laplacian = 3.0 * STENCIL[0] * center
    for reach in (1, 2, 3):
        weight = STENCIL[reach]
        laplacian = laplacian + weight * (
            padded[:, width - reach : width - reach + tile_x, width : width + tile_y]
            + padded[:, width + reach : width + reach + tile_x, width : width + tile_y]
            + padded[:, width : width + tile_x, width - reach : width - reach + tile_y]
            + padded[:, width : width + tile_x, width + reach : width + reach + tile_y]
            + shift_z(center, reach)
            + shift_z(center, -reach)
        )
    return -0.5 * laplacian


def box_targets(places, tile_x, tile_y, depth):
    box_steps = jnp.arange(12, dtype=jnp.int32)
    tile_shift = jnp.arange(3, dtype=jnp.int32) - 1
    target_x = (
        tile_shift[:, None, None, None] * tile_x + places[:, :, :, 0][..., None] - 6 + box_steps
    )
    target_y = (
        tile_shift[None, :, None, None] * tile_y + places[:, :, :, 1][..., None] - 6 + box_steps
    )
    target_z = places[:, :, :, 2][..., None] - 6 + box_steps
    target_x = jnp.where((target_x >= 0) & (target_x < tile_x), target_x, tile_x + 12)
    target_y = jnp.where((target_y >= 0) & (target_y < tile_y), target_y, tile_y + 12)
    depth_cells = jnp.arange(depth, dtype=jnp.int32)
    window = (target_z[..., None] == depth_cells).astype(jnp.float32)
    return (target_x, target_y, window)


def own_intersection(widened, atom_offsets, window, projector_rows):
    nbands = widened.shape[0]
    box_steps = jnp.arange(12, dtype=jnp.int32)
    owned = atom_offsets[0, 0]
    index_x = (owned[:, 0:1] + box_steps[None, :])[:, :, None]
    index_y = (owned[:, 1:2] + box_steps[None, :])[:, None, :]
    columns = widened[:, index_x, index_y]
    box_values = jnp.einsum("bauvz,akz->bauvk", columns, window[1, 1], precision=PRECISE)
    box_values = box_values.reshape(nbands, -1, 1728)
    return jnp.einsum("ik,bak->aib", projector_rows, box_values, precision=PRECISE)


def projector_terms(
    intersection, proj_counts, targets, dh_matrix, ds_matrix, projector_rows, field_shape
):
    nbands, tile_x, tile_y, depth = field_shape
    active = (jnp.arange(NPROJ, dtype=jnp.int32)[None, :] < proj_counts[0, 0][:, None]).astype(
        jnp.float32
    )
    intersection = intersection * active[:, :, None]
    coefficients = jnp.stack(
        [
            jnp.einsum("aij,ajb->aib", dh_matrix[0, 0], intersection, precision=PRECISE),
            jnp.einsum("aij,ajb->aib", ds_matrix[0, 0], intersection, precision=PRECISE),
        ]
    )
    coefficients = coefficients * active[None, :, :, None]
    nearby = extended(coefficients[None, None], (("dx", 0), ("dy", 1)), 1)
    spread = jnp.einsum("ik,uvhaib->hbuvak", projector_rows, nearby, precision=PRECISE)
    spread = spread.reshape(2, nbands, 3, 3, -1, 144, 12)
    target_x, target_y, window = targets
    placed = jnp.einsum("hbuvaxk,uvakz->hbuvaxz", spread, window, precision=PRECISE)
    placed = placed.reshape(2, nbands, 3, 3, -1, 12, 12, depth)
    correction = jnp.zeros((2, nbands, tile_x, tile_y, depth), jnp.float32)
    correction = correction.at[:, :, target_x[..., :, None], target_y[..., None, :]].add(
        placed, mode="drop"
    )
    return (correction[0], correction[1])


def hamiltonian(
    field, full_potential, atom_offsets, proj_counts, targets, dh_matrix, ds_matrix, projector_rows
):
    tile_x, tile_y = (field.shape[1], field.shape[2])
    widened = extended(field, (("dx", 1), ("dy", 2)), 6)
    kinetic_part = kinetic_padded(widened, 6, tile_x, tile_y)
    intersection = own_intersection(widened, atom_offsets, targets[2], projector_rows)
    corr_h, corr_s = projector_terms(
        intersection, proj_counts, targets, dh_matrix, ds_matrix, projector_rows, field.shape
    )
    return (kinetic_part + full_potential[None] * field + corr_h, field + corr_s)


def domain_sums(values):
    return lax.psum(values, ("dx", "dy"))


def diagonal_of(level):
    return 3.0 / 4.0**level + MASS_SHIFT


def tile_apply(field, level):
    padded = extended(field, (("dx", 1), ("dy", 2)), 1)
    neighbours = (
        padded[:, :-2, 1:-1]
        + padded[:, 2:, 1:-1]
        + padded[:, 1:-1, :-2]
        + padded[:, 1:-1, 2:]
        + shift_z(field, 1)
        + shift_z(field, -1)
    )
    return -0.5 * (neighbours - 6.0 * field) / 4.0**level + MASS_SHIFT * field


def pair_table(depth):
    fine_cells = jnp.arange(depth, dtype=jnp.int32)[:, None] // 2
    coarse_cells = jnp.arange(depth // 2, dtype=jnp.int32)[None, :]
    return (fine_cells == coarse_cells).astype(jnp.float32)


def restrict(field):
    nbands, size_x, size_y, size_z = field.shape
    planar = field.reshape(nbands, size_x // 2, 2, size_y // 2, 2, size_z).mean(axis=(2, 4))
    return jnp.einsum("bxyz,zw->bxyw", planar, 0.5 * pair_table(size_z), precision=PRECISE)


def prolong(field):
    size_z = field.shape[3]
    widened = jnp.repeat(jnp.repeat(field, 2, axis=1), 2, axis=2)
    return jnp.einsum("bxyw,zw->bxyz", widened, pair_table(2 * size_z), precision=PRECISE)


def precondition(source_zero):
    guess_zero = RELAXATION * source_zero / diagonal_of(0)
    source_one = restrict(source_zero - tile_apply(guess_zero, 0))
    guess_one = RELAXATION * source_one / diagonal_of(1)
    source_two = restrict(source_one - tile_apply(guess_one, 1))
    guess_two = RELAXATION * source_two / diagonal_of(2)
    for _ in range(COARSE_SWEEPS):
        guess_two = guess_two + RELAXATION * (source_two - tile_apply(guess_two, 2)) / diagonal_of(
            2
        )
    guess_one = guess_one + prolong(guess_two)
    guess_one = guess_one + RELAXATION * (source_one - tile_apply(guess_one, 1)) / diagonal_of(1)
    guess_zero = guess_zero + prolong(guess_one)
    return guess_zero + RELAXATION * (source_zero - tile_apply(guess_zero, 0)) / diagonal_of(0)


def distributed(wave_bands, potential, atom_offsets, proj_counts, dh_matrix, ds_matrix):
    projector_rows = projector_table()
    full_potential = lax.all_gather(potential, "band", axis=2, tiled=True)
    places = extended(atom_offsets, (("dx", 0), ("dy", 1)), 1)
    targets = box_targets(places, wave_bands.shape[1], wave_bands.shape[2], wave_bands.shape[3])
    h_band, s_band = hamiltonian(
        wave_bands,
        full_potential,
        atom_offsets,
        proj_counts,
        targets,
        dh_matrix,
        ds_matrix,
        projector_rows,
    )
    energy_sums = domain_sums(
        jnp.stack(
            [
                jnp.sum(wave_bands * h_band, axis=(1, 2, 3)),
                jnp.sum(wave_bands * s_band, axis=(1, 2, 3)),
            ]
        )
    )
    band_energy = energy_sums[0] / energy_sums[1]
    energy_grid = band_energy[:, None, None, None]
    residual = h_band - energy_grid * s_band
    direction = precondition(residual)
    h_dir, s_dir = hamiltonian(
        direction,
        full_potential,
        atom_offsets,
        proj_counts,
        targets,
        dh_matrix,
        ds_matrix,
        projector_rows,
    )
    change = h_dir - energy_grid * s_dir
    line_sums = domain_sums(
        jnp.stack(
            [jnp.sum(residual * change, axis=(1, 2, 3)), jnp.sum(change * change, axis=(1, 2, 3))]
        )
    )
    step_grid = (-line_sums[0] / line_sums[1])[:, None, None, None]
    return (wave_bands + step_grid * direction, residual + step_grid * change, band_energy)


BOX_LOW = 6
BOX_CELLS = 12
LANES = 128
SUBLANES = 8
RADIAL_WIDTHS = (8.0, 9.68, 11.52)
PLANE_FACTORS = (
    (0, 0, 0),
    (1, 1, 0),
    (1, 0, 1),
    (1, 0, 0),
    (2, 1, 1),
    (2, 0, 1),
    (2, 1, 0),
    (2, 2, 0),
    (2, 0, 0),
    (2, 0, 2),
)
D_SCALE = 0.28867513
DEPTH_SCALE = 180.0
BLOCK = 8
VMEM_BUDGET = 40 * 1024 * 1024
VMEM_GRANT = 24 * 1024 * 1024


class Sizes:
    def __init__(self, wave, potential, atoms, tiles_x, tiles_y, groups):
        self.tile_x, self.tile_y, self.depth = wave.shape[1:]
        self.atoms = atoms
        self.tiles_x, self.tiles_y, self.groups = tiles_x, tiles_y, groups
        self.grid_x, self.grid_y = tiles_x * self.tile_x, tiles_y * self.tile_y
        self.cells = self.grid_x * self.grid_y
        self.chunk = potential.shape[2]
        self.all_atoms = tiles_x * tiles_y * atoms
        self.wave_rows = self.tile_x * self.tile_y
        self.pot_rows = self.wave_rows // groups
        self.param_rows = -(-2 * atoms // SUBLANES) * SUBLANES
        self.rows = self.wave_rows + self.pot_rows + self.param_rows
        self.factors = len(PLANE_FACTORS) * self.all_atoms

    def fits(self, vmem_bytes):
        return (
            self.depth == LANES
            and self.chunk * self.groups == LANES
            and self.tile_x % max(self.groups, BLOCK) == 0
            and self.tile_y % 16 == 0
            and self.grid_x >= 2 * BLOCK
            and self.grid_y >= 32
            and self.all_atoms % 16 == 0
            and LANES % self.all_atoms == 0
            and self.cells * (60 * LANES + 8 * self.factors) <= vmem_bytes
        )


def lanes_of(rows=1):
    return lax.broadcasted_iota(jnp.int32, (rows, LANES), 1)


def split(value):
    high = value.astype(jnp.bfloat16)
    return high, (value - high.astype(jnp.float32)).astype(jnp.bfloat16)


def halves(value):
    return value[:, :LANES] + value[:, LANES:]


def dot(left, right):
    return jnp.dot(left, right, preferred_element_type=jnp.float32)


META_LANE = 96


def pack_kernel(sz, wave_ref, pot_ref, offs_ref, counts_ref, dh_ref, ds_ref, out_ref, *scratch):
    *places, sems = scratch
    pot, offs, counts, dh, ds = places
    start, base = sz.wave_rows, sz.wave_rows + sz.pot_rows
    sources = (pot_ref, offs_ref, counts_ref, dh_ref, ds_ref, wave_ref)
    places = places + [out_ref.at[pl.ds(0, start)]]
    copies = [
        pltpu.make_async_copy(a, b, sems.at[i])
        for i, (a, b) in enumerate(zip(sources, places))
    ]
    for copy in copies:
        copy.start()
    out_ref[base:, :] = jnp.zeros((sz.param_rows, LANES), jnp.float32)
    for copy in copies:
        copy.wait()
    per = sz.tile_x // sz.groups
    pieces = [
        pot[g * per : (g + 1) * per].reshape(sz.pot_rows, sz.chunk) for g in range(sz.groups)
    ]
    out_ref[start:base, :] = pltpu.roll(
        jnp.concatenate(pieces, axis=1), lax.axis_index("band") * sz.chunk, 1
    )
    for j in range(NPROJ):
        lanes = slice(j * NPROJ, (j + 1) * NPROJ)
        out_ref[base : base + sz.atoms, lanes] = dh[0, 0, j]
        out_ref[base + sz.atoms : base + 2 * sz.atoms, lanes] = ds[0, 0, j]
    lane = lanes_of(1)
    for a in range(sz.atoms):
        row = jnp.where(lane == META_LANE + 3, counts[0, 0, a].astype(jnp.float32), 0.0)
        for k in range(3):
            row = jnp.where(lane == META_LANE + k, offs[0, k, 0, a].astype(jnp.float32), row)
        out_ref[base + a : base + a + 1, META_LANE : META_LANE + 4] = row[:, META_LANE : META_LANE + 4]


def wrapped(cell, centre, count):
    offset = cell - centre + float(BOX_LOW)
    offset = jnp.where(offset < 0.0, offset + float(count), offset)
    offset = jnp.where(offset >= float(count), offset - float(count), offset)
    inside = offset < float(BOX_CELLS)
    return offset - float(BOX_LOW), inside


def fill_rims(ref, width, count_x, count_y):
    ref[:, 0:SUBLANES, :] = ref[:, count_y : count_y + SUBLANES, :]
    ref[:, count_y + SUBLANES : count_y + 2 * SUBLANES, :] = ref[:, SUBLANES : 2 * SUBLANES, :]
    ref[0:width] = ref[count_x : count_x + width]
    ref[count_x + width : count_x + 2 * width] = ref[width : 2 * width]


def shifted_pair(value, reach):
    lane = lanes_of(1)
    below = jnp.where(lane >= reach, pltpu.roll(value, reach, 1), 0.0)
    above = jnp.where(lane < LANES - reach, pltpu.roll(value, LANES - reach, 1), 0.0)
    return below + above


def planar_kinetic(ref, x0, y0, rows, count):
    at = lambda x, y: ref[x0 + x + 3, pl.ds(SUBLANES + y0 + y, rows), :]
    planes = [at(x, 0) for x in range(-3, count + 3)]
    found = []
    for x in range(count):
        total = (-1.5 * STENCIL[0]) * planes[x + 3]
        for reach in (1, 2, 3):
            around = (planes[x + 3 - reach] + planes[x + 3 + reach]) + (at(x, -reach) + at(x, reach))
            total = total + (-0.5 * STENCIL[reach]) * around
        found.append((planes[x + 3], total))
    return found


def depth_matrix():
    row = lax.broadcasted_iota(jnp.int32, (2 * LANES, LANES), 0) % LANES
    reach = jnp.abs(row - lax.broadcasted_iota(jnp.int32, (2 * LANES, LANES), 1))
    value = jnp.zeros((2 * LANES, LANES), jnp.float32)
    for k in (1, 2, 3):
        value = jnp.where(reach == k, -0.5 * STENCIL[k] * DEPTH_SCALE, value)
    return value.astype(jnp.bfloat16)


def neighbour_block(ref, x0, y0, rows, count, step):
    at = lambda x, y: ref[x0 + x + 1, pl.ds(SUBLANES + y0 + y, rows), :]
    planes = [at(x, 0) for x in range(-1, count + 1)]
    found = []
    for x in range(count):
        center = planes[x + 1]
        around = (planes[x] + planes[x + 2]) + (at(x, -1) + at(x, 1)) + shifted_pair(center, step)
        found.append((center, around))
    return found


def over_blocks(count, body):
    if count <= 2 * BLOCK:
        for x0 in range(0, count, BLOCK):
            body(x0)
        return

    def step(index, carry):
        body(index * BLOCK)
        return carry

    lax.fori_loop(0, count // BLOCK, step, 0)


def plane_weights(sz, meta, w_ref, a_ref, wx_ref, wy_ref):
    atoms = sz.all_atoms
    widths = [-1.0 / w for w in RADIAL_WIDTHS]
    for tile in range(sz.cells // LANES):
        cell = lanes_of(1) + tile * LANES
        cell_x = (cell // sz.grid_y).astype(jnp.float32)
        cell_y = (cell % sz.grid_y).astype(jnp.float32)
        for start in range(0, atoms, 16):
            rx, inside_x = wrapped(cell_x, meta[start : start + 16, 0:1], sz.grid_x)
            ry, inside_y = wrapped(cell_y, meta[start : start + 16, 1:2], sz.grid_y)
            square = rx * rx + ry * ry
            inside = jnp.logical_and(inside_x, inside_y)
            radial = [jnp.where(inside, jnp.exp(square * w), 0.0) for w in widths]
            powers_x, powers_y = [None, rx, rx * rx], [None, ry, ry * ry]
            for index, (kind, px, py) in enumerate(PLANE_FACTORS):
                value = radial[kind]
                value = value if px == 0 else value * powers_x[px]
                value = value if py == 0 else value * powers_y[py]
                high, low = split(value)
                at = index * atoms + start
                lanes = slice(tile * LANES, (tile + 1) * LANES)
                w_ref[at : at + 16, lanes] = high
                w_ref[sz.factors + at : sz.factors + at + 16, lanes] = low
    turned = jnp.concatenate([meta] * (LANES // atoms), axis=0).T
    tiles = 2 * sz.factors // LANES
    for axis, count, ref in ((0, sz.grid_x, wx_ref), (1, sz.grid_y, wy_ref)):
        centre = turned[axis : axis + 1, :]
        cell = lax.broadcasted_iota(jnp.int32, (count, LANES), 0).astype(jnp.float32)
        offset, inside = wrapped(cell, centre, count)
        radial = [jnp.where(inside, jnp.exp(offset * offset * w), 0.0) for w in widths]
        powers = [1.0, offset, offset * offset]
        for tile in range(tiles):
            place = lanes_of(1) // atoms + tile * (LANES // atoms)
            value = None
            for slot in range(LANES // atoms):
                index = tile * (LANES // atoms) + slot
                kind, *power = PLANE_FACTORS[index % len(PLANE_FACTORS)]
                term = radial[kind] if power[axis] == 0 else radial[kind] * powers[power[axis]]
                value = term if value is None else jnp.where(place == index, term, value)
            ref[tile] = value

    def planes(x):
        rows = pl.ds(pl.multiple_of(x * sz.grid_y, 16), sz.grid_y)
        for tile in range(tiles):
            lanes = slice(tile * LANES, (tile + 1) * LANES)
            value = wx_ref[tile, pl.ds(x, 1), :] * wy_ref[tile]
            high = value.astype(jnp.bfloat16)
            if (tile + 1) * LANES > sz.factors:
                low = value - high.astype(jnp.float32)
                if tile * LANES < sz.factors:
                    low = jnp.where(lanes_of(1) + tile * LANES < sz.factors, value, low)
                high = low.astype(jnp.bfloat16)
            a_ref[rows, lanes] = high

    lax.fori_loop(0, sz.grid_x, lambda x, c: (planes(x), c)[1], 0, unroll=4)


def depth_weights(meta, wz_ref):
    offset = lanes_of(1).astype(jnp.float32) - meta[:, 2:3]
    inside = jnp.logical_and(offset >= -float(BOX_LOW), offset < float(BOX_CELLS - BOX_LOW))
    radial = [
        jnp.where(inside, (AMPLITUDE * scale) * jnp.exp(offset * offset * (-1.0 / w)), 0.0)
        for scale, w in zip((1.0, 1.0 / 2.2, 1.0 / 5.76), RADIAL_WIDTHS)
    ]
    wz_ref[0] = radial[0]
    wz_ref[1] = radial[1]
    wz_ref[2] = radial[1] * offset
    wz_ref[3] = radial[2]
    wz_ref[4] = radial[2] * offset
    wz_ref[5] = radial[2] * (offset * offset)


def intersections(sz, w_ref, parts, wz_ref, active):
    high, low = parts[:, :LANES], parts[:, LANES:]
    sums = dot(w_ref[: sz.factors], high)
    sums = sums + (dot(w_ref[: sz.factors], low) + dot(w_ref[sz.factors :], high))
    u = [sums[c * sz.all_atoms : (c + 1) * sz.all_atoms] for c in range(len(PLANE_FACTORS))]
    products = [
        u[0] * wz_ref[0],
        u[1] * wz_ref[1],
        u[2] * wz_ref[1],
        u[3] * wz_ref[2],
        u[4] * wz_ref[3],
        u[5] * wz_ref[4],
        u[6] * wz_ref[4],
        (0.5 * (u[7] - u[9])) * wz_ref[3],
        D_SCALE * (2.0 * u[8] * wz_ref[5] - (u[7] + u[9]) * wz_ref[3]),
    ]
    return [jnp.sum(p, axis=1, keepdims=True) * active[i] for i, p in enumerate(products)]


def active_columns(meta):
    return [(meta[:, 3:4] > float(i)).astype(jnp.float32) for i in range(NPROJ)]


def inner_lanes(columns):
    lane = lanes_of(1)
    inner = jnp.zeros((columns[0].shape[0], LANES), jnp.float32)
    for k in range(NPROJ):
        inner = jnp.where(jnp.logical_and(lane % NPROJ == k, lane < NPROJ * NPROJ), columns[k], inner)
    return inner


def projector_sources(sz, matrix, inner, active, wz_ref, q_ref):
    lane = lanes_of(1)
    terms = DEPTH_SCALE * (matrix * inner)
    coef = [
        jnp.sum(jnp.where(lane // NPROJ == i, terms, 0.0), axis=1, keepdims=True) * active[i]
        for i in range(NPROJ)
    ]
    tilt = (0.5 * coef[7]) * wz_ref[3]
    ring = (D_SCALE * coef[8]) * wz_ref[3]
    blocks = [
        coef[0] * wz_ref[0],
        coef[1] * wz_ref[1],
        coef[2] * wz_ref[1],
        coef[3] * wz_ref[2],
        coef[4] * wz_ref[3],
        coef[5] * wz_ref[4],
        coef[6] * wz_ref[4],
        tilt - ring,
        (2.0 * D_SCALE * coef[8]) * wz_ref[5],
        -(tilt + ring),
    ]
    for index, block in enumerate(blocks):
        at = index * sz.all_atoms
        high, low = split(block)
        q_ref[at : at + sz.all_atoms, :LANES] = high
        q_ref[at : at + sz.all_atoms, LANES:] = low
        q_ref[sz.factors + at : sz.factors + at + sz.all_atoms, :LANES] = high


def tile_at(sz, index):
    turn_y, turn_x = divmod(index, sz.tiles_x)
    tile_x = partner(lax.axis_index("dx"), turn_x, sz.tiles_x)
    tile_y = partner(lax.axis_index("dy"), turn_y, sz.tiles_y)
    return tile_x, tile_y


def add_projectors(sz, a_ref, q_ref, emit):
    part = sz.cells // 2
    for at in range(0, sz.cells, part):
        emit(at, part, halves(dot(a_ref[at : at + part, :], q_ref[...])))


def first_kernel(sz, *refs):
    blocks, refs = refs[: sz.tiles_x * sz.tiles_y], refs[sz.tiles_x * sz.tiles_y :]
    (psi, spsi, zkin, inner_ref, w_ref, a_ref, wz_ref, par_ref), refs = refs[:8], refs[8:]
    (parts, q_ref, wx_ref, wy_ref) = refs
    nx, ny = sz.grid_x, sz.grid_y
    for index, block in enumerate(blocks):
        tile_x, tile_y = tile_at(sz, index)
        at_y = pl.multiple_of(tile_y * sz.tile_y, 16)
        for x in range(sz.tile_x):
            value = block[x * sz.tile_y : (x + 1) * sz.tile_y, :]
            cell_x = tile_x * sz.tile_x + x
            psi[cell_x + 3, pl.ds(at_y + SUBLANES, sz.tile_y), :] = value
            rows = pl.ds(pl.multiple_of(cell_x * ny + at_y, 16), sz.tile_y)
            high, low = split(value)
            parts[rows, :LANES] = high
            parts[rows, LANES:] = low
        tile = tile_x * sz.tiles_y + tile_y
        for k in range(2):
            at = sz.wave_rows + sz.pot_rows + k * sz.atoms
            par_ref[k, pl.ds(tile * sz.atoms, sz.atoms), :] = block[at : at + sz.atoms, :]
    fill_rims(psi, 3, nx, ny)
    owners = lax.broadcasted_iota(jnp.int32, (sz.all_atoms, LANES), 0) // sz.atoms
    lane = lanes_of(sz.all_atoms)
    meta = pltpu.roll(par_ref[0], LANES - META_LANE, 1)
    meta = meta + jnp.where(lane == 0, (owners // sz.tiles_y * sz.tile_x).astype(jnp.float32), 0.0)
    meta = meta + jnp.where(lane == 1, (owners % sz.tiles_y * sz.tile_y).astype(jnp.float32), 0.0)
    par_ref[2] = meta
    depth_weights(meta, wz_ref)
    plane_weights(sz, meta, w_ref, a_ref, wx_ref, wy_ref)
    active = active_columns(meta)
    columns = intersections(sz, w_ref, parts[...], wz_ref, active)
    zkin[...] = dot(parts[...], depth_matrix())
    inner = inner_lanes(columns)
    inner_ref[...] = inner
    q_ref[sz.factors :, LANES:] = jnp.zeros((sz.factors, LANES), jnp.bfloat16)
    projector_sources(sz, par_ref[1], inner, active, wz_ref, q_ref)

    def emit_s(at, rows, value):
        x0, count = at // ny, rows // ny
        center = psi[x0 + 3 : x0 + 3 + count, SUBLANES : SUBLANES + ny, :]
        spsi[x0 : x0 + count] = center + (1.0 / DEPTH_SCALE) * value.reshape(count, ny, LANES)

    add_projectors(sz, a_ref, q_ref, emit_s)


def second_kernel(sz, *refs):
    (psi, spsi, zkin, inner_ref, a_ref, wz_ref, par_ref, hpsi, sums_ref, q_ref) = refs
    nx, ny = sz.grid_x, sz.grid_y
    q_ref[sz.factors :, LANES:] = jnp.zeros((sz.factors, LANES), jnp.bfloat16)
    active = active_columns(par_ref[2])
    projector_sources(sz, par_ref[0], inner_ref[...], active, wz_ref, q_ref)

    def emit_h(at, rows, value):
        x0, count = at // ny, rows // ny
        total = value + zkin[at : at + rows, :]
        hpsi[x0 : x0 + count] = (1.0 / DEPTH_SCALE) * total.reshape(count, ny, LANES)

    add_projectors(sz, a_ref, q_ref, emit_h)

    def block(index, carry):
        x0, (energy, norm) = index * BLOCK, carry
        for y0 in range(0, ny, SUBLANES):
            rows = pl.ds(y0, SUBLANES)
            for x, (center, value) in enumerate(planar_kinetic(psi, x0, y0, SUBLANES, BLOCK)):
                value = value + hpsi[x0 + x, rows, :]
                hpsi[x0 + x, rows, :] = value
                energy = energy + value * center
                norm = norm + spsi[x0 + x, rows, :] * center
        return energy, norm

    zero = jnp.zeros((SUBLANES, LANES), jnp.float32)
    energy, norm = lax.fori_loop(0, nx // BLOCK, block, (zero, zero))
    sums_ref[0:1, :] = jnp.sum(energy, axis=0, keepdims=True)
    sums_ref[1:2, :] = jnp.sum(norm, axis=0, keepdims=True)


def pair_lanes(value, step):
    lane = lanes_of(1)
    other = jnp.where(
        (lane // step) % 2 == 1, pltpu.roll(value, step, 1), pltpu.roll(value, LANES - step, 1)
    )
    return value + other


def level_numbers(level):
    return 0.5 / 4.0**level, RELAXATION / diagonal_of(level)


def restrict_into(count_x, count_y, level, source, target, rows_ref):
    spread, guess = level_numbers(level)
    rows = 2 * SUBLANES

    def body(x0):
        for y0 in range(0, count_y, rows):
            found = neighbour_block(source, x0, y0, rows, BLOCK, 2**level)
            values = [(1.0 - RELAXATION) * c + (spread * guess) * n for c, n in found]
            for x in range(BLOCK // 2):
                slot = y0 // rows * (BLOCK // 2) + x
                rows_ref[slot] = values[2 * x] + values[2 * x + 1]
                total = (
                    rows_ref[slot, pl.ds(0, SUBLANES, stride=2), :]
                    + rows_ref[slot, pl.ds(1, SUBLANES, stride=2), :]
                )
                target[x0 // 2 + x + 1, pl.ds(SUBLANES + y0 // 2, SUBLANES), :] = 0.125 * pair_lanes(
                    total, 2**level
                )

    over_blocks(count_x, body)
    fill_rims(target, 1, count_x // 2, count_y // 2)


def relax_rows(count_x, count_y, level, guess_ref, source, emit):
    spread, guess = level_numbers(level)
    rows = min(2 * SUBLANES, count_y)

    def body(x0):
        for y0 in range(0, count_y, rows):
            found = neighbour_block(guess_ref, x0, y0, rows, BLOCK, 2**level)
            for x, (center, around) in enumerate(found):
                right = source[x0 + x + 1, pl.ds(SUBLANES + y0, rows), :]
                value = (1.0 - RELAXATION) * center + guess * right + (guess * spread) * around
                emit(x0 + x, y0, rows, value)

    over_blocks(count_x, body)


def prolong_into(count_x, count_y, level, coarse, source, target):
    guess = level_numbers(level)[1]

    def body(x0):
        for y0 in range(0, count_y, 2 * SUBLANES):
            for half in range(BLOCK // 2):
                value = coarse(x0 // 2 + half, y0 // 2)
                for part in range(2):
                    at = x0 + 2 * half + part + 1
                    for row in range(2):
                        rows = pl.ds(SUBLANES + y0 + row, SUBLANES, stride=2)
                        target[at, rows, :] = value + guess * source[at, rows, :]

    over_blocks(count_x, body)
    fill_rims(target, 1, count_x, count_y)


def place_potential(sz, pots, psi, pot, sums):
    per = sz.tile_x // sz.groups
    slot = lanes_of(1) // sz.chunk
    here_group = lax.axis_index("band")
    for index in range(sz.tiles_x * sz.tiles_y):
        shift_y, shift_x = divmod(index, sz.tiles_x)
        tile_x, tile_y = tile_at(sz, index)
        at_y = pl.multiple_of(tile_y * sz.tile_y, 16)
        total = jnp.zeros((sz.tile_y, LANES), jnp.float32)
        for g in range(sz.groups):
            value = None
            for shift_b in range(sz.groups):
                source = partner(here_group, shift_b, sz.groups)
                at = (shift_b * sz.tiles_x + shift_x) * sz.pot_rows
                piece = pots[shift_y][at : at + sz.pot_rows, :]
                chosen = slot == lax.rem(source + g, sz.groups)
                value = piece if value is None else jnp.where(chosen, piece, value)
            if g:
                value = pltpu.roll(value, LANES - g * sz.chunk, 1)
            for k in range(per):
                cell_x = tile_x * sz.tile_x + g * per + k
                plane = value[k * sz.tile_y : (k + 1) * sz.tile_y]
                pot[cell_x, pl.ds(at_y, sz.tile_y), :] = plane
                center = psi[cell_x + 3, pl.ds(at_y + SUBLANES, sz.tile_y), :]
                total = total + plane * (center * center)
        sums[tile_x * sz.tiles_y + tile_y] = total
    total = sums[0]
    for tile in range(1, sz.tiles_x * sz.tiles_y):
        total = total + sums[tile]
    return total


def step_kernel(sz, *refs):
    pots, refs = refs[: sz.tiles_y], refs[sz.tiles_y :]
    (psi, hpsi, spsi, w_ref, a_ref, wz_ref, par_ref, sums_ref), refs = refs[:8], refs[8:]
    (bands_ref, resid_ref, energy_ref), refs = refs[:3], refs[3:]
    (pot, corr, res, zfield, direct, change, b1, z1, x1, b2, x2, rows_ref, parts, q_ref, zkin, tile_sums) = refs
    nx, ny = sz.grid_x, sz.grid_y
    here_x, here_y = lax.axis_index("dx"), lax.axis_index("dy")
    total = place_potential(sz, pots, psi, pot, tile_sums)
    energy = (jnp.sum(total) + jnp.sum(sums_ref[0:1, :])) / jnp.sum(sums_ref[1:2, :])
    energy_ref[0] = energy

    def residual(x0):
        for x in range(BLOCK):
            center = psi[x0 + x + 3, pl.ds(SUBLANES, ny), :]
            value = hpsi[x0 + x] + pot[x0 + x] * center - energy * spsi[x0 + x]
            res[x0 + x + 1, pl.ds(SUBLANES, ny), :] = value

    over_blocks(nx, residual)
    fill_rims(res, 1, nx, ny)
    restrict_into(nx, ny, 0, res, b1, rows_ref)
    restrict_into(nx // 2, ny // 2, 1, b1, b2, rows_ref)
    quarter_x, quarter_y = nx // 4, ny // 4
    x2[...] = level_numbers(2)[1] * b2[...]
    for _ in range(COARSE_SWEEPS):
        planes = []
        relax_rows(quarter_x, quarter_y, 2, x2, b2, lambda *piece: planes.append(piece))
        for x, y0, rows, value in planes:
            x2[x + 1, pl.ds(SUBLANES + y0, rows), :] = value
        fill_rims(x2, 1, quarter_x, quarter_y)
    coarse_two = lambda x, y: x2[x + 1, pl.ds(SUBLANES + y, SUBLANES), :]
    prolong_into(nx // 2, ny // 2, 1, coarse_two, b1, z1)

    def emit_one(x, y0, rows, value):
        x1[x, pl.ds(y0, rows), :] = value

    relax_rows(nx // 2, ny // 2, 1, z1, b1, emit_one)
    prolong_into(nx, ny, 0, lambda x, y: x1[x, pl.ds(y, SUBLANES), :], res, zfield)

    def emit_zero(x, y0, rows, value):
        direct[x + 3, pl.ds(SUBLANES + y0, rows), :] = value
        cells = pl.ds(pl.multiple_of(x * ny + y0, 16), rows)
        high, low = split(value)
        parts[cells, :LANES] = high
        parts[cells, LANES:] = low

    relax_rows(nx, ny, 0, zfield, res, emit_zero)
    fill_rims(direct, 3, nx, ny)
    zkin[...] = dot(parts[...], depth_matrix())
    active = active_columns(par_ref[2])
    columns = intersections(sz, w_ref, parts[...], wz_ref, active)
    q_ref[sz.factors :, LANES:] = jnp.zeros((sz.factors, LANES), jnp.bfloat16)
    matrix = par_ref[0] - energy * par_ref[1]
    projector_sources(sz, matrix, inner_lanes(columns), active, wz_ref, q_ref)

    def emit_change(at, rows, value):
        corr[at : at + rows, :] = value + zkin[at : at + rows, :]

    add_projectors(sz, a_ref, q_ref, emit_change)

    def line(index, carry):
        x0, (over, under) = index * BLOCK, carry
        for y0 in range(0, ny, SUBLANES):
            rows = pl.ds(y0, SUBLANES)
            for x, (center, value) in enumerate(planar_kinetic(direct, x0, y0, SUBLANES, BLOCK)):
                cells = pl.ds(pl.multiple_of((x0 + x) * ny + y0, SUBLANES), SUBLANES)
                value = value + (pot[x0 + x, rows, :] - energy) * center
                value = value + (1.0 / DEPTH_SCALE) * corr[cells, :]
                change[x0 + x, rows, :] = value
                over = over + value * res[x0 + x + 1, pl.ds(SUBLANES + y0, SUBLANES), :]
                under = under + value * value
        return over, under

    zero = jnp.zeros((SUBLANES, LANES), jnp.float32)
    over, under = lax.fori_loop(0, nx // BLOCK, line, (zero, zero))
    step = -jnp.sum(over) / jnp.sum(under)
    at_x, at_y = here_x * sz.tile_x, pl.multiple_of(here_y * sz.tile_y, 16)
    for x in range(sz.tile_x):
        cell = at_x + x
        inner = pl.ds(at_y + SUBLANES, sz.tile_y)
        bands_ref[0, x] = psi[cell + 3, inner, :] + step * direct[cell + 3, inner, :]
        resid_ref[0, x] = res[cell + 1, inner, :] + step * change[cell, pl.ds(at_y, sz.tile_y), :]


def partner(here, turn, count):
    return here ^ turn if count & (count - 1) == 0 else (here + turn) % count


def gathered(value, axis):
    count = lax.axis_size(axis)
    pairs = lambda turn: [(partner(i, turn, count), i) for i in range(count)]
    found = [value]
    for turn in range(1, count):
        found.append(lax.ppermute(value, axis, pairs(turn)))
    return found


def replicated(sz, wave_bands, potential, atom_offsets, proj_counts, dh_matrix, ds_matrix):
    vmem = pl.BlockSpec(memory_space=pltpu.VMEM)
    smem = pl.BlockSpec(memory_space=pltpu.SMEM)
    hbm = pl.BlockSpec(memory_space=pltpu.HBM)
    shape = lambda *dims: jax.ShapeDtypeStruct(dims, jnp.float32)
    half = lambda *dims: jax.ShapeDtypeStruct(dims, jnp.bfloat16)
    scratch = lambda *dims: pltpu.VMEM(dims, jnp.float32)
    grant = pltpu.CompilerParams(vmem_limit_bytes=VMEM_GRANT)
    cost = lambda flops: pl.CostEstimate(flops=flops, transcendentals=0, bytes_accessed=0)
    inputs = (
        wave_bands.reshape(sz.wave_rows, LANES),
        potential,
        atom_offsets.transpose(0, 3, 1, 2),
        proj_counts,
        dh_matrix.transpose(0, 1, 3, 2, 4),
        ds_matrix.transpose(0, 1, 3, 2, 4),
    )
    own = pl.pallas_call(
        functools.partial(pack_kernel, sz),
        out_shape=shape(sz.rows, LANES),
        in_specs=[hbm] * 6,
        out_specs=vmem,
        scratch_shapes=[
            scratch(*inputs[1].shape),
            pltpu.SMEM(inputs[2].shape, jnp.int32),
            pltpu.SMEM(inputs[3].shape, jnp.int32),
            scratch(*inputs[4].shape),
            scratch(*inputs[5].shape),
            pltpu.SemaphoreType.DMA((6,)),
        ],
        compiler_params=grant,
        name="pack",
    )(*(pltpu.with_memory_space_constraint(value, pltpu.HBM) for value in inputs))
    line = gathered(own, "dx")
    crossed = [gathered(block, "dy") for block in line]
    blocks = [each[turn] for turn in range(sz.tiles_y) for each in crossed]
    pieces = [block[sz.wave_rows : sz.wave_rows + sz.pot_rows] for block in line]
    chunks = jnp.concatenate(gathered(jnp.concatenate(pieces, axis=0), "band"), axis=0)
    pots = gathered(chunks, "dy")
    nx, ny = sz.grid_x, sz.grid_y
    padded = lambda x, y, width: (x + 2 * width, y + 2 * SUBLANES, LANES)
    q_scratch = pltpu.VMEM((2 * sz.factors, 2 * LANES), jnp.bfloat16)
    psi, spsi, zkin, inner, w, a, wz, par = pl.pallas_call(
        functools.partial(first_kernel, sz),
        out_shape=(
            shape(*padded(nx, ny, 3)),
            shape(nx, ny, LANES),
            shape(sz.cells, LANES),
            shape(sz.all_atoms, LANES),
            half(2 * sz.factors, sz.cells),
            half(sz.cells, 2 * sz.factors),
            shape(6, sz.all_atoms, LANES),
            shape(3, sz.all_atoms, LANES),
        ),
        in_specs=[vmem] * len(blocks),
        out_specs=(vmem,) * 8,
        scratch_shapes=[pltpu.VMEM((sz.cells, 2 * LANES), jnp.bfloat16), q_scratch]
        + [scratch(2 * sz.factors // LANES, n, LANES) for n in (nx, ny)],
        compiler_params=grant,
        cost_estimate=cost(3_000_000_000),
        name="first",
    )(*blocks)
    hpsi, sums = pl.pallas_call(
        functools.partial(second_kernel, sz),
        out_shape=(shape(nx, ny, LANES), shape(2, LANES)),
        in_specs=[vmem] * 7,
        out_specs=(vmem,) * 2,
        scratch_shapes=[q_scratch],
        compiler_params=grant,
        cost_estimate=cost(2_000_000_000),
        name="second",
    )(psi, spsi, zkin, inner, a, wz, par)
    made = (psi, hpsi, spsi, w, a, wz, par, sums)
    return pl.pallas_call(
        functools.partial(step_kernel, sz),
        out_shape=(
            jax.ShapeDtypeStruct(wave_bands.shape, jnp.float32),
            jax.ShapeDtypeStruct(wave_bands.shape, jnp.float32),
            shape(1),
        ),
        in_specs=[vmem] * (len(pots) + 8),
        out_specs=(vmem, vmem, smem),
        scratch_shapes=[
            scratch(nx, ny, LANES),
            scratch(sz.cells, LANES),
            scratch(*padded(nx, ny, 1)),
            scratch(*padded(nx, ny, 1)),
            scratch(*padded(nx, ny, 3)),
            scratch(nx, ny, LANES),
            scratch(*padded(nx // 2, ny // 2, 1)),
            scratch(*padded(nx // 2, ny // 2, 1)),
            scratch(nx // 2, ny // 2, LANES),
            scratch(*padded(nx // 4, ny // 4, 1)),
            scratch(*padded(nx // 4, ny // 4, 1)),
            scratch(ny // 2 // SUBLANES * (BLOCK // 2), 2 * SUBLANES, LANES),
            pltpu.VMEM((sz.cells, 2 * LANES), jnp.bfloat16),
            pltpu.VMEM((2 * sz.factors, 2 * LANES), jnp.bfloat16),
            scratch(sz.cells, LANES),
            scratch(sz.tiles_x * sz.tiles_y, sz.tile_y, LANES),
        ],
        compiler_params=grant,
        cost_estimate=cost(6_000_000_000),
        name="step",
    )(*pots, *made)


def on_device(wave_bands, potential, atom_offsets, proj_counts, dh_matrix, ds_matrix):
    sz = Sizes(
        wave_bands,
        potential,
        proj_counts.shape[2],
        lax.axis_size("dx"),
        lax.axis_size("dy"),
        lax.axis_size("band"),
    )
    step = functools.partial(replicated, sz) if sz.fits(VMEM_BUDGET) else distributed
    return step(wave_bands, potential, atom_offsets, proj_counts, dh_matrix, ds_matrix)


def solution(mesh):
    return jax.shard_map(
        on_device,
        mesh=mesh,
        in_specs=(
            P("band", "dx", "dy", None),
            P("dx", "dy", "band"),
            P("dx", "dy", None, None),
            P("dx", "dy", None),
            P("dx", "dy", None, None, None),
            P("dx", "dy", None, None, None),
        ),
        out_specs=(P("band", "dx", "dy", None), P("band", "dx", "dy", None), P("band")),
        check_vma=False,
    )
```

```python
import functools

import jax
import jax.numpy as jnp
from jax import lax
from jax.experimental import pallas as pl
from jax.experimental.pallas import tpu as pltpu
from jax.sharding import PartitionSpec as P

NPROJ = 9
COARSE_SWEEPS = 2


STENCIL = (-49.0 / 18.0, 1.5, -0.15, 1.0 / 90.0)
RELAXATION = 2.0 / 3.0
MASS_SHIFT = 0.25
AMPLITUDE = 0.15
PRECISE = lax.Precision.HIGHEST


def extended(cells, sides, width):
    for axis, dim in sides:
        count = lax.axis_size(axis)
        head = lax.slice_in_dim(cells, 0, width, axis=dim)
        tail = lax.slice_in_dim(cells, cells.shape[dim] - width, cells.shape[dim], axis=dim)
        cells = jnp.concatenate(
            [
                lax.ppermute(tail, axis, [(i, (i + 1) % count) for i in range(count)]),
                cells,
                lax.ppermute(head, axis, [((i + 1) % count, i) for i in range(count)]),
            ],
            axis=dim,
        )
    return cells


def projector_table():
    box_steps = jnp.arange(12, dtype=jnp.float32) - 6.0
    filler = jnp.ones((12, 12, 12), jnp.float32)
    along_x = box_steps[:, None, None] * filler
    along_y = box_steps[None, :, None] * filler
    along_z = box_steps[None, None, :] * filler
    radius_sq = along_x * along_x + along_y * along_y + along_z * along_z
    radial_s = jnp.exp(-radius_sq / 8.0)
    radial_p = jnp.exp(-radius_sq / 9.68) / 2.2
    radial_d = jnp.exp(-radius_sq / 11.52) / 5.76
    angular = [
        radial_s,
        radial_p * along_x,
        radial_p * along_y,
        radial_p * along_z,
        radial_d * along_x * along_y,
        radial_d * along_y * along_z,
        radial_d * along_z * along_x,
        0.5 * radial_d * (along_x * along_x - along_y * along_y),
        radial_d * (3.0 * along_z * along_z - radius_sq) * 0.28867513,
    ]
    return AMPLITUDE * jnp.stack(angular).reshape(9, 1728)


def shift_z(field, reach):
    depth = field.shape[-1]
    zeros_rim = jnp.zeros(field.shape[:-1] + (abs(reach),), field.dtype)
    if reach > 0:
        return jnp.concatenate([zeros_rim, field[..., : depth - reach]], axis=-1)
    return jnp.concatenate([field[..., -reach:], zeros_rim], axis=-1)


def kinetic_padded(padded, width, tile_x, tile_y):
    center = padded[:, width : width + tile_x, width : width + tile_y]
    laplacian = 3.0 * STENCIL[0] * center
    for reach in (1, 2, 3):
        weight = STENCIL[reach]
        laplacian = laplacian + weight * (
            padded[:, width - reach : width - reach + tile_x, width : width + tile_y]
            + padded[:, width + reach : width + reach + tile_x, width : width + tile_y]
            + padded[:, width : width + tile_x, width - reach : width - reach + tile_y]
            + padded[:, width : width + tile_x, width + reach : width + reach + tile_y]
            + shift_z(center, reach)
            + shift_z(center, -reach)
        )
    return -0.5 * laplacian


def box_targets(places, tile_x, tile_y, depth):
    box_steps = jnp.arange(12, dtype=jnp.int32)
    tile_shift = jnp.arange(3, dtype=jnp.int32) - 1
    target_x = (
        tile_shift[:, None, None, None] * tile_x + places[:, :, :, 0][..., None] - 6 + box_steps
    )
    target_y = (
        tile_shift[None, :, None, None] * tile_y + places[:, :, :, 1][..., None] - 6 + box_steps
    )
    target_z = places[:, :, :, 2][..., None] - 6 + box_steps
    target_x = jnp.where((target_x >= 0) & (target_x < tile_x), target_x, tile_x + 12)
    target_y = jnp.where((target_y >= 0) & (target_y < tile_y), target_y, tile_y + 12)
    depth_cells = jnp.arange(depth, dtype=jnp.int32)
    window = (target_z[..., None] == depth_cells).astype(jnp.float32)
    return (target_x, target_y, window)


def own_intersection(widened, atom_offsets, window, projector_rows):
    nbands = widened.shape[0]
    box_steps = jnp.arange(12, dtype=jnp.int32)
    owned = atom_offsets[0, 0]
    index_x = (owned[:, 0:1] + box_steps[None, :])[:, :, None]
    index_y = (owned[:, 1:2] + box_steps[None, :])[:, None, :]
    columns = widened[:, index_x, index_y]
    box_values = jnp.einsum("bauvz,akz->bauvk", columns, window[1, 1], precision=PRECISE)
    box_values = box_values.reshape(nbands, -1, 1728)
    return jnp.einsum("ik,bak->aib", projector_rows, box_values, precision=PRECISE)


def projector_terms(
    intersection, proj_counts, targets, dh_matrix, ds_matrix, projector_rows, field_shape
):
    nbands, tile_x, tile_y, depth = field_shape
    active = (jnp.arange(NPROJ, dtype=jnp.int32)[None, :] < proj_counts[0, 0][:, None]).astype(
        jnp.float32
    )
    intersection = intersection * active[:, :, None]
    coefficients = jnp.stack(
        [
            jnp.einsum("aij,ajb->aib", dh_matrix[0, 0], intersection, precision=PRECISE),
            jnp.einsum("aij,ajb->aib", ds_matrix[0, 0], intersection, precision=PRECISE),
        ]
    )
    coefficients = coefficients * active[None, :, :, None]
    nearby = extended(coefficients[None, None], (("dx", 0), ("dy", 1)), 1)
    spread = jnp.einsum("ik,uvhaib->hbuvak", projector_rows, nearby, precision=PRECISE)
    spread = spread.reshape(2, nbands, 3, 3, -1, 144, 12)
    target_x, target_y, window = targets
    placed = jnp.einsum("hbuvaxk,uvakz->hbuvaxz", spread, window, precision=PRECISE)
    placed = placed.reshape(2, nbands, 3, 3, -1, 12, 12, depth)
    correction = jnp.zeros((2, nbands, tile_x, tile_y, depth), jnp.float32)
    correction = correction.at[:, :, target_x[..., :, None], target_y[..., None, :]].add(
        placed, mode="drop"
    )
    return (correction[0], correction[1])


def hamiltonian(
    field, full_potential, atom_offsets, proj_counts, targets, dh_matrix, ds_matrix, projector_rows
):
    tile_x, tile_y = (field.shape[1], field.shape[2])
    widened = extended(field, (("dx", 1), ("dy", 2)), 6)
    kinetic_part = kinetic_padded(widened, 6, tile_x, tile_y)
    intersection = own_intersection(widened, atom_offsets, targets[2], projector_rows)
    corr_h, corr_s = projector_terms(
        intersection, proj_counts, targets, dh_matrix, ds_matrix, projector_rows, field.shape
    )
    return (kinetic_part + full_potential[None] * field + corr_h, field + corr_s)


def domain_sums(values):
    return lax.psum(values, ("dx", "dy"))


def diagonal_of(level):
    return 3.0 / 4.0**level + MASS_SHIFT


def tile_apply(field, level):
    padded = extended(field, (("dx", 1), ("dy", 2)), 1)
    neighbours = (
        padded[:, :-2, 1:-1]
        + padded[:, 2:, 1:-1]
        + padded[:, 1:-1, :-2]
        + padded[:, 1:-1, 2:]
        + shift_z(field, 1)
        + shift_z(field, -1)
    )
    return -0.5 * (neighbours - 6.0 * field) / 4.0**level + MASS_SHIFT * field


def pair_table(depth):
    fine_cells = jnp.arange(depth, dtype=jnp.int32)[:, None] // 2
    coarse_cells = jnp.arange(depth // 2, dtype=jnp.int32)[None, :]
    return (fine_cells == coarse_cells).astype(jnp.float32)


def restrict(field):
    nbands, size_x, size_y, size_z = field.shape
    planar = field.reshape(nbands, size_x // 2, 2, size_y // 2, 2, size_z).mean(axis=(2, 4))
    return jnp.einsum("bxyz,zw->bxyw", planar, 0.5 * pair_table(size_z), precision=PRECISE)


def prolong(field):
    size_z = field.shape[3]
    widened = jnp.repeat(jnp.repeat(field, 2, axis=1), 2, axis=2)
    return jnp.einsum("bxyw,zw->bxyz", widened, pair_table(2 * size_z), precision=PRECISE)


def precondition(source_zero):
    guess_zero = RELAXATION * source_zero / diagonal_of(0)
    source_one = restrict(source_zero - tile_apply(guess_zero, 0))
    guess_one = RELAXATION * source_one / diagonal_of(1)
    source_two = restrict(source_one - tile_apply(guess_one, 1))
    guess_two = RELAXATION * source_two / diagonal_of(2)
    for _ in range(COARSE_SWEEPS):
        guess_two = guess_two + RELAXATION * (source_two - tile_apply(guess_two, 2)) / diagonal_of(
            2
        )
    guess_one = guess_one + prolong(guess_two)
    guess_one = guess_one + RELAXATION * (source_one - tile_apply(guess_one, 1)) / diagonal_of(1)
    guess_zero = guess_zero + prolong(guess_one)
    return guess_zero + RELAXATION * (source_zero - tile_apply(guess_zero, 0)) / diagonal_of(0)


def distributed(wave_bands, potential, atom_offsets, proj_counts, dh_matrix, ds_matrix):
    projector_rows = projector_table()
    full_potential = lax.all_gather(potential, "band", axis=2, tiled=True)
    places = extended(atom_offsets, (("dx", 0), ("dy", 1)), 1)
    targets = box_targets(places, wave_bands.shape[1], wave_bands.shape[2], wave_bands.shape[3])
    h_band, s_band = hamiltonian(
        wave_bands,
        full_potential,
        atom_offsets,
        proj_counts,
        targets,
        dh_matrix,
        ds_matrix,
        projector_rows,
    )
    energy_sums = domain_sums(
        jnp.stack(
            [
                jnp.sum(wave_bands * h_band, axis=(1, 2, 3)),
                jnp.sum(wave_bands * s_band, axis=(1, 2, 3)),
            ]
        )
    )
    band_energy = energy_sums[0] / energy_sums[1]
    energy_grid = band_energy[:, None, None, None]
    residual = h_band - energy_grid * s_band
    direction = precondition(residual)
    h_dir, s_dir = hamiltonian(
        direction,
        full_potential,
        atom_offsets,
        proj_counts,
        targets,
        dh_matrix,
        ds_matrix,
        projector_rows,
    )
    change = h_dir - energy_grid * s_dir
    line_sums = domain_sums(
        jnp.stack(
            [jnp.sum(residual * change, axis=(1, 2, 3)), jnp.sum(change * change, axis=(1, 2, 3))]
        )
    )
    step_grid = (-line_sums[0] / line_sums[1])[:, None, None, None]
    return (wave_bands + step_grid * direction, residual + step_grid * change, band_energy)


BOX_LOW = 6
BOX_CELLS = 12
LANES = 128
SUBLANES = 8
RADIAL_WIDTHS = (8.0, 9.68, 11.52)
PLANE_FACTORS = (
    (0, 0, 0),
    (1, 1, 0),
    (1, 0, 1),
    (1, 0, 0),
    (2, 1, 1),
    (2, 0, 1),
    (2, 1, 0),
    (2, 2, 0),
    (2, 0, 0),
    (2, 0, 2),
)
D_SCALE = 0.28867513
DEPTH_SCALE = 180.0
BLOCK = 8
VMEM_BUDGET = 40 * 1024 * 1024
VMEM_GRANT = 24 * 1024 * 1024


class Sizes:
    def __init__(self, wave, potential, atoms, tiles_x, tiles_y, groups):
        self.tile_x, self.tile_y, self.depth = wave.shape[1:]
        self.atoms = atoms
        self.tiles_x, self.tiles_y, self.groups = tiles_x, tiles_y, groups
        self.grid_x, self.grid_y = tiles_x * self.tile_x, tiles_y * self.tile_y
        self.cells = self.grid_x * self.grid_y
        self.chunk = potential.shape[2]
        self.all_atoms = tiles_x * tiles_y * atoms
        self.wave_rows = self.tile_x * self.tile_y
        self.pot_rows = self.wave_rows // groups
        self.param_rows = -(-2 * atoms // SUBLANES) * SUBLANES
        self.rows = self.wave_rows + self.pot_rows + self.param_rows
        self.factors = len(PLANE_FACTORS) * self.all_atoms

    def fits(self, vmem_bytes):
        return (
            self.depth == LANES
            and self.chunk * self.groups == LANES
            and self.tile_x % max(self.groups, BLOCK) == 0
            and self.tile_y % 16 == 0
            and self.grid_x >= 2 * BLOCK
            and self.grid_y >= 32
            and self.all_atoms % 16 == 0
            and LANES % self.all_atoms == 0
            and self.cells * (60 * LANES + 8 * self.factors) <= vmem_bytes
        )


def lanes_of(rows=1):
    return lax.broadcasted_iota(jnp.int32, (rows, LANES), 1)


def split(value):
    high = value.astype(jnp.bfloat16)
    return high, (value - high.astype(jnp.float32)).astype(jnp.bfloat16)


def halves(value):
    return value[:, :LANES] + value[:, LANES:]


def dot(left, right):
    return jnp.dot(left, right, preferred_element_type=jnp.float32)


META_LANE = 96


def pack_kernel(sz, wave_ref, pot_ref, offs_ref, counts_ref, dh_ref, ds_ref, out_ref, *scratch):
    *places, sems = scratch
    pot, offs, counts, dh, ds = places
    start, base = sz.wave_rows, sz.wave_rows + sz.pot_rows
    sources = (pot_ref, offs_ref, counts_ref, dh_ref, ds_ref, wave_ref)
    places = places + [out_ref.at[pl.ds(0, start)]]
    copies = [
        pltpu.make_async_copy(a, b, sems.at[i])
        for i, (a, b) in enumerate(zip(sources, places))
    ]
    for copy in copies:
        copy.start()
    out_ref[base:, :] = jnp.zeros((sz.param_rows, LANES), jnp.float32)
    for copy in copies:
        copy.wait()
    per = sz.tile_x // sz.groups
    pieces = [
        pot[g * per : (g + 1) * per].reshape(sz.pot_rows, sz.chunk) for g in range(sz.groups)
    ]
    out_ref[start:base, :] = pltpu.roll(
        jnp.concatenate(pieces, axis=1), lax.axis_index("band") * sz.chunk, 1
    )
    for j in range(NPROJ):
        lanes = slice(j * NPROJ, (j + 1) * NPROJ)
        out_ref[base : base + sz.atoms, lanes] = dh[0, 0, j]
        out_ref[base + sz.atoms : base + 2 * sz.atoms, lanes] = ds[0, 0, j]
    lane = lanes_of(1)
    for a in range(sz.atoms):
        row = jnp.where(lane == META_LANE + 3, counts[0, 0, a].astype(jnp.float32), 0.0)
        for k in range(3):
            row = jnp.where(lane == META_LANE + k, offs[0, k, 0, a].astype(jnp.float32), row)
        out_ref[base + a : base + a + 1, META_LANE : META_LANE + 4] = row[:, META_LANE : META_LANE + 4]


def wrapped(cell, centre, count):
    offset = cell - centre + float(BOX_LOW)
    offset = jnp.where(offset < 0.0, offset + float(count), offset)
    offset = jnp.where(offset >= float(count), offset - float(count), offset)
    inside = offset < float(BOX_CELLS)
    return offset - float(BOX_LOW), inside


def fill_rims(ref, width, count_x, count_y):
    ref[:, 0:SUBLANES, :] = ref[:, count_y : count_y + SUBLANES, :]
    ref[:, count_y + SUBLANES : count_y + 2 * SUBLANES, :] = ref[:, SUBLANES : 2 * SUBLANES, :]
    ref[0:width] = ref[count_x : count_x + width]
    ref[count_x + width : count_x + 2 * width] = ref[width : 2 * width]


def shifted_pair(value, reach):
    lane = lanes_of(1)
    below = jnp.where(lane >= reach, pltpu.roll(value, reach, 1), 0.0)
    above = jnp.where(lane < LANES - reach, pltpu.roll(value, LANES - reach, 1), 0.0)
    return below + above


def planar_kinetic(ref, x0, y0, rows, count):
    at = lambda x, y: ref[x0 + x + 3, pl.ds(SUBLANES + y0 + y, rows), :]
    planes = [at(x, 0) for x in range(-3, count + 3)]
    found = []
    for x in range(count):
        total = (-1.5 * STENCIL[0]) * planes[x + 3]
        for reach in (1, 2, 3):
            around = (planes[x + 3 - reach] + planes[x + 3 + reach]) + (at(x, -reach) + at(x, reach))
            total = total + (-0.5 * STENCIL[reach]) * around
        found.append((planes[x + 3], total))
    return found


def depth_matrix():
    row = lax.broadcasted_iota(jnp.int32, (2 * LANES, LANES), 0) % LANES
    reach = jnp.abs(row - lax.broadcasted_iota(jnp.int32, (2 * LANES, LANES), 1))
    value = jnp.zeros((2 * LANES, LANES), jnp.float32)
    for k in (1, 2, 3):
        value = jnp.where(reach == k, -0.5 * STENCIL[k] * DEPTH_SCALE, value)
    return value.astype(jnp.bfloat16)


def neighbour_block(ref, x0, y0, rows, count, step):
    at = lambda x, y: ref[x0 + x + 1, pl.ds(SUBLANES + y0 + y, rows), :]
    planes = [at(x, 0) for x in range(-1, count + 1)]
    found = []
    for x in range(count):
        center = planes[x + 1]
        around = (planes[x] + planes[x + 2]) + (at(x, -1) + at(x, 1)) + shifted_pair(center, step)
        found.append((center, around))
    return found


def over_blocks(count, body):
    for x0 in range(0, count, BLOCK):
        body(x0)


def plane_weights(sz, meta, w_ref, a_ref, wx_ref, wy_ref):
    atoms = sz.all_atoms
    widths = [-1.0 / w for w in RADIAL_WIDTHS]
    for tile in range(sz.cells // LANES):
        cell = lanes_of(1) + tile * LANES
        cell_x = (cell // sz.grid_y).astype(jnp.float32)
        cell_y = (cell % sz.grid_y).astype(jnp.float32)
        for start in range(0, atoms, 16):
            rx, inside_x = wrapped(cell_x, meta[start : start + 16, 0:1], sz.grid_x)
            ry, inside_y = wrapped(cell_y, meta[start : start + 16, 1:2], sz.grid_y)
            square = rx * rx + ry * ry
            inside = jnp.logical_and(inside_x, inside_y)
            radial = [jnp.where(inside, jnp.exp(square * w), 0.0) for w in widths]
            powers_x, powers_y = [None, rx, rx * rx], [None, ry, ry * ry]
            for index, (kind, px, py) in enumerate(PLANE_FACTORS):
                value = radial[kind]
                value = value if px == 0 else value * powers_x[px]
                value = value if py == 0 else value * powers_y[py]
                high, low = split(value)
                at = index * atoms + start
                lanes = slice(tile * LANES, (tile + 1) * LANES)
                w_ref[at : at + 16, lanes] = high
                w_ref[sz.factors + at : sz.factors + at + 16, lanes] = low
    turned = jnp.concatenate([meta] * (LANES // atoms), axis=0).T
    tiles = 2 * sz.factors // LANES
    for axis, count, ref in ((0, sz.grid_x, wx_ref), (1, sz.grid_y, wy_ref)):
        centre = turned[axis : axis + 1, :]
        cell = lax.broadcasted_iota(jnp.int32, (count, LANES), 0).astype(jnp.float32)
        offset, inside = wrapped(cell, centre, count)
        radial = [jnp.where(inside, jnp.exp(offset * offset * w), 0.0) for w in widths]
        powers = [1.0, offset, offset * offset]
        for tile in range(tiles):
            place = lanes_of(1) // atoms + tile * (LANES // atoms)
            value = None
            for slot in range(LANES // atoms):
                index = tile * (LANES // atoms) + slot
                kind, *power = PLANE_FACTORS[index % len(PLANE_FACTORS)]
                term = radial[kind] if power[axis] == 0 else radial[kind] * powers[power[axis]]
                value = term if value is None else jnp.where(place == index, term, value)
            ref[tile] = value

    def planes(x):
        rows = pl.ds(pl.multiple_of(x * sz.grid_y, 16), sz.grid_y)
        for tile in range(tiles):
            lanes = slice(tile * LANES, (tile + 1) * LANES)
            value = wx_ref[tile, pl.ds(x, 1), :] * wy_ref[tile]
            high = value.astype(jnp.bfloat16)
            if (tile + 1) * LANES > sz.factors:
                low = value - high.astype(jnp.float32)
                if tile * LANES < sz.factors:
                    low = jnp.where(lanes_of(1) + tile * LANES < sz.factors, value, low)
                high = low.astype(jnp.bfloat16)
            a_ref[rows, lanes] = high

    lax.fori_loop(0, sz.grid_x, lambda x, c: (planes(x), c)[1], 0, unroll=4)


def depth_weights(meta, wz_ref):
    offset = lanes_of(1).astype(jnp.float32) - meta[:, 2:3]
    inside = jnp.logical_and(offset >= -float(BOX_LOW), offset < float(BOX_CELLS - BOX_LOW))
    radial = [
        jnp.where(inside, (AMPLITUDE * scale) * jnp.exp(offset * offset * (-1.0 / w)), 0.0)
        for scale, w in zip((1.0, 1.0 / 2.2, 1.0 / 5.76), RADIAL_WIDTHS)
    ]
    wz_ref[0] = radial[0]
    wz_ref[1] = radial[1]
    wz_ref[2] = radial[1] * offset
    wz_ref[3] = radial[2]
    wz_ref[4] = radial[2] * offset
    wz_ref[5] = radial[2] * (offset * offset)


def plane_sums(sz, w_ref, parts, x0):
    cells = slice(x0 * sz.grid_y, (x0 + BLOCK) * sz.grid_y)
    field = parts[cells, :]
    sums = dot(w_ref[:, cells], field)
    return halves(sums[: sz.factors]) + sums[sz.factors :, :LANES]


def intersections(sz, sums, wz_ref, active):
    u = [sums[c * sz.all_atoms : (c + 1) * sz.all_atoms] for c in range(len(PLANE_FACTORS))]
    products = [
        u[0] * wz_ref[0],
        u[1] * wz_ref[1],
        u[2] * wz_ref[1],
        u[3] * wz_ref[2],
        u[4] * wz_ref[3],
        u[5] * wz_ref[4],
        u[6] * wz_ref[4],
        (0.5 * (u[7] - u[9])) * wz_ref[3],
        D_SCALE * (2.0 * u[8] * wz_ref[5] - (u[7] + u[9]) * wz_ref[3]),
    ]
    return [jnp.sum(p, axis=1, keepdims=True) * active[i] for i, p in enumerate(products)]


def active_columns(meta):
    return [(meta[:, 3:4] > float(i)).astype(jnp.float32) for i in range(NPROJ)]


def inner_lanes(columns):
    lane = lanes_of(1)
    inner = jnp.zeros((columns[0].shape[0], LANES), jnp.float32)
    for k in range(NPROJ):
        inner = jnp.where(jnp.logical_and(lane % NPROJ == k, lane < NPROJ * NPROJ), columns[k], inner)
    return inner


def projector_sources(sz, matrix, inner, active, wz_ref, q_ref):
    lane = lanes_of(1)
    terms = DEPTH_SCALE * (matrix * inner)
    coef = [
        jnp.sum(jnp.where(lane // NPROJ == i, terms, 0.0), axis=1, keepdims=True) * active[i]
        for i in range(NPROJ)
    ]
    tilt = (0.5 * coef[7]) * wz_ref[3]
    ring = (D_SCALE * coef[8]) * wz_ref[3]
    blocks = [
        coef[0] * wz_ref[0],
        coef[1] * wz_ref[1],
        coef[2] * wz_ref[1],
        coef[3] * wz_ref[2],
        coef[4] * wz_ref[3],
        coef[5] * wz_ref[4],
        coef[6] * wz_ref[4],
        tilt - ring,
        (2.0 * D_SCALE * coef[8]) * wz_ref[5],
        -(tilt + ring),
    ]
    for index, block in enumerate(blocks):
        at = index * sz.all_atoms
        high, low = split(block)
        q_ref[at : at + sz.all_atoms, :LANES] = high
        q_ref[at : at + sz.all_atoms, LANES:] = low
        q_ref[sz.factors + at : sz.factors + at + sz.all_atoms, :LANES] = high


def tile_at(sz, index):
    turn_y, turn_x = divmod(index, sz.tiles_x)
    tile_x = partner(lax.axis_index("dx"), turn_x, sz.tiles_x)
    tile_y = partner(lax.axis_index("dy"), turn_y, sz.tiles_y)
    return tile_x, tile_y


def add_projectors(sz, a_ref, q_ref, emit):
    part = sz.cells // 2
    for at in range(0, sz.cells, part):
        emit(at, part, halves(dot(a_ref[at : at + part, :], q_ref[...])))


def first_kernel(sz, *refs):
    blocks, refs = refs[: sz.tiles_x * sz.tiles_y], refs[sz.tiles_x * sz.tiles_y :]
    (psi, zkin, inner_ref, w_ref, a_ref, wz_ref, par_ref, parts, wx_ref, wy_ref) = refs
    nx, ny = sz.grid_x, sz.grid_y
    for index, block in enumerate(blocks):
        tile_x, tile_y = tile_at(sz, index)
        at_y = pl.multiple_of(tile_y * sz.tile_y, 16)
        for x in range(sz.tile_x):
            value = block[x * sz.tile_y : (x + 1) * sz.tile_y, :]
            cell_x = tile_x * sz.tile_x + x
            psi[cell_x + 3, pl.ds(at_y + SUBLANES, sz.tile_y), :] = value
            rows = pl.ds(pl.multiple_of(cell_x * ny + at_y, 16), sz.tile_y)
            high, low = split(value)
            parts[rows, :LANES] = high
            parts[rows, LANES:] = low
        tile = tile_x * sz.tiles_y + tile_y
        for k in range(2):
            at = sz.wave_rows + sz.pot_rows + k * sz.atoms
            par_ref[k, pl.ds(tile * sz.atoms, sz.atoms), :] = block[at : at + sz.atoms, :]
    fill_rims(psi, 3, nx, ny)
    owners = lax.broadcasted_iota(jnp.int32, (sz.all_atoms, LANES), 0) // sz.atoms
    lane = lanes_of(sz.all_atoms)
    meta = pltpu.roll(par_ref[0], LANES - META_LANE, 1)
    meta = meta + jnp.where(lane == 0, (owners // sz.tiles_y * sz.tile_x).astype(jnp.float32), 0.0)
    meta = meta + jnp.where(lane == 1, (owners % sz.tiles_y * sz.tile_y).astype(jnp.float32), 0.0)
    par_ref[2] = meta
    depth_weights(meta, wz_ref)
    plane_weights(sz, meta, w_ref, a_ref, wx_ref, wy_ref)
    active = active_columns(meta)
    sums = None
    for x0 in range(0, nx, BLOCK):
        term = plane_sums(sz, w_ref, parts, x0)
        sums = term if sums is None else sums + term
    columns = intersections(sz, sums, wz_ref, active)
    zkin[...] = dot(parts[...], depth_matrix())
    inner = inner_lanes(columns)
    inner_ref[...] = inner


def second_kernel(sz, *refs):
    (psi, zkin, inner_ref, a_ref, wz_ref, par_ref, hpsi, spsi, sums_ref, q_ref) = refs
    nx, ny = sz.grid_x, sz.grid_y
    q_ref[sz.factors :, LANES:] = jnp.zeros((sz.factors, LANES), jnp.bfloat16)
    active = active_columns(par_ref[2])
    projector_sources(sz, par_ref[1], inner_ref[...], active, wz_ref, q_ref)

    def emit_s(at, rows, value):
        x0, count = at // ny, rows // ny
        center = psi[x0 + 3 : x0 + 3 + count, SUBLANES : SUBLANES + ny, :]
        spsi[x0 : x0 + count] = center + (1.0 / DEPTH_SCALE) * value.reshape(count, ny, LANES)

    add_projectors(sz, a_ref, q_ref, emit_s)
    projector_sources(sz, par_ref[0], inner_ref[...], active, wz_ref, q_ref)
    for x0 in range(0, nx, BLOCK):
        for y0 in range(0, ny, SUBLANES):
            for x, (_, value) in enumerate(planar_kinetic(psi, x0, y0, SUBLANES, BLOCK)):
                hpsi[x0 + x, y0 : y0 + SUBLANES, :] = value
    found = []

    def emit_h(at, rows, value):
        planes = slice(at // ny, (at + rows) // ny)
        shape = (rows // ny, ny, LANES)
        center = psi[at // ny + 3 : (at + rows) // ny + 3, SUBLANES : SUBLANES + ny, :]
        value = (1.0 / DEPTH_SCALE) * (value + zkin[at : at + rows, :]).reshape(shape)
        value = value + hpsi[planes]
        hpsi[planes] = value
        found.append((folded(value * center), folded(spsi[planes] * center)))

    add_projectors(sz, a_ref, q_ref, emit_h)
    for row in range(2):
        total = found[0][row] + found[1][row]
        sums_ref[row : row + 1, :] = jnp.sum(total, axis=0, keepdims=True)


def folded(value):
    return jnp.sum(value.reshape(-1, SUBLANES, LANES), axis=0)


def pair_lanes(value, step):
    lane = lanes_of(1)
    other = jnp.where(
        (lane // step) % 2 == 1, pltpu.roll(value, step, 1), pltpu.roll(value, LANES - step, 1)
    )
    return value + other


def level_numbers(level):
    return 0.5 / 4.0**level, RELAXATION / diagonal_of(level)


def restrict_into(count_x, count_y, level, source, target, rows_ref):
    spread, guess = level_numbers(level)
    rows = 2 * SUBLANES

    def body(x0):
        for y0 in range(0, count_y, rows):
            found = neighbour_block(source, x0, y0, rows, BLOCK, 2**level)
            values = [(1.0 - RELAXATION) * c + (spread * guess) * n for c, n in found]
            for x in range(BLOCK // 2):
                slot = y0 // rows * (BLOCK // 2) + x
                rows_ref[slot] = values[2 * x] + values[2 * x + 1]
                total = (
                    rows_ref[slot, pl.ds(0, SUBLANES, stride=2), :]
                    + rows_ref[slot, pl.ds(1, SUBLANES, stride=2), :]
                )
                target[x0 // 2 + x + 1, pl.ds(SUBLANES + y0 // 2, SUBLANES), :] = 0.125 * pair_lanes(
                    total, 2**level
                )

    over_blocks(count_x, body)
    fill_rims(target, 1, count_x // 2, count_y // 2)


def relax_rows(count_x, count_y, level, guess_ref, source, emit, after_block=lambda x0: None):
    spread, guess = level_numbers(level)
    rows = min(2 * SUBLANES, count_y)

    def body(x0):
        for y0 in range(0, count_y, rows):
            found = neighbour_block(guess_ref, x0, y0, rows, BLOCK, 2**level)
            for x, (center, around) in enumerate(found):
                right = source[x0 + x + 1, pl.ds(SUBLANES + y0, rows), :]
                value = (1.0 - RELAXATION) * center + guess * right + (guess * spread) * around
                emit(x0 + x, y0, rows, value)
        after_block(x0)

    over_blocks(count_x, body)


def prolong_into(count_x, count_y, level, coarse, source, target):
    guess = level_numbers(level)[1]

    def body(x0):
        for y0 in range(0, count_y, 2 * SUBLANES):
            for half in range(BLOCK // 2):
                value = coarse(x0 // 2 + half, y0 // 2)
                for part in range(2):
                    at = x0 + 2 * half + part + 1
                    for row in range(2):
                        rows = pl.ds(SUBLANES + y0 + row, SUBLANES, stride=2)
                        target[at, rows, :] = value + guess * source[at, rows, :]

    over_blocks(count_x, body)
    fill_rims(target, 1, count_x, count_y)


def place_potential(sz, pots, psi, pot, sums):
    per = sz.tile_x // sz.groups
    slot = lanes_of(1) // sz.chunk
    here_group = lax.axis_index("band")
    for index in range(sz.tiles_x * sz.tiles_y):
        shift_y, shift_x = divmod(index, sz.tiles_x)
        tile_x, tile_y = tile_at(sz, index)
        at_y = pl.multiple_of(tile_y * sz.tile_y, 16)
        total = jnp.zeros((sz.tile_y, LANES), jnp.float32)
        for g in range(sz.groups):
            value = None
            for shift_b in range(sz.groups):
                source = partner(here_group, shift_b, sz.groups)
                at = (shift_b * sz.tiles_x + shift_x) * sz.pot_rows
                piece = pots[shift_y][at : at + sz.pot_rows, :]
                chosen = slot == lax.rem(source + g, sz.groups)
                value = piece if value is None else jnp.where(chosen, piece, value)
            if g:
                value = pltpu.roll(value, LANES - g * sz.chunk, 1)
            for k in range(per):
                cell_x = tile_x * sz.tile_x + g * per + k
                plane = value[k * sz.tile_y : (k + 1) * sz.tile_y]
                pot[cell_x, pl.ds(at_y, sz.tile_y), :] = plane
                center = psi[cell_x + 3, pl.ds(at_y + SUBLANES, sz.tile_y), :]
                total = total + plane * (center * center)
        sums[tile_x * sz.tiles_y + tile_y] = total
    total = sums[0]
    for tile in range(1, sz.tiles_x * sz.tiles_y):
        total = total + sums[tile]
    return total


def step_kernel(sz, *refs):
    pots, refs = refs[: sz.tiles_y], refs[sz.tiles_y :]
    (psi, hpsi, spsi, w_ref, a_ref, wz_ref, par_ref, sums_ref), refs = refs[:8], refs[8:]
    (bands_ref, resid_ref, energy_ref), refs = refs[:3], refs[3:]
    (pot, res, zfield, direct, change, b1, z1, x1, b2, x2, rows_ref, parts, q_ref, zkin, tile_sums) = refs
    nx, ny = sz.grid_x, sz.grid_y
    here_x, here_y = lax.axis_index("dx"), lax.axis_index("dy")
    total = place_potential(sz, pots, psi, pot, tile_sums)
    energy = (jnp.sum(total) + jnp.sum(sums_ref[0:1, :])) / jnp.sum(sums_ref[1:2, :])
    energy_ref[0] = energy

    def residual(x0):
        for x in range(BLOCK):
            center = psi[x0 + x + 3, pl.ds(SUBLANES, ny), :]
            value = hpsi[x0 + x] + pot[x0 + x] * center - energy * spsi[x0 + x]
            res[x0 + x + 1, pl.ds(SUBLANES, ny), :] = value

    over_blocks(nx, residual)
    fill_rims(res, 1, nx, ny)
    restrict_into(nx, ny, 0, res, b1, rows_ref)
    restrict_into(nx // 2, ny // 2, 1, b1, b2, rows_ref)
    quarter_x, quarter_y = nx // 4, ny // 4
    x2[...] = level_numbers(2)[1] * b2[...]
    for _ in range(COARSE_SWEEPS):
        planes = []
        relax_rows(quarter_x, quarter_y, 2, x2, b2, lambda *piece: planes.append(piece))
        for x, y0, rows, value in planes:
            x2[x + 1, pl.ds(SUBLANES + y0, rows), :] = value
        fill_rims(x2, 1, quarter_x, quarter_y)
    coarse_two = lambda x, y: x2[x + 1, pl.ds(SUBLANES + y, SUBLANES), :]
    prolong_into(nx // 2, ny // 2, 1, coarse_two, b1, z1)

    def emit_one(x, y0, rows, value):
        x1[x, pl.ds(y0, rows), :] = value

    relax_rows(nx // 2, ny // 2, 1, z1, b1, emit_one)
    prolong_into(nx, ny, 0, lambda x, y: x1[x, pl.ds(y, SUBLANES), :], res, zfield)

    def emit_zero(x, y0, rows, value):
        direct[x + 3, pl.ds(SUBLANES + y0, rows), :] = value
        cells = slice(x * ny + y0, x * ny + y0 + rows)
        high, low = split(value)
        parts[cells, :LANES] = high
        parts[cells, LANES:] = low

    found = []

    def after_block(x0):
        cells = slice(x0 * ny, (x0 + BLOCK) * ny)
        zkin[cells, :] = dot(parts[cells, :], depth_matrix())
        term = plane_sums(sz, w_ref, parts, x0)
        found.append(term if not found else found[-1] + term)

    relax_rows(nx, ny, 0, zfield, res, emit_zero, after_block)
    fill_rims(direct, 3, nx, ny)
    active = active_columns(par_ref[2])
    columns = intersections(sz, found[-1], wz_ref, active)
    for x0 in range(0, nx, BLOCK):
        for y0 in range(0, ny, SUBLANES):
            for x, (center, value) in enumerate(planar_kinetic(direct, x0, y0, SUBLANES, BLOCK)):
                rows = slice(y0, y0 + SUBLANES)
                change[x0 + x, rows, :] = value + (pot[x0 + x, rows, :] - energy) * center
    q_ref[sz.factors :, LANES:] = jnp.zeros((sz.factors, LANES), jnp.bfloat16)
    matrix = par_ref[0] - energy * par_ref[1]
    projector_sources(sz, matrix, inner_lanes(columns), active, wz_ref, q_ref)
    found = []

    def emit_change(at, rows, value):
        planes = slice(at // ny, (at + rows) // ny)
        shape = (rows // ny, ny, LANES)
        value = (1.0 / DEPTH_SCALE) * (value + zkin[at : at + rows, :]).reshape(shape)
        value = value + change[planes]
        change[planes] = value
        before = res[at // ny + 1 : (at + rows) // ny + 1, SUBLANES : SUBLANES + ny, :]
        found.append((folded(value * before), folded(value * value)))

    add_projectors(sz, a_ref, q_ref, emit_change)
    over, under = (found[0][k] + found[1][k] for k in range(2))
    step = -jnp.sum(over) / jnp.sum(under)
    at_x, at_y = here_x * sz.tile_x, pl.multiple_of(here_y * sz.tile_y, 16)
    for x in range(sz.tile_x):
        cell = at_x + x
        inner = pl.ds(at_y + SUBLANES, sz.tile_y)
        bands_ref[0, x] = psi[cell + 3, inner, :] + step * direct[cell + 3, inner, :]
        resid_ref[0, x] = res[cell + 1, inner, :] + step * change[cell, pl.ds(at_y, sz.tile_y), :]


def partner(here, turn, count):
    return here ^ turn if count & (count - 1) == 0 else (here + turn) % count


def gathered(value, axis):
    count = lax.axis_size(axis)
    pairs = lambda turn: [(partner(i, turn, count), i) for i in range(count)]
    found = [value]
    for turn in range(1, count):
        found.append(lax.ppermute(value, axis, pairs(turn)))
    return found


def replicated(sz, wave_bands, potential, atom_offsets, proj_counts, dh_matrix, ds_matrix):
    vmem = pl.BlockSpec(memory_space=pltpu.VMEM)
    smem = pl.BlockSpec(memory_space=pltpu.SMEM)
    hbm = pl.BlockSpec(memory_space=pltpu.HBM)
    shape = lambda *dims: jax.ShapeDtypeStruct(dims, jnp.float32)
    half = lambda *dims: jax.ShapeDtypeStruct(dims, jnp.bfloat16)
    scratch = lambda *dims: pltpu.VMEM(dims, jnp.float32)
    grant = pltpu.CompilerParams(vmem_limit_bytes=VMEM_GRANT)
    cost = lambda flops: pl.CostEstimate(flops=flops, transcendentals=0, bytes_accessed=0)
    inputs = (
        wave_bands.reshape(sz.wave_rows, LANES),
        potential,
        atom_offsets.transpose(0, 3, 1, 2),
        proj_counts,
        dh_matrix.transpose(0, 1, 3, 2, 4),
        ds_matrix.transpose(0, 1, 3, 2, 4),
    )
    own = pl.pallas_call(
        functools.partial(pack_kernel, sz),
        out_shape=shape(sz.rows, LANES),
        in_specs=[hbm] * 6,
        out_specs=vmem,
        scratch_shapes=[
            scratch(*inputs[1].shape),
            pltpu.SMEM(inputs[2].shape, jnp.int32),
            pltpu.SMEM(inputs[3].shape, jnp.int32),
            scratch(*inputs[4].shape),
            scratch(*inputs[5].shape),
            pltpu.SemaphoreType.DMA((6,)),
        ],
        compiler_params=grant,
        name="pack",
    )(*(pltpu.with_memory_space_constraint(value, pltpu.HBM) for value in inputs))
    line = gathered(own, "dx")
    crossed = [gathered(block, "dy") for block in line]
    blocks = [each[turn] for turn in range(sz.tiles_y) for each in crossed]
    pieces = [block[sz.wave_rows : sz.wave_rows + sz.pot_rows] for block in line]
    chunks = jnp.concatenate(gathered(jnp.concatenate(pieces, axis=0), "band"), axis=0)
    pots = gathered(chunks, "dy")
    nx, ny = sz.grid_x, sz.grid_y
    padded = lambda x, y, width: (x + 2 * width, y + 2 * SUBLANES, LANES)
    q_scratch = pltpu.VMEM((2 * sz.factors, 2 * LANES), jnp.bfloat16)
    psi, zkin, inner, w, a, wz, par = pl.pallas_call(
        functools.partial(first_kernel, sz),
        out_shape=(
            shape(*padded(nx, ny, 3)),
            shape(sz.cells, LANES),
            shape(sz.all_atoms, LANES),
            half(2 * sz.factors, sz.cells),
            half(sz.cells, 2 * sz.factors),
            shape(6, sz.all_atoms, LANES),
            shape(3, sz.all_atoms, LANES),
        ),
        in_specs=[vmem] * len(blocks),
        out_specs=(vmem,) * 7,
        scratch_shapes=[pltpu.VMEM((sz.cells, 2 * LANES), jnp.bfloat16)]
        + [scratch(2 * sz.factors // LANES, n, LANES) for n in (nx, ny)],
        compiler_params=grant,
        cost_estimate=cost(3_000_000_000),
        name="first",
    )(*blocks)
    hpsi, spsi, sums = pl.pallas_call(
        functools.partial(second_kernel, sz),
        out_shape=(shape(nx, ny, LANES), shape(nx, ny, LANES), shape(2, LANES)),
        in_specs=[vmem] * 6,
        out_specs=(vmem,) * 3,
        scratch_shapes=[q_scratch],
        compiler_params=grant,
        cost_estimate=cost(2_000_000_000),
        name="second",
    )(psi, zkin, inner, a, wz, par)
    made = (psi, hpsi, spsi, w, a, wz, par, sums)
    return pl.pallas_call(
        functools.partial(step_kernel, sz),
        out_shape=(
            jax.ShapeDtypeStruct(wave_bands.shape, jnp.float32),
            jax.ShapeDtypeStruct(wave_bands.shape, jnp.float32),
            shape(1),
        ),
        in_specs=[vmem] * (len(pots) + 8),
        out_specs=(vmem, vmem, smem),
        scratch_shapes=[
            scratch(nx, ny, LANES),
            scratch(*padded(nx, ny, 1)),
            scratch(*padded(nx, ny, 1)),
            scratch(*padded(nx, ny, 3)),
            scratch(nx, ny, LANES),
            scratch(*padded(nx // 2, ny // 2, 1)),
            scratch(*padded(nx // 2, ny // 2, 1)),
            scratch(nx // 2, ny // 2, LANES),
            scratch(*padded(nx // 4, ny // 4, 1)),
            scratch(*padded(nx // 4, ny // 4, 1)),
            scratch(ny // 2 // SUBLANES * (BLOCK // 2), 2 * SUBLANES, LANES),
            pltpu.VMEM((sz.cells, 2 * LANES), jnp.bfloat16),
            pltpu.VMEM((2 * sz.factors, 2 * LANES), jnp.bfloat16),
            scratch(sz.cells, LANES),
            scratch(sz.tiles_x * sz.tiles_y, sz.tile_y, LANES),
        ],
        compiler_params=grant,
        cost_estimate=cost(6_000_000_000),
        name="step",
    )(*pots, *made)


def on_device(wave_bands, potential, atom_offsets, proj_counts, dh_matrix, ds_matrix):
    sz = Sizes(
        wave_bands,
        potential,
        proj_counts.shape[2],
        lax.axis_size("dx"),
        lax.axis_size("dy"),
        lax.axis_size("band"),
    )
    step = functools.partial(replicated, sz) if sz.fits(VMEM_BUDGET) else distributed
    return step(wave_bands, potential, atom_offsets, proj_counts, dh_matrix, ds_matrix)


def solution(mesh):
    return jax.shard_map(
        on_device,
        mesh=mesh,
        in_specs=(
            P("band", "dx", "dy", None),
            P("dx", "dy", "band"),
            P("dx", "dy", None, None),
            P("dx", "dy", None),
            P("dx", "dy", None, None, None),
            P("dx", "dy", None, None, None),
        ),
        out_specs=(P("band", "dx", "dy", None), P("band", "dx", "dy", None), P("band")),
        check_vma=False,
    )
```

```python
import functools

import jax
import jax.numpy as jnp
from jax import lax
from jax.experimental import pallas as pl
from jax.experimental.pallas import tpu as pltpu
from jax.sharding import PartitionSpec as P

NPROJ = 9
COARSE_SWEEPS = 2


STENCIL = (-49.0 / 18.0, 1.5, -0.15, 1.0 / 90.0)
RELAXATION = 2.0 / 3.0
MASS_SHIFT = 0.25
AMPLITUDE = 0.15
PRECISE = lax.Precision.HIGHEST


def extended(cells, sides, width):
    for axis, dim in sides:
        count = lax.axis_size(axis)
        head = lax.slice_in_dim(cells, 0, width, axis=dim)
        tail = lax.slice_in_dim(cells, cells.shape[dim] - width, cells.shape[dim], axis=dim)
        cells = jnp.concatenate(
            [
                lax.ppermute(tail, axis, [(i, (i + 1) % count) for i in range(count)]),
                cells,
                lax.ppermute(head, axis, [((i + 1) % count, i) for i in range(count)]),
            ],
            axis=dim,
        )
    return cells


def projector_table():
    box_steps = jnp.arange(12, dtype=jnp.float32) - 6.0
    filler = jnp.ones((12, 12, 12), jnp.float32)
    along_x = box_steps[:, None, None] * filler
    along_y = box_steps[None, :, None] * filler
    along_z = box_steps[None, None, :] * filler
    radius_sq = along_x * along_x + along_y * along_y + along_z * along_z
    radial_s = jnp.exp(-radius_sq / 8.0)
    radial_p = jnp.exp(-radius_sq / 9.68) / 2.2
    radial_d = jnp.exp(-radius_sq / 11.52) / 5.76
    angular = [
        radial_s,
        radial_p * along_x,
        radial_p * along_y,
        radial_p * along_z,
        radial_d * along_x * along_y,
        radial_d * along_y * along_z,
        radial_d * along_z * along_x,
        0.5 * radial_d * (along_x * along_x - along_y * along_y),
        radial_d * (3.0 * along_z * along_z - radius_sq) * 0.28867513,
    ]
    return AMPLITUDE * jnp.stack(angular).reshape(9, 1728)


def shift_z(field, reach):
    depth = field.shape[-1]
    zeros_rim = jnp.zeros(field.shape[:-1] + (abs(reach),), field.dtype)
    if reach > 0:
        return jnp.concatenate([zeros_rim, field[..., : depth - reach]], axis=-1)
    return jnp.concatenate([field[..., -reach:], zeros_rim], axis=-1)


def kinetic_padded(padded, width, tile_x, tile_y):
    center = padded[:, width : width + tile_x, width : width + tile_y]
    laplacian = 3.0 * STENCIL[0] * center
    for reach in (1, 2, 3):
        weight = STENCIL[reach]
        laplacian = laplacian + weight * (
            padded[:, width - reach : width - reach + tile_x, width : width + tile_y]
            + padded[:, width + reach : width + reach + tile_x, width : width + tile_y]
            + padded[:, width : width + tile_x, width - reach : width - reach + tile_y]
            + padded[:, width : width + tile_x, width + reach : width + reach + tile_y]
            + shift_z(center, reach)
            + shift_z(center, -reach)
        )
    return -0.5 * laplacian


def box_targets(places, tile_x, tile_y, depth):
    box_steps = jnp.arange(12, dtype=jnp.int32)
    tile_shift = jnp.arange(3, dtype=jnp.int32) - 1
    target_x = (
        tile_shift[:, None, None, None] * tile_x + places[:, :, :, 0][..., None] - 6 + box_steps
    )
    target_y = (
        tile_shift[None, :, None, None] * tile_y + places[:, :, :, 1][..., None] - 6 + box_steps
    )
    target_z = places[:, :, :, 2][..., None] - 6 + box_steps
    target_x = jnp.where((target_x >= 0) & (target_x < tile_x), target_x, tile_x + 12)
    target_y = jnp.where((target_y >= 0) & (target_y < tile_y), target_y, tile_y + 12)
    depth_cells = jnp.arange(depth, dtype=jnp.int32)
    window = (target_z[..., None] == depth_cells).astype(jnp.float32)
    return (target_x, target_y, window)


def own_intersection(widened, atom_offsets, window, projector_rows):
    nbands = widened.shape[0]
    box_steps = jnp.arange(12, dtype=jnp.int32)
    owned = atom_offsets[0, 0]
    index_x = (owned[:, 0:1] + box_steps[None, :])[:, :, None]
    index_y = (owned[:, 1:2] + box_steps[None, :])[:, None, :]
    columns = widened[:, index_x, index_y]
    box_values = jnp.einsum("bauvz,akz->bauvk", columns, window[1, 1], precision=PRECISE)
    box_values = box_values.reshape(nbands, -1, 1728)
    return jnp.einsum("ik,bak->aib", projector_rows, box_values, precision=PRECISE)


def projector_terms(
    intersection, proj_counts, targets, dh_matrix, ds_matrix, projector_rows, field_shape
):
    nbands, tile_x, tile_y, depth = field_shape
    active = (jnp.arange(NPROJ, dtype=jnp.int32)[None, :] < proj_counts[0, 0][:, None]).astype(
        jnp.float32
    )
    intersection = intersection * active[:, :, None]
    coefficients = jnp.stack(
        [
            jnp.einsum("aij,ajb->aib", dh_matrix[0, 0], intersection, precision=PRECISE),
            jnp.einsum("aij,ajb->aib", ds_matrix[0, 0], intersection, precision=PRECISE),
        ]
    )
    coefficients = coefficients * active[None, :, :, None]
    nearby = extended(coefficients[None, None], (("dx", 0), ("dy", 1)), 1)
    spread = jnp.einsum("ik,uvhaib->hbuvak", projector_rows, nearby, precision=PRECISE)
    spread = spread.reshape(2, nbands, 3, 3, -1, 144, 12)
    target_x, target_y, window = targets
    placed = jnp.einsum("hbuvaxk,uvakz->hbuvaxz", spread, window, precision=PRECISE)
    placed = placed.reshape(2, nbands, 3, 3, -1, 12, 12, depth)
    correction = jnp.zeros((2, nbands, tile_x, tile_y, depth), jnp.float32)
    correction = correction.at[:, :, target_x[..., :, None], target_y[..., None, :]].add(
        placed, mode="drop"
    )
    return (correction[0], correction[1])


def hamiltonian(
    field, full_potential, atom_offsets, proj_counts, targets, dh_matrix, ds_matrix, projector_rows
):
    tile_x, tile_y = (field.shape[1], field.shape[2])
    widened = extended(field, (("dx", 1), ("dy", 2)), 6)
    kinetic_part = kinetic_padded(widened, 6, tile_x, tile_y)
    intersection = own_intersection(widened, atom_offsets, targets[2], projector_rows)
    corr_h, corr_s = projector_terms(
        intersection, proj_counts, targets, dh_matrix, ds_matrix, projector_rows, field.shape
    )
    return (kinetic_part + full_potential[None] * field + corr_h, field + corr_s)


def domain_sums(values):
    return lax.psum(values, ("dx", "dy"))


def diagonal_of(level):
    return 3.0 / 4.0**level + MASS_SHIFT


def tile_apply(field, level):
    padded = extended(field, (("dx", 1), ("dy", 2)), 1)
    neighbours = (
        padded[:, :-2, 1:-1]
        + padded[:, 2:, 1:-1]
        + padded[:, 1:-1, :-2]
        + padded[:, 1:-1, 2:]
        + shift_z(field, 1)
        + shift_z(field, -1)
    )
    return -0.5 * (neighbours - 6.0 * field) / 4.0**level + MASS_SHIFT * field


def pair_table(depth):
    fine_cells = jnp.arange(depth, dtype=jnp.int32)[:, None] // 2
    coarse_cells = jnp.arange(depth // 2, dtype=jnp.int32)[None, :]
    return (fine_cells == coarse_cells).astype(jnp.float32)


def restrict(field):
    nbands, size_x, size_y, size_z = field.shape
    planar = field.reshape(nbands, size_x // 2, 2, size_y // 2, 2, size_z).mean(axis=(2, 4))
    return jnp.einsum("bxyz,zw->bxyw", planar, 0.5 * pair_table(size_z), precision=PRECISE)


def prolong(field):
    size_z = field.shape[3]
    widened = jnp.repeat(jnp.repeat(field, 2, axis=1), 2, axis=2)
    return jnp.einsum("bxyw,zw->bxyz", widened, pair_table(2 * size_z), precision=PRECISE)


def precondition(source_zero):
    guess_zero = RELAXATION * source_zero / diagonal_of(0)
    source_one = restrict(source_zero - tile_apply(guess_zero, 0))
    guess_one = RELAXATION * source_one / diagonal_of(1)
    source_two = restrict(source_one - tile_apply(guess_one, 1))
    guess_two = RELAXATION * source_two / diagonal_of(2)
    for _ in range(COARSE_SWEEPS):
        guess_two = guess_two + RELAXATION * (source_two - tile_apply(guess_two, 2)) / diagonal_of(
            2
        )
    guess_one = guess_one + prolong(guess_two)
    guess_one = guess_one + RELAXATION * (source_one - tile_apply(guess_one, 1)) / diagonal_of(1)
    guess_zero = guess_zero + prolong(guess_one)
    return guess_zero + RELAXATION * (source_zero - tile_apply(guess_zero, 0)) / diagonal_of(0)


def distributed(wave_bands, potential, atom_offsets, proj_counts, dh_matrix, ds_matrix):
    projector_rows = projector_table()
    full_potential = lax.all_gather(potential, "band", axis=2, tiled=True)
    places = extended(atom_offsets, (("dx", 0), ("dy", 1)), 1)
    targets = box_targets(places, wave_bands.shape[1], wave_bands.shape[2], wave_bands.shape[3])
    h_band, s_band = hamiltonian(
        wave_bands,
        full_potential,
        atom_offsets,
        proj_counts,
        targets,
        dh_matrix,
        ds_matrix,
        projector_rows,
    )
    energy_sums = domain_sums(
        jnp.stack(
            [
                jnp.sum(wave_bands * h_band, axis=(1, 2, 3)),
                jnp.sum(wave_bands * s_band, axis=(1, 2, 3)),
            ]
        )
    )
    band_energy = energy_sums[0] / energy_sums[1]
    energy_grid = band_energy[:, None, None, None]
    residual = h_band - energy_grid * s_band
    direction = precondition(residual)
    h_dir, s_dir = hamiltonian(
        direction,
        full_potential,
        atom_offsets,
        proj_counts,
        targets,
        dh_matrix,
        ds_matrix,
        projector_rows,
    )
    change = h_dir - energy_grid * s_dir
    line_sums = domain_sums(
        jnp.stack(
            [jnp.sum(residual * change, axis=(1, 2, 3)), jnp.sum(change * change, axis=(1, 2, 3))]
        )
    )
    step_grid = (-line_sums[0] / line_sums[1])[:, None, None, None]
    return (wave_bands + step_grid * direction, residual + step_grid * change, band_energy)


BOX_LOW = 6
BOX_CELLS = 12
LANES = 128
SUBLANES = 8
RADIAL_WIDTHS = (8.0, 9.68, 11.52)
PLANE_FACTORS = (
    (0, 0, 0),
    (1, 1, 0),
    (1, 0, 1),
    (1, 0, 0),
    (2, 1, 1),
    (2, 0, 1),
    (2, 1, 0),
    (2, 2, 0),
    (2, 0, 0),
    (2, 0, 2),
)
D_SCALE = 0.28867513
DEPTH_SCALE = 180.0
BLOCK = 8
VMEM_BUDGET = 40 * 1024 * 1024
VMEM_GRANT = 24 * 1024 * 1024


class Sizes:
    def __init__(self, wave, potential, atoms, tiles_x, tiles_y, groups):
        self.tile_x, self.tile_y, self.depth = wave.shape[1:]
        self.atoms = atoms
        self.tiles_x, self.tiles_y, self.groups = tiles_x, tiles_y, groups
        self.grid_x, self.grid_y = tiles_x * self.tile_x, tiles_y * self.tile_y
        self.cells = self.grid_x * self.grid_y
        self.chunk = potential.shape[2]
        self.all_atoms = tiles_x * tiles_y * atoms
        self.wave_rows = self.tile_x * self.tile_y
        self.pot_rows = self.wave_rows // groups
        self.param_rows = -(-2 * atoms // SUBLANES) * SUBLANES
        self.rows = self.pot_rows + self.param_rows
        self.factors = len(PLANE_FACTORS) * self.all_atoms

    def fits(self, vmem_bytes):
        return (
            self.depth == LANES
            and self.chunk * self.groups == LANES
            and self.tile_x % max(self.groups, BLOCK) == 0
            and self.tile_y % 16 == 0
            and self.grid_x >= 2 * BLOCK
            and self.grid_y >= 32
            and self.all_atoms % 16 == 0
            and LANES % self.all_atoms == 0
            and self.cells * (60 * LANES + 8 * self.factors) <= vmem_bytes
        )


def lanes_of(rows=1):
    return lax.broadcasted_iota(jnp.int32, (rows, LANES), 1)


def split(value):
    high = value.astype(jnp.bfloat16)
    return high, (value - high.astype(jnp.float32)).astype(jnp.bfloat16)


def halves(value):
    return value[:, :LANES] + value[:, LANES:]


def dot(left, right):
    return jnp.dot(left, right, preferred_element_type=jnp.float32)


META_LANE = 96


def pack_kernel(sz, pot_ref, offs_ref, counts_ref, dh_ref, ds_ref, wave_ref, out_ref, own_ref, *scratch):
    *places, sems = scratch
    pot, offs, counts, dh, ds = places
    base = sz.pot_rows
    sources = (pot_ref, offs_ref, counts_ref, dh_ref, ds_ref, wave_ref)
    places = places + [own_ref]
    copies = [
        pltpu.make_async_copy(a, b, sems.at[i])
        for i, (a, b) in enumerate(zip(sources, places))
    ]
    for copy in copies:
        copy.start()
    out_ref[base:, :] = jnp.zeros((sz.param_rows, LANES), jnp.float32)
    for copy in copies:
        copy.wait()
    per = sz.tile_x // sz.groups
    pieces = [
        pot[g * per : (g + 1) * per].reshape(sz.pot_rows, sz.chunk) for g in range(sz.groups)
    ]
    out_ref[:base, :] = pltpu.roll(
        jnp.concatenate(pieces, axis=1), lax.axis_index("band") * sz.chunk, 1
    )
    for j in range(NPROJ):
        lanes = slice(j * NPROJ, (j + 1) * NPROJ)
        out_ref[base : base + sz.atoms, lanes] = dh[0, 0, j]
        out_ref[base + sz.atoms : base + 2 * sz.atoms, lanes] = ds[0, 0, j]
    lane = lanes_of(1)
    for a in range(sz.atoms):
        row = jnp.where(lane == META_LANE + 3, counts[0, 0, a].astype(jnp.float32), 0.0)
        for k in range(3):
            row = jnp.where(lane == META_LANE + k, offs[0, k, 0, a].astype(jnp.float32), row)
        out_ref[base + a : base + a + 1, META_LANE : META_LANE + 4] = row[:, META_LANE : META_LANE + 4]


def wrapped(cell, centre, count):
    offset = cell - centre + float(BOX_LOW)
    offset = jnp.where(offset < 0.0, offset + float(count), offset)
    offset = jnp.where(offset >= float(count), offset - float(count), offset)
    inside = offset < float(BOX_CELLS)
    return offset - float(BOX_LOW), inside


def fill_rims(ref, width, count_x, count_y):
    ref[:, 0:SUBLANES, :] = ref[:, count_y : count_y + SUBLANES, :]
    ref[:, count_y + SUBLANES : count_y + 2 * SUBLANES, :] = ref[:, SUBLANES : 2 * SUBLANES, :]
    ref[0:width] = ref[count_x : count_x + width]
    ref[count_x + width : count_x + 2 * width] = ref[width : 2 * width]


def shifted_pair(value, reach):
    lane = lanes_of(1)
    below = jnp.where(lane >= reach, pltpu.roll(value, reach, 1), 0.0)
    above = jnp.where(lane < LANES - reach, pltpu.roll(value, LANES - reach, 1), 0.0)
    return below + above


def planar_kinetic(ref, x0, y0, rows, count):
    at = lambda x, y: ref[x0 + x + 3, pl.ds(SUBLANES + y0 + y, rows), :]
    planes = [at(x, 0) for x in range(-3, count + 3)]
    found = []
    for x in range(count):
        total = None
        for reach in (1, 2, 3):
            around = (planes[x + 3 - reach] + planes[x + 3 + reach]) + (at(x, -reach) + at(x, reach))
            term = (-0.5 * STENCIL[reach]) * around
            total = term if total is None else total + term
        found.append((planes[x + 3], total))
    return found


def depth_matrix():
    row = lax.broadcasted_iota(jnp.int32, (2 * LANES, LANES), 0) % LANES
    reach = jnp.abs(row - lax.broadcasted_iota(jnp.int32, (2 * LANES, LANES), 1))
    value = jnp.zeros((2 * LANES, LANES), jnp.float32)
    for k in (1, 2, 3):
        value = jnp.where(reach == k, -0.5 * STENCIL[k] * DEPTH_SCALE, value)
    return value.astype(jnp.bfloat16)


def neighbour_block(ref, x0, y0, rows, count, step):
    at = lambda x, y: ref[x0 + x + 1, pl.ds(SUBLANES + y0 + y, rows), :]
    planes = [at(x, 0) for x in range(-1, count + 1)]
    found = []
    for x in range(count):
        center = planes[x + 1]
        around = (planes[x] + planes[x + 2]) + (at(x, -1) + at(x, 1)) + shifted_pair(center, step)
        found.append((center, around))
    return found


def over_blocks(count, body):
    for x0 in range(0, count, BLOCK):
        body(x0)


def plane_weights(sz, meta, w_ref, a_ref, wx_ref, wy_ref):
    atoms = sz.all_atoms
    widths = [-1.0 / w for w in RADIAL_WIDTHS]
    for tile in range(sz.cells // LANES):
        cell = lanes_of(1) + tile * LANES
        cell_x = (cell // sz.grid_y).astype(jnp.float32)
        cell_y = (cell % sz.grid_y).astype(jnp.float32)
        for start in range(0, atoms, 16):
            rx, inside_x = wrapped(cell_x, meta[start : start + 16, 0:1], sz.grid_x)
            ry, inside_y = wrapped(cell_y, meta[start : start + 16, 1:2], sz.grid_y)
            square = rx * rx + ry * ry
            inside = jnp.logical_and(inside_x, inside_y)
            radial = [jnp.where(inside, jnp.exp(square * w), 0.0) for w in widths]
            powers_x, powers_y = [None, rx, rx * rx], [None, ry, ry * ry]
            for index, (kind, px, py) in enumerate(PLANE_FACTORS):
                value = radial[kind]
                value = value if px == 0 else value * powers_x[px]
                value = value if py == 0 else value * powers_y[py]
                high, low = split(value)
                at = index * atoms + start
                lanes = slice(tile * LANES, (tile + 1) * LANES)
                w_ref[at : at + 16, lanes] = high
                w_ref[sz.factors + at : sz.factors + at + 16, lanes] = low
    turned = jnp.concatenate([meta] * (LANES // atoms), axis=0).T
    tiles = 2 * sz.factors // LANES
    for axis, count, ref in ((0, sz.grid_x, wx_ref), (1, sz.grid_y, wy_ref)):
        centre = turned[axis : axis + 1, :]
        cell = lax.broadcasted_iota(jnp.int32, (count, LANES), 0).astype(jnp.float32)
        offset, inside = wrapped(cell, centre, count)
        radial = [jnp.where(inside, jnp.exp(offset * offset * w), 0.0) for w in widths]
        powers = [1.0, offset, offset * offset]
        for tile in range(tiles):
            place = lanes_of(1) // atoms + tile * (LANES // atoms)
            value = None
            for slot in range(LANES // atoms):
                index = tile * (LANES // atoms) + slot
                kind, *power = PLANE_FACTORS[index % len(PLANE_FACTORS)]
                term = radial[kind] if power[axis] == 0 else radial[kind] * powers[power[axis]]
                value = term if value is None else jnp.where(place == index, term, value)
            ref[tile] = value

    def planes(x):
        rows = pl.ds(pl.multiple_of(x * sz.grid_y, 16), sz.grid_y)
        for tile in range(tiles):
            lanes = slice(tile * LANES, (tile + 1) * LANES)
            value = wx_ref[tile, pl.ds(x, 1), :] * wy_ref[tile]
            high = value.astype(jnp.bfloat16)
            if (tile + 1) * LANES > sz.factors:
                low = value - high.astype(jnp.float32)
                if tile * LANES < sz.factors:
                    low = jnp.where(lanes_of(1) + tile * LANES < sz.factors, value, low)
                high = low.astype(jnp.bfloat16)
            a_ref[rows, lanes] = high

    lax.fori_loop(0, sz.grid_x, lambda x, c: (planes(x), c)[1], 0, unroll=4)


def depth_weights(meta, wz_ref):
    offset = lanes_of(1).astype(jnp.float32) - meta[:, 2:3]
    inside = jnp.logical_and(offset >= -float(BOX_LOW), offset < float(BOX_CELLS - BOX_LOW))
    radial = [
        jnp.where(inside, (AMPLITUDE * scale) * jnp.exp(offset * offset * (-1.0 / w)), 0.0)
        for scale, w in zip((1.0, 1.0 / 2.2, 1.0 / 5.76), RADIAL_WIDTHS)
    ]
    wz_ref[0] = radial[0]
    wz_ref[1] = radial[1]
    wz_ref[2] = radial[1] * offset
    wz_ref[3] = radial[2]
    wz_ref[4] = radial[2] * offset
    wz_ref[5] = radial[2] * (offset * offset)


def plane_sums(sz, w_ref, parts, x0):
    cells = slice(x0 * sz.grid_y, (x0 + BLOCK) * sz.grid_y)
    field = parts[cells, :]
    sums = dot(w_ref[:, cells], field)
    return halves(sums[: sz.factors]) + sums[sz.factors :, :LANES]


def intersections(sz, sums, wz_ref, active):
    u = [sums[c * sz.all_atoms : (c + 1) * sz.all_atoms] for c in range(len(PLANE_FACTORS))]
    products = [
        u[0] * wz_ref[0],
        u[1] * wz_ref[1],
        u[2] * wz_ref[1],
        u[3] * wz_ref[2],
        u[4] * wz_ref[3],
        u[5] * wz_ref[4],
        u[6] * wz_ref[4],
        (0.5 * (u[7] - u[9])) * wz_ref[3],
        D_SCALE * (2.0 * u[8] * wz_ref[5] - (u[7] + u[9]) * wz_ref[3]),
    ]
    return [jnp.sum(p, axis=1, keepdims=True) * active[i] for i, p in enumerate(products)]


def active_columns(meta):
    return [(meta[:, 3:4] > float(i)).astype(jnp.float32) for i in range(NPROJ)]


def inner_lanes(columns):
    lane = lanes_of(1)
    inner = jnp.zeros((columns[0].shape[0], LANES), jnp.float32)
    for k in range(NPROJ):
        inner = jnp.where(jnp.logical_and(lane % NPROJ == k, lane < NPROJ * NPROJ), columns[k], inner)
    return inner


def projector_sources(sz, matrix, inner, active, wz_ref, q_ref):
    lane = lanes_of(1)
    terms = DEPTH_SCALE * (matrix * inner)
    coef = [
        jnp.sum(jnp.where(lane // NPROJ == i, terms, 0.0), axis=1, keepdims=True) * active[i]
        for i in range(NPROJ)
    ]
    tilt = (0.5 * coef[7]) * wz_ref[3]
    ring = (D_SCALE * coef[8]) * wz_ref[3]
    blocks = [
        coef[0] * wz_ref[0],
        coef[1] * wz_ref[1],
        coef[2] * wz_ref[1],
        coef[3] * wz_ref[2],
        coef[4] * wz_ref[3],
        coef[5] * wz_ref[4],
        coef[6] * wz_ref[4],
        tilt - ring,
        (2.0 * D_SCALE * coef[8]) * wz_ref[5],
        -(tilt + ring),
    ]
    for index, block in enumerate(blocks):
        at = index * sz.all_atoms
        high, low = split(block)
        q_ref[at : at + sz.all_atoms, :LANES] = high
        q_ref[at : at + sz.all_atoms, LANES:] = low
        q_ref[sz.factors + at : sz.factors + at + sz.all_atoms, :LANES] = high


def tile_at(sz, index):
    turn_y, turn_x = divmod(index, sz.tiles_x)
    tile_x = partner(lax.axis_index("dx"), turn_x, sz.tiles_x)
    tile_y = partner(lax.axis_index("dy"), turn_y, sz.tiles_y)
    return tile_x, tile_y


def add_projectors(sz, a_ref, q_ref, emit):
    part = sz.cells // 2
    for at in range(0, sz.cells, part):
        emit(at, part, halves(dot(a_ref[at : at + part, :], q_ref[...])))


def weights_kernel(sz, *refs):
    params, (w_ref, a_ref, wz_ref, par_ref, wx_ref, wy_ref) = refs[: sz.tiles_y], refs[sz.tiles_y :]
    for index in range(sz.tiles_x * sz.tiles_y):
        turn_y, turn_x = divmod(index, sz.tiles_x)
        tile_x, tile_y = tile_at(sz, index)
        tile = tile_x * sz.tiles_y + tile_y
        for k in range(2):
            at = turn_x * sz.param_rows + k * sz.atoms
            par_ref[k, pl.ds(tile * sz.atoms, sz.atoms), :] = params[turn_y][at : at + sz.atoms, :]
    owners = lax.broadcasted_iota(jnp.int32, (sz.all_atoms, LANES), 0) // sz.atoms
    lane = lanes_of(sz.all_atoms)
    meta = pltpu.roll(par_ref[0], LANES - META_LANE, 1)
    meta = meta + jnp.where(lane == 0, (owners // sz.tiles_y * sz.tile_x).astype(jnp.float32), 0.0)
    meta = meta + jnp.where(lane == 1, (owners % sz.tiles_y * sz.tile_y).astype(jnp.float32), 0.0)
    par_ref[2] = meta
    depth_weights(meta, wz_ref)
    plane_weights(sz, meta, w_ref, a_ref, wx_ref, wy_ref)


def first_kernel(sz, *refs):
    blocks, refs = refs[: sz.tiles_x * sz.tiles_y], refs[sz.tiles_x * sz.tiles_y :]
    (w_ref, wz_ref, par_ref, psi, zkin, inner_ref, parts) = refs
    nx, ny = sz.grid_x, sz.grid_y
    for index, block in enumerate(blocks):
        tile_x, tile_y = tile_at(sz, index)
        at_y = pl.multiple_of(tile_y * sz.tile_y, 16)
        for x in range(sz.tile_x):
            value = block[0, x]
            cell_x = tile_x * sz.tile_x + x
            psi[cell_x + 3, pl.ds(at_y + SUBLANES, sz.tile_y), :] = value
            rows = pl.ds(pl.multiple_of(cell_x * ny + at_y, 16), sz.tile_y)
            high, low = split(value)
            parts[rows, :LANES] = high
            parts[rows, LANES:] = low
    fill_rims(psi, 3, nx, ny)
    meta = par_ref[2]
    active = active_columns(meta)
    sums = None
    for x0 in range(0, nx, BLOCK):
        term = plane_sums(sz, w_ref, parts, x0)
        sums = term if sums is None else sums + term
    columns = intersections(sz, sums, wz_ref, active)
    zkin[...] = dot(parts[...], depth_matrix())
    inner = inner_lanes(columns)
    inner_ref[...] = inner


def second_kernel(sz, *refs):
    (psi, zkin, inner_ref, a_ref, wz_ref, par_ref, hpsi, spsi, sums_ref, q_ref) = refs
    nx, ny = sz.grid_x, sz.grid_y
    q_ref[sz.factors :, LANES:] = jnp.zeros((sz.factors, LANES), jnp.bfloat16)
    active = active_columns(par_ref[2])
    projector_sources(sz, par_ref[1], inner_ref[...], active, wz_ref, q_ref)

    def emit_s(at, rows, value):
        x0, count = at // ny, rows // ny
        center = psi[x0 + 3 : x0 + 3 + count, SUBLANES : SUBLANES + ny, :]
        spsi[x0 : x0 + count] = center + (1.0 / DEPTH_SCALE) * value.reshape(count, ny, LANES)

    add_projectors(sz, a_ref, q_ref, emit_s)
    projector_sources(sz, par_ref[0], inner_ref[...], active, wz_ref, q_ref)
    for x0 in range(0, nx, BLOCK):
        for y0 in range(0, ny, SUBLANES):
            for x, (center, value) in enumerate(planar_kinetic(psi, x0, y0, SUBLANES, BLOCK)):
                hpsi[x0 + x, y0 : y0 + SUBLANES, :] = value + (-1.5 * STENCIL[0]) * center
    found = []

    def emit_h(at, rows, value):
        planes = slice(at // ny, (at + rows) // ny)
        shape = (rows // ny, ny, LANES)
        center = psi[at // ny + 3 : (at + rows) // ny + 3, SUBLANES : SUBLANES + ny, :]
        value = (1.0 / DEPTH_SCALE) * (value + zkin[at : at + rows, :]).reshape(shape)
        value = value + hpsi[planes]
        hpsi[planes] = value
        found.append((folded(value * center), folded(spsi[planes] * center)))

    add_projectors(sz, a_ref, q_ref, emit_h)
    for row in range(2):
        total = found[0][row] + found[1][row]
        sums_ref[row : row + 1, :] = jnp.sum(total, axis=0, keepdims=True)


def folded(value):
    return jnp.sum(value.reshape(-1, SUBLANES, LANES), axis=0)


def pair_lanes(value, step):
    lane = lanes_of(1)
    other = jnp.where(
        (lane // step) % 2 == 1, pltpu.roll(value, step, 1), pltpu.roll(value, LANES - step, 1)
    )
    return value + other


def level_numbers(level):
    return 0.5 / 4.0**level, RELAXATION / diagonal_of(level)


def restrict_planes(count_x, count_y, level, source, emit):
    spread, guess = level_numbers(level)
    weight, step = spread * guess, 2**level
    for x in range(count_x // 2):
        for y0 in range(0, count_y // 2, SUBLANES):
            at = lambda dx, dy: source[
                2 * x + dx + 1, pl.ds(SUBLANES + 2 * y0 + dy, SUBLANES, stride=2), :
            ]
            inside = (at(0, 0) + at(0, 1)) + (at(1, 0) + at(1, 1))
            beside = (at(-1, 0) + at(-1, 1)) + (at(2, 0) + at(2, 1))
            beside = beside + ((at(0, -1) + at(1, -1)) + (at(0, 2) + at(1, 2)))
            beside = beside + shifted_pair(inside, step)
            total = (0.125 * (1.0 - RELAXATION + 2.0 * weight)) * inside + (0.125 * weight) * beside
            emit(x, y0, pair_lanes(total, step))


def coarsest(source):
    spread, guess = level_numbers(2)
    count, rows = len(source), source[0].shape[0]
    planes = [guess * b for b in source]
    for _ in range(COARSE_SWEEPS):
        fresh = []
        for x, b in enumerate(source):
            center = planes[x]
            around = planes[x - 1] + planes[(x + 1) % count]
            around = around + (pltpu.roll(center, 1, 0) + pltpu.roll(center, rows - 1, 0))
            around = around + shifted_pair(center, 4)
            fresh.append((1.0 - RELAXATION) * center + guess * b + (guess * spread) * around)
        planes = fresh
    return planes


def relax_rows(count_x, count_y, level, guess_ref, source, emit, after_block=lambda x0: None):
    spread, guess = level_numbers(level)
    rows = min(2 * SUBLANES, count_y)

    def body(x0):
        for y0 in range(0, count_y, rows):
            found = neighbour_block(guess_ref, x0, y0, rows, BLOCK, 2**level)
            for x, (center, around) in enumerate(found):
                right = source[x0 + x + 1, pl.ds(SUBLANES + y0, rows), :]
                value = (1.0 - RELAXATION) * center + guess * right + (guess * spread) * around
                emit(x0 + x, y0, rows, value)
        after_block(x0)

    over_blocks(count_x, body)


def prolong_into(count_x, count_y, level, coarse, source, target):
    guess = level_numbers(level)[1]

    def body(x0):
        for y0 in range(0, count_y, 2 * SUBLANES):
            for half in range(BLOCK // 2):
                value = coarse(x0 // 2 + half, y0 // 2)
                for part in range(2):
                    at = x0 + 2 * half + part + 1
                    for row in range(2):
                        rows = pl.ds(SUBLANES + y0 + row, SUBLANES, stride=2)
                        target[at, rows, :] = value + guess * source[at, rows, :]

    over_blocks(count_x, body)
    fill_rims(target, 1, count_x, count_y)


def place_potential(sz, pots, psi, pot, sums):
    per = sz.tile_x // sz.groups
    slot = lanes_of(1) // sz.chunk
    here_group = lax.axis_index("band")
    for index in range(sz.tiles_x * sz.tiles_y):
        shift_y, shift_x = divmod(index, sz.tiles_x)
        tile_x, tile_y = tile_at(sz, index)
        at_y = pl.multiple_of(tile_y * sz.tile_y, 16)
        total = jnp.zeros((sz.tile_y, LANES), jnp.float32)
        for g in range(sz.groups):
            value = None
            for shift_b in range(sz.groups):
                source = partner(here_group, shift_b, sz.groups)
                at = (shift_b * sz.tiles_x + shift_x) * sz.pot_rows
                piece = pots[shift_y][at : at + sz.pot_rows, :]
                chosen = slot == lax.rem(source + g, sz.groups)
                value = piece if value is None else jnp.where(chosen, piece, value)
            if g:
                value = pltpu.roll(value, LANES - g * sz.chunk, 1)
            for k in range(per):
                cell_x = tile_x * sz.tile_x + g * per + k
                plane = value[k * sz.tile_y : (k + 1) * sz.tile_y]
                pot[cell_x, pl.ds(at_y, sz.tile_y), :] = plane
                center = psi[cell_x + 3, pl.ds(at_y + SUBLANES, sz.tile_y), :]
                total = total + plane * (center * center)
        sums[tile_x * sz.tiles_y + tile_y] = total
    total = sums[0]
    for tile in range(1, sz.tiles_x * sz.tiles_y):
        total = total + sums[tile]
    return total


def step_kernel(sz, *refs):
    pots, refs = refs[: sz.tiles_y], refs[sz.tiles_y :]
    (psi, hpsi, spsi, w_ref, a_ref, wz_ref, par_ref, sums_ref), refs = refs[:8], refs[8:]
    (bands_ref, resid_ref, energy_ref), refs = refs[:3], refs[3:]
    (pot, res, zfield, direct, change, b1, z1, x1, parts, q_ref, zkin, tile_sums) = refs
    nx, ny = sz.grid_x, sz.grid_y
    here_x, here_y = lax.axis_index("dx"), lax.axis_index("dy")
    total = place_potential(sz, pots, psi, pot, tile_sums)
    energy = (jnp.sum(total) + jnp.sum(sums_ref[0:1, :])) / jnp.sum(sums_ref[1:2, :])
    energy_ref[0] = energy

    def residual(x0):
        for x in range(BLOCK):
            center = psi[x0 + x + 3, pl.ds(SUBLANES, ny), :]
            value = hpsi[x0 + x] + pot[x0 + x] * center - energy * spsi[x0 + x]
            pot[x0 + x] = pot[x0 + x] + (-1.5 * STENCIL[0] - energy)
            res[x0 + x + 1, pl.ds(SUBLANES, ny), :] = value

    over_blocks(nx, residual)
    fill_rims(res, 1, nx, ny)

    def emit_b1(x, y0, value):
        b1[x + 1, SUBLANES + y0 : 2 * SUBLANES + y0, :] = value

    restrict_planes(nx, ny, 0, res, emit_b1)
    fill_rims(b1, 1, nx // 2, ny // 2)
    pieces = {}

    def emit_b2(x, y0, value):
        pieces[x, y0] = value

    restrict_planes(nx // 2, ny // 2, 1, b1, emit_b2)
    tops = range(0, ny // 4, SUBLANES)
    planes = coarsest(
        [jnp.concatenate([pieces[x, y0] for y0 in tops], axis=0) for x in range(nx // 4)]
    )
    coarse_two = lambda x, y: planes[x][y : y + SUBLANES]
    prolong_into(nx // 2, ny // 2, 1, coarse_two, b1, z1)

    def emit_one(x, y0, rows, value):
        x1[x, pl.ds(y0, rows), :] = value

    relax_rows(nx // 2, ny // 2, 1, z1, b1, emit_one)
    prolong_into(nx, ny, 0, lambda x, y: x1[x, pl.ds(y, SUBLANES), :], res, zfield)

    def emit_zero(x, y0, rows, value):
        direct[x + 3, pl.ds(SUBLANES + y0, rows), :] = value
        cells = slice(x * ny + y0, x * ny + y0 + rows)
        high, low = split(value)
        parts[cells, :LANES] = high
        parts[cells, LANES:] = low

    found = []

    def after_block(x0):
        cells = slice(x0 * ny, (x0 + BLOCK) * ny)
        zkin[cells, :] = dot(parts[cells, :], depth_matrix())
        term = plane_sums(sz, w_ref, parts, x0)
        found.append(term if not found else found[-1] + term)

    relax_rows(nx, ny, 0, zfield, res, emit_zero, after_block)
    fill_rims(direct, 3, nx, ny)
    active = active_columns(par_ref[2])
    columns = intersections(sz, found[-1], wz_ref, active)
    for x0 in range(0, nx, BLOCK):
        for y0 in range(0, ny, SUBLANES):
            for x, (center, value) in enumerate(planar_kinetic(direct, x0, y0, SUBLANES, BLOCK)):
                rows = slice(y0, y0 + SUBLANES)
                change[x0 + x, rows, :] = value + pot[x0 + x, rows, :] * center
    q_ref[sz.factors :, LANES:] = jnp.zeros((sz.factors, LANES), jnp.bfloat16)
    matrix = par_ref[0] - energy * par_ref[1]
    projector_sources(sz, matrix, inner_lanes(columns), active, wz_ref, q_ref)
    found = []

    def emit_change(at, rows, value):
        planes = slice(at // ny, (at + rows) // ny)
        shape = (rows // ny, ny, LANES)
        value = (1.0 / DEPTH_SCALE) * (value + zkin[at : at + rows, :]).reshape(shape)
        value = value + change[planes]
        change[planes] = value
        before = res[at // ny + 1 : (at + rows) // ny + 1, SUBLANES : SUBLANES + ny, :]
        found.append((folded(value * before), folded(value * value)))

    add_projectors(sz, a_ref, q_ref, emit_change)
    over, under = (found[0][k] + found[1][k] for k in range(2))
    step = -jnp.sum(over) / jnp.sum(under)
    at_x, at_y = here_x * sz.tile_x, pl.multiple_of(here_y * sz.tile_y, 16)
    for x in range(sz.tile_x):
        cell = at_x + x
        inner = pl.ds(at_y + SUBLANES, sz.tile_y)
        bands_ref[0, x] = psi[cell + 3, inner, :] + step * direct[cell + 3, inner, :]
        resid_ref[0, x] = res[cell + 1, inner, :] + step * change[cell, pl.ds(at_y, sz.tile_y), :]


def partner(here, turn, count):
    return here ^ turn if count & (count - 1) == 0 else (here + turn) % count


def gathered(value, axis):
    count = lax.axis_size(axis)
    pairs = lambda turn: [(partner(i, turn, count), i) for i in range(count)]
    found = [value]
    for turn in range(1, count):
        found.append(lax.ppermute(value, axis, pairs(turn)))
    return found


def replicated(sz, wave_bands, potential, atom_offsets, proj_counts, dh_matrix, ds_matrix):
    vmem = pl.BlockSpec(memory_space=pltpu.VMEM)
    smem = pl.BlockSpec(memory_space=pltpu.SMEM)
    hbm = pl.BlockSpec(memory_space=pltpu.HBM)
    shape = lambda *dims: jax.ShapeDtypeStruct(dims, jnp.float32)
    half = lambda *dims: jax.ShapeDtypeStruct(dims, jnp.bfloat16)
    scratch = lambda *dims: pltpu.VMEM(dims, jnp.float32)
    grant = pltpu.CompilerParams(vmem_limit_bytes=VMEM_GRANT)
    cost = lambda flops: pl.CostEstimate(flops=flops, transcendentals=0, bytes_accessed=0)
    inputs = (
        potential,
        atom_offsets.transpose(0, 3, 1, 2),
        proj_counts,
        dh_matrix.transpose(0, 1, 3, 2, 4),
        ds_matrix.transpose(0, 1, 3, 2, 4),
        wave_bands,
    )
    own, wave = pl.pallas_call(
        functools.partial(pack_kernel, sz),
        out_shape=(shape(sz.rows, LANES), shape(*wave_bands.shape)),
        in_specs=[hbm] * 6,
        out_specs=(vmem, vmem),
        scratch_shapes=[
            scratch(*inputs[0].shape),
            pltpu.SMEM(inputs[1].shape, jnp.int32),
            pltpu.SMEM(inputs[2].shape, jnp.int32),
            scratch(*inputs[3].shape),
            scratch(*inputs[4].shape),
            pltpu.SemaphoreType.DMA((6,)),
        ],
        compiler_params=grant,
        name="pack",
    )(*(pltpu.with_memory_space_constraint(value, pltpu.HBM) for value in inputs))
    small = gathered(own, "dx")
    line = gathered(wave, "dx")
    chunk = jnp.concatenate([block[: sz.pot_rows] for block in small], axis=0)
    chunks = jnp.concatenate(gathered(chunk, "band"), axis=0)
    params = gathered(jnp.concatenate([block[sz.pot_rows :] for block in small], axis=0), "dy")
    crossed = [gathered(block, "dy") for block in line]
    blocks = [each[turn] for turn in range(sz.tiles_y) for each in crossed]
    pots = gathered(chunks, "dy")
    nx, ny = sz.grid_x, sz.grid_y
    padded = lambda x, y, width: (x + 2 * width, y + 2 * SUBLANES, LANES)
    q_scratch = pltpu.VMEM((2 * sz.factors, 2 * LANES), jnp.bfloat16)
    w, a, wz, par = pl.pallas_call(
        functools.partial(weights_kernel, sz),
        out_shape=(
            half(2 * sz.factors, sz.cells),
            half(sz.cells, 2 * sz.factors),
            shape(6, sz.all_atoms, LANES),
            shape(3, sz.all_atoms, LANES),
        ),
        in_specs=[vmem] * len(params),
        out_specs=(vmem,) * 4,
        scratch_shapes=[scratch(2 * sz.factors // LANES, n, LANES) for n in (nx, ny)],
        compiler_params=grant,
        cost_estimate=cost(1_000_000_000),
        name="weights",
    )(*params)
    psi, zkin, inner = pl.pallas_call(
        functools.partial(first_kernel, sz),
        out_shape=(shape(*padded(nx, ny, 3)), shape(sz.cells, LANES), shape(sz.all_atoms, LANES)),
        in_specs=[vmem] * (len(blocks) + 3),
        out_specs=(vmem,) * 3,
        scratch_shapes=[pltpu.VMEM((sz.cells, 2 * LANES), jnp.bfloat16)],
        compiler_params=grant,
        cost_estimate=cost(2_000_000_000),
        name="first",
    )(*blocks, w, wz, par)
    hpsi, spsi, sums = pl.pallas_call(
        functools.partial(second_kernel, sz),
        out_shape=(shape(nx, ny, LANES), shape(nx, ny, LANES), shape(2, LANES)),
        in_specs=[vmem] * 6,
        out_specs=(vmem,) * 3,
        scratch_shapes=[q_scratch],
        compiler_params=grant,
        cost_estimate=cost(2_000_000_000),
        name="second",
    )(psi, zkin, inner, a, wz, par)
    made = (psi, hpsi, spsi, w, a, wz, par, sums)
    return pl.pallas_call(
        functools.partial(step_kernel, sz),
        out_shape=(
            jax.ShapeDtypeStruct(wave_bands.shape, jnp.float32),
            jax.ShapeDtypeStruct(wave_bands.shape, jnp.float32),
            shape(1),
        ),
        in_specs=[vmem] * (len(pots) + 8),
        out_specs=(vmem, vmem, smem),
        scratch_shapes=[
            scratch(nx, ny, LANES),
            scratch(*padded(nx, ny, 1)),
            scratch(*padded(nx, ny, 1)),
            scratch(*padded(nx, ny, 3)),
            scratch(nx, ny, LANES),
            scratch(*padded(nx // 2, ny // 2, 1)),
            scratch(*padded(nx // 2, ny // 2, 1)),
            scratch(nx // 2, ny // 2, LANES),
            pltpu.VMEM((sz.cells, 2 * LANES), jnp.bfloat16),
            pltpu.VMEM((2 * sz.factors, 2 * LANES), jnp.bfloat16),
            scratch(sz.cells, LANES),
            scratch(sz.tiles_x * sz.tiles_y, sz.tile_y, LANES),
        ],
        compiler_params=grant,
        cost_estimate=cost(6_000_000_000),
        name="step",
    )(*pots, *made)


def on_device(wave_bands, potential, atom_offsets, proj_counts, dh_matrix, ds_matrix):
    sz = Sizes(
        wave_bands,
        potential,
        proj_counts.shape[2],
        lax.axis_size("dx"),
        lax.axis_size("dy"),
        lax.axis_size("band"),
    )
    step = functools.partial(replicated, sz) if sz.fits(VMEM_BUDGET) else distributed
    return step(wave_bands, potential, atom_offsets, proj_counts, dh_matrix, ds_matrix)


def solution(mesh):
    return jax.shard_map(
        on_device,
        mesh=mesh,
        in_specs=(
            P("band", "dx", "dy", None),
            P("dx", "dy", "band"),
            P("dx", "dy", None, None),
            P("dx", "dy", None),
            P("dx", "dy", None, None, None),
            P("dx", "dy", None, None, None),
        ),
        out_specs=(P("band", "dx", "dy", None), P("band", "dx", "dy", None), P("band")),
        check_vma=False,
    )
```

```python
import functools

import jax
import jax.numpy as jnp
from jax import lax
from jax.experimental import pallas as pl
from jax.experimental.pallas import tpu as pltpu
from jax.sharding import PartitionSpec as P

NPROJ = 9
COARSE_SWEEPS = 2


STENCIL = (-49.0 / 18.0, 1.5, -0.15, 1.0 / 90.0)
RELAXATION = 2.0 / 3.0
MASS_SHIFT = 0.25
AMPLITUDE = 0.15
PRECISE = lax.Precision.HIGHEST


def extended(cells, sides, width):
    for axis, dim in sides:
        count = lax.axis_size(axis)
        head = lax.slice_in_dim(cells, 0, width, axis=dim)
        tail = lax.slice_in_dim(cells, cells.shape[dim] - width, cells.shape[dim], axis=dim)
        cells = jnp.concatenate(
            [
                lax.ppermute(tail, axis, [(i, (i + 1) % count) for i in range(count)]),
                cells,
                lax.ppermute(head, axis, [((i + 1) % count, i) for i in range(count)]),
            ],
            axis=dim,
        )
    return cells


def projector_table():
    box_steps = jnp.arange(12, dtype=jnp.float32) - 6.0
    filler = jnp.ones((12, 12, 12), jnp.float32)
    along_x = box_steps[:, None, None] * filler
    along_y = box_steps[None, :, None] * filler
    along_z = box_steps[None, None, :] * filler
    radius_sq = along_x * along_x + along_y * along_y + along_z * along_z
    radial_s = jnp.exp(-radius_sq / 8.0)
    radial_p = jnp.exp(-radius_sq / 9.68) / 2.2
    radial_d = jnp.exp(-radius_sq / 11.52) / 5.76
    angular = [
        radial_s,
        radial_p * along_x,
        radial_p * along_y,
        radial_p * along_z,
        radial_d * along_x * along_y,
        radial_d * along_y * along_z,
        radial_d * along_z * along_x,
        0.5 * radial_d * (along_x * along_x - along_y * along_y),
        radial_d * (3.0 * along_z * along_z - radius_sq) * 0.28867513,
    ]
    return AMPLITUDE * jnp.stack(angular).reshape(9, 1728)


def shift_z(field, reach):
    depth = field.shape[-1]
    zeros_rim = jnp.zeros(field.shape[:-1] + (abs(reach),), field.dtype)
    if reach > 0:
        return jnp.concatenate([zeros_rim, field[..., : depth - reach]], axis=-1)
    return jnp.concatenate([field[..., -reach:], zeros_rim], axis=-1)


def kinetic_padded(padded, width, tile_x, tile_y):
    center = padded[:, width : width + tile_x, width : width + tile_y]
    laplacian = 3.0 * STENCIL[0] * center
    for reach in (1, 2, 3):
        weight = STENCIL[reach]
        laplacian = laplacian + weight * (
            padded[:, width - reach : width - reach + tile_x, width : width + tile_y]
            + padded[:, width + reach : width + reach + tile_x, width : width + tile_y]
            + padded[:, width : width + tile_x, width - reach : width - reach + tile_y]
            + padded[:, width : width + tile_x, width + reach : width + reach + tile_y]
            + shift_z(center, reach)
            + shift_z(center, -reach)
        )
    return -0.5 * laplacian


def box_targets(places, tile_x, tile_y, depth):
    box_steps = jnp.arange(12, dtype=jnp.int32)
    tile_shift = jnp.arange(3, dtype=jnp.int32) - 1
    target_x = (
        tile_shift[:, None, None, None] * tile_x + places[:, :, :, 0][..., None] - 6 + box_steps
    )
    target_y = (
        tile_shift[None, :, None, None] * tile_y + places[:, :, :, 1][..., None] - 6 + box_steps
    )
    target_z = places[:, :, :, 2][..., None] - 6 + box_steps
    target_x = jnp.where((target_x >= 0) & (target_x < tile_x), target_x, tile_x + 12)
    target_y = jnp.where((target_y >= 0) & (target_y < tile_y), target_y, tile_y + 12)
    depth_cells = jnp.arange(depth, dtype=jnp.int32)
    window = (target_z[..., None] == depth_cells).astype(jnp.float32)
    return (target_x, target_y, window)


def own_intersection(widened, atom_offsets, window, projector_rows):
    nbands = widened.shape[0]
    box_steps = jnp.arange(12, dtype=jnp.int32)
    owned = atom_offsets[0, 0]
    index_x = (owned[:, 0:1] + box_steps[None, :])[:, :, None]
    index_y = (owned[:, 1:2] + box_steps[None, :])[:, None, :]
    columns = widened[:, index_x, index_y]
    box_values = jnp.einsum("bauvz,akz->bauvk", columns, window[1, 1], precision=PRECISE)
    box_values = box_values.reshape(nbands, -1, 1728)
    return jnp.einsum("ik,bak->aib", projector_rows, box_values, precision=PRECISE)


def projector_terms(
    intersection, proj_counts, targets, dh_matrix, ds_matrix, projector_rows, field_shape
):
    nbands, tile_x, tile_y, depth = field_shape
    active = (jnp.arange(NPROJ, dtype=jnp.int32)[None, :] < proj_counts[0, 0][:, None]).astype(
        jnp.float32
    )
    intersection = intersection * active[:, :, None]
    coefficients = jnp.stack(
        [
            jnp.einsum("aij,ajb->aib", dh_matrix[0, 0], intersection, precision=PRECISE),
            jnp.einsum("aij,ajb->aib", ds_matrix[0, 0], intersection, precision=PRECISE),
        ]
    )
    coefficients = coefficients * active[None, :, :, None]
    nearby = extended(coefficients[None, None], (("dx", 0), ("dy", 1)), 1)
    spread = jnp.einsum("ik,uvhaib->hbuvak", projector_rows, nearby, precision=PRECISE)
    spread = spread.reshape(2, nbands, 3, 3, -1, 144, 12)
    target_x, target_y, window = targets
    placed = jnp.einsum("hbuvaxk,uvakz->hbuvaxz", spread, window, precision=PRECISE)
    placed = placed.reshape(2, nbands, 3, 3, -1, 12, 12, depth)
    correction = jnp.zeros((2, nbands, tile_x, tile_y, depth), jnp.float32)
    correction = correction.at[:, :, target_x[..., :, None], target_y[..., None, :]].add(
        placed, mode="drop"
    )
    return (correction[0], correction[1])


def hamiltonian(
    field, full_potential, atom_offsets, proj_counts, targets, dh_matrix, ds_matrix, projector_rows
):
    tile_x, tile_y = (field.shape[1], field.shape[2])
    widened = extended(field, (("dx", 1), ("dy", 2)), 6)
    kinetic_part = kinetic_padded(widened, 6, tile_x, tile_y)
    intersection = own_intersection(widened, atom_offsets, targets[2], projector_rows)
    corr_h, corr_s = projector_terms(
        intersection, proj_counts, targets, dh_matrix, ds_matrix, projector_rows, field.shape
    )
    return (kinetic_part + full_potential[None] * field + corr_h, field + corr_s)


def domain_sums(values):
    return lax.psum(values, ("dx", "dy"))


def diagonal_of(level):
    return 3.0 / 4.0**level + MASS_SHIFT


def tile_apply(field, level):
    padded = extended(field, (("dx", 1), ("dy", 2)), 1)
    neighbours = (
        padded[:, :-2, 1:-1]
        + padded[:, 2:, 1:-1]
        + padded[:, 1:-1, :-2]
        + padded[:, 1:-1, 2:]
        + shift_z(field, 1)
        + shift_z(field, -1)
    )
    return -0.5 * (neighbours - 6.0 * field) / 4.0**level + MASS_SHIFT * field


def pair_table(depth):
    fine_cells = jnp.arange(depth, dtype=jnp.int32)[:, None] // 2
    coarse_cells = jnp.arange(depth // 2, dtype=jnp.int32)[None, :]
    return (fine_cells == coarse_cells).astype(jnp.float32)


def restrict(field):
    nbands, size_x, size_y, size_z = field.shape
    planar = field.reshape(nbands, size_x // 2, 2, size_y // 2, 2, size_z).mean(axis=(2, 4))
    return jnp.einsum("bxyz,zw->bxyw", planar, 0.5 * pair_table(size_z), precision=PRECISE)


def prolong(field):
    size_z = field.shape[3]
    widened = jnp.repeat(jnp.repeat(field, 2, axis=1), 2, axis=2)
    return jnp.einsum("bxyw,zw->bxyz", widened, pair_table(2 * size_z), precision=PRECISE)


def precondition(source_zero):
    guess_zero = RELAXATION * source_zero / diagonal_of(0)
    source_one = restrict(source_zero - tile_apply(guess_zero, 0))
    guess_one = RELAXATION * source_one / diagonal_of(1)
    source_two = restrict(source_one - tile_apply(guess_one, 1))
    guess_two = RELAXATION * source_two / diagonal_of(2)
    for _ in range(COARSE_SWEEPS):
        guess_two = guess_two + RELAXATION * (source_two - tile_apply(guess_two, 2)) / diagonal_of(
            2
        )
    guess_one = guess_one + prolong(guess_two)
    guess_one = guess_one + RELAXATION * (source_one - tile_apply(guess_one, 1)) / diagonal_of(1)
    guess_zero = guess_zero + prolong(guess_one)
    return guess_zero + RELAXATION * (source_zero - tile_apply(guess_zero, 0)) / diagonal_of(0)


def distributed(wave_bands, potential, atom_offsets, proj_counts, dh_matrix, ds_matrix):
    projector_rows = projector_table()
    full_potential = lax.all_gather(potential, "band", axis=2, tiled=True)
    places = extended(atom_offsets, (("dx", 0), ("dy", 1)), 1)
    targets = box_targets(places, wave_bands.shape[1], wave_bands.shape[2], wave_bands.shape[3])
    h_band, s_band = hamiltonian(
        wave_bands,
        full_potential,
        atom_offsets,
        proj_counts,
        targets,
        dh_matrix,
        ds_matrix,
        projector_rows,
    )
    energy_sums = domain_sums(
        jnp.stack(
            [
                jnp.sum(wave_bands * h_band, axis=(1, 2, 3)),
                jnp.sum(wave_bands * s_band, axis=(1, 2, 3)),
            ]
        )
    )
    band_energy = energy_sums[0] / energy_sums[1]
    energy_grid = band_energy[:, None, None, None]
    residual = h_band - energy_grid * s_band
    direction = precondition(residual)
    h_dir, s_dir = hamiltonian(
        direction,
        full_potential,
        atom_offsets,
        proj_counts,
        targets,
        dh_matrix,
        ds_matrix,
        projector_rows,
    )
    change = h_dir - energy_grid * s_dir
    line_sums = domain_sums(
        jnp.stack(
            [jnp.sum(residual * change, axis=(1, 2, 3)), jnp.sum(change * change, axis=(1, 2, 3))]
        )
    )
    step_grid = (-line_sums[0] / line_sums[1])[:, None, None, None]
    return (wave_bands + step_grid * direction, residual + step_grid * change, band_energy)


BOX_LOW = 6
BOX_CELLS = 12
LANES = 128
SUBLANES = 8
RADIAL_WIDTHS = (8.0, 9.68, 11.52)
PLANE_FACTORS = (
    (0, 0, 0),
    (1, 1, 0),
    (1, 0, 1),
    (1, 0, 0),
    (2, 1, 1),
    (2, 0, 1),
    (2, 1, 0),
    (2, 2, 0),
    (2, 0, 0),
    (2, 0, 2),
)
D_SCALE = 0.28867513
DEPTH_SCALE = 180.0
BLOCK = 8
LUMP = 2
VMEM_BUDGET = 40 * 1024 * 1024
VMEM_GRANT = 24 * 1024 * 1024


class Sizes:
    def __init__(self, wave, potential, atoms, tiles_x, tiles_y, groups):
        self.tile_x, self.tile_y, self.depth = wave.shape[1:]
        self.atoms = atoms
        self.tiles_x, self.tiles_y, self.groups = tiles_x, tiles_y, groups
        self.grid_x, self.grid_y = tiles_x * self.tile_x, tiles_y * self.tile_y
        self.cells = self.grid_x * self.grid_y
        self.chunk = potential.shape[2]
        self.all_atoms = tiles_x * tiles_y * atoms
        self.wave_rows = self.tile_x * self.tile_y
        self.pot_rows = self.wave_rows // groups
        self.param_rows = -(-2 * atoms // SUBLANES) * SUBLANES
        self.rows = self.pot_rows + self.param_rows
        self.factors = len(PLANE_FACTORS) * self.all_atoms

    def fits(self, vmem_bytes):
        return (
            self.depth == LANES
            and self.chunk * self.groups == LANES
            and self.tile_x % max(self.groups, BLOCK) == 0
            and self.tile_y % 16 == 0
            and self.grid_x >= 2 * BLOCK
            and self.grid_y >= 32
            and self.all_atoms % 16 == 0
            and LANES % self.all_atoms == 0
            and self.cells * (60 * LANES + 8 * self.factors) <= vmem_bytes
        )


def lanes_of(rows=1):
    return lax.broadcasted_iota(jnp.int32, (rows, LANES), 1)


def split(value):
    high = value.astype(jnp.bfloat16)
    return high, (value - high.astype(jnp.float32)).astype(jnp.bfloat16)


def halves(value):
    return value[:, :LANES] + value[:, LANES:]


def dot(left, right):
    return jnp.dot(left, right, preferred_element_type=jnp.float32)


META_LANE = 96


def pack_kernel(sz, pot_ref, offs_ref, counts_ref, dh_ref, ds_ref, wave_ref, out_ref, own_ref, *scratch):
    *places, sems = scratch
    pot, offs, counts, dh, ds = places
    base = sz.pot_rows
    sources = (pot_ref, offs_ref, counts_ref, dh_ref, ds_ref, wave_ref)
    places = places + [own_ref]
    copies = [
        pltpu.make_async_copy(a, b, sems.at[i])
        for i, (a, b) in enumerate(zip(sources, places))
    ]
    for copy in copies:
        copy.start()
    out_ref[base:, :] = jnp.zeros((sz.param_rows, LANES), jnp.float32)
    for copy in copies:
        copy.wait()
    per = sz.tile_x // sz.groups
    pieces = [
        pot[g * per : (g + 1) * per].reshape(sz.pot_rows, sz.chunk) for g in range(sz.groups)
    ]
    out_ref[:base, :] = pltpu.roll(
        jnp.concatenate(pieces, axis=1), lax.axis_index("band") * sz.chunk, 1
    )
    for j in range(NPROJ):
        lanes = slice(j * NPROJ, (j + 1) * NPROJ)
        out_ref[base : base + sz.atoms, lanes] = dh[0, 0, j]
        out_ref[base + sz.atoms : base + 2 * sz.atoms, lanes] = ds[0, 0, j]
    lane = lanes_of(1)
    for a in range(sz.atoms):
        row = jnp.where(lane == META_LANE + 3, counts[0, 0, a].astype(jnp.float32), 0.0)
        for k in range(3):
            row = jnp.where(lane == META_LANE + k, offs[0, k, 0, a].astype(jnp.float32), row)
        out_ref[base + a : base + a + 1, META_LANE : META_LANE + 4] = row[:, META_LANE : META_LANE + 4]


def wrapped(cell, centre, count):
    offset = cell - centre + float(BOX_LOW)
    offset = jnp.where(offset < 0.0, offset + float(count), offset)
    offset = jnp.where(offset >= float(count), offset - float(count), offset)
    inside = offset < float(BOX_CELLS)
    return offset - float(BOX_LOW), inside


def fill_rims(ref, width, count_x, count_y):
    ref[:, 0:SUBLANES, :] = ref[:, count_y : count_y + SUBLANES, :]
    ref[:, count_y + SUBLANES : count_y + 2 * SUBLANES, :] = ref[:, SUBLANES : 2 * SUBLANES, :]
    ref[0:width] = ref[count_x : count_x + width]
    ref[count_x + width : count_x + 2 * width] = ref[width : 2 * width]


def shifted_pair(value, reach):
    lane = lanes_of(1)
    below = jnp.where(lane >= reach, pltpu.roll(value, reach, 1), 0.0)
    above = jnp.where(lane < LANES - reach, pltpu.roll(value, LANES - reach, 1), 0.0)
    return below + above


def planar_kinetic(ref, x0, y0, rows, count):
    at = lambda x, y: ref[x0 + x + 3, pl.ds(SUBLANES + y0 + y, rows), :]
    planes = [at(x, 0) for x in range(-3, count + 3)]
    found = []
    for x in range(count):
        total = None
        for reach in (1, 2, 3):
            around = (planes[x + 3 - reach] + planes[x + 3 + reach]) + (at(x, -reach) + at(x, reach))
            term = (-0.5 * STENCIL[reach]) * around
            total = term if total is None else total + term
        found.append((planes[x + 3], total))
    return found


def depth_matrix():
    row = lax.broadcasted_iota(jnp.int32, (2 * LANES, LANES), 0) % LANES
    reach = jnp.abs(row - lax.broadcasted_iota(jnp.int32, (2 * LANES, LANES), 1))
    value = jnp.zeros((2 * LANES, LANES), jnp.float32)
    for k in (1, 2, 3):
        value = jnp.where(reach == k, -0.5 * STENCIL[k] * DEPTH_SCALE, value)
    return value.astype(jnp.bfloat16)


def neighbour_block(ref, x0, y0, rows, count, step):
    at = lambda x, y: ref[x0 + x + 1, pl.ds(SUBLANES + y0 + y, rows), :]
    planes = [at(x, 0) for x in range(-1, count + 1)]
    found = []
    for x in range(count):
        center = planes[x + 1]
        around = (planes[x] + planes[x + 2]) + (at(x, -1) + at(x, 1)) + shifted_pair(center, step)
        found.append((center, around))
    return found


def over_blocks(count, body):
    for x0 in range(0, count, BLOCK):
        body(x0)


def plane_weights(sz, meta, w_ref, a_ref, wx_ref, wy_ref):
    atoms = sz.all_atoms
    widths = [-1.0 / w for w in RADIAL_WIDTHS]
    for tile in range(sz.cells // LANES):
        cell = lanes_of(1) + tile * LANES
        cell_x = (cell // sz.grid_y).astype(jnp.float32)
        cell_y = (cell % sz.grid_y).astype(jnp.float32)
        for start in range(0, atoms, 16):
            rx, inside_x = wrapped(cell_x, meta[start : start + 16, 0:1], sz.grid_x)
            ry, inside_y = wrapped(cell_y, meta[start : start + 16, 1:2], sz.grid_y)
            square = rx * rx + ry * ry
            inside = jnp.logical_and(inside_x, inside_y)
            radial = [jnp.where(inside, jnp.exp(square * w), 0.0) for w in widths]
            powers_x, powers_y = [None, rx, rx * rx], [None, ry, ry * ry]
            for index, (kind, px, py) in enumerate(PLANE_FACTORS):
                value = radial[kind]
                value = value if px == 0 else value * powers_x[px]
                value = value if py == 0 else value * powers_y[py]
                high, low = split(value)
                at = index * atoms + start
                lanes = slice(tile * LANES, (tile + 1) * LANES)
                w_ref[at : at + 16, lanes] = high
                w_ref[sz.factors + at : sz.factors + at + 16, lanes] = low
    turned = jnp.concatenate([meta] * (LANES // atoms), axis=0).T
    tiles = 2 * sz.factors // LANES
    for axis, count, ref in ((0, sz.grid_x, wx_ref), (1, sz.grid_y, wy_ref)):
        centre = turned[axis : axis + 1, :]
        cell = lax.broadcasted_iota(jnp.int32, (count, LANES), 0).astype(jnp.float32)
        offset, inside = wrapped(cell, centre, count)
        radial = [jnp.where(inside, jnp.exp(offset * offset * w), 0.0) for w in widths]
        powers = [1.0, offset, offset * offset]
        for tile in range(tiles):
            place = lanes_of(1) // atoms + tile * (LANES // atoms)
            value = None
            for slot in range(LANES // atoms):
                index = tile * (LANES // atoms) + slot
                kind, *power = PLANE_FACTORS[index % len(PLANE_FACTORS)]
                term = radial[kind] if power[axis] == 0 else radial[kind] * powers[power[axis]]
                value = term if value is None else jnp.where(place == index, term, value)
            ref[tile] = value

    def planes(x):
        rows = pl.ds(pl.multiple_of(x * sz.grid_y, 16), sz.grid_y)
        for tile in range(tiles):
            lanes = slice(tile * LANES, (tile + 1) * LANES)
            value = wx_ref[tile, pl.ds(x, 1), :] * wy_ref[tile]
            high = value.astype(jnp.bfloat16)
            if (tile + 1) * LANES > sz.factors:
                low = value - high.astype(jnp.float32)
                if tile * LANES < sz.factors:
                    low = jnp.where(lanes_of(1) + tile * LANES < sz.factors, value, low)
                high = low.astype(jnp.bfloat16)
            a_ref[rows, lanes] = high

    lax.fori_loop(0, sz.grid_x, lambda x, c: (planes(x), c)[1], 0, unroll=4)


def depth_weights(meta, wz_ref):
    offset = lanes_of(1).astype(jnp.float32) - meta[:, 2:3]
    inside = jnp.logical_and(offset >= -float(BOX_LOW), offset < float(BOX_CELLS - BOX_LOW))
    radial = [
        jnp.where(inside, (AMPLITUDE * scale) * jnp.exp(offset * offset * (-1.0 / w)), 0.0)
        for scale, w in zip((1.0, 1.0 / 2.2, 1.0 / 5.76), RADIAL_WIDTHS)
    ]
    wz_ref[0] = radial[0]
    wz_ref[1] = radial[1]
    wz_ref[2] = radial[1] * offset
    wz_ref[3] = radial[2]
    wz_ref[4] = radial[2] * offset
    wz_ref[5] = radial[2] * (offset * offset)


def plane_sums(sz, w_ref, parts, x0, x1):
    cells = slice(x0 * sz.grid_y, x1 * sz.grid_y)
    field = parts[cells, :]
    sums = dot(w_ref[:, cells], field)
    return halves(sums[: sz.factors]) + sums[sz.factors :, :LANES]


def intersections(sz, sums, wz_ref, active):
    u = [sums[c * sz.all_atoms : (c + 1) * sz.all_atoms] for c in range(len(PLANE_FACTORS))]
    products = [
        u[0] * wz_ref[0],
        u[1] * wz_ref[1],
        u[2] * wz_ref[1],
        u[3] * wz_ref[2],
        u[4] * wz_ref[3],
        u[5] * wz_ref[4],
        u[6] * wz_ref[4],
        (0.5 * (u[7] - u[9])) * wz_ref[3],
        D_SCALE * (2.0 * u[8] * wz_ref[5] - (u[7] + u[9]) * wz_ref[3]),
    ]
    return [jnp.sum(p, axis=1, keepdims=True) * active[i] for i, p in enumerate(products)]


def active_columns(meta):
    return [(meta[:, 3:4] > float(i)).astype(jnp.float32) for i in range(NPROJ)]


def inner_lanes(columns):
    lane = lanes_of(1)
    inner = jnp.zeros((columns[0].shape[0], LANES), jnp.float32)
    for k in range(NPROJ):
        inner = jnp.where(jnp.logical_and(lane % NPROJ == k, lane < NPROJ * NPROJ), columns[k], inner)
    return inner


def projector_sources(sz, matrix, inner, active, wz_ref, q_ref):
    lane = lanes_of(1)
    terms = DEPTH_SCALE * (matrix * inner)
    coef = [
        jnp.sum(jnp.where(lane // NPROJ == i, terms, 0.0), axis=1, keepdims=True) * active[i]
        for i in range(NPROJ)
    ]
    tilt = (0.5 * coef[7]) * wz_ref[3]
    ring = (D_SCALE * coef[8]) * wz_ref[3]
    blocks = [
        coef[0] * wz_ref[0],
        coef[1] * wz_ref[1],
        coef[2] * wz_ref[1],
        coef[3] * wz_ref[2],
        coef[4] * wz_ref[3],
        coef[5] * wz_ref[4],
        coef[6] * wz_ref[4],
        tilt - ring,
        (2.0 * D_SCALE * coef[8]) * wz_ref[5],
        -(tilt + ring),
    ]
    for index, block in enumerate(blocks):
        at = index * sz.all_atoms
        high, low = split(block)
        q_ref[at : at + sz.all_atoms, :LANES] = high
        q_ref[at : at + sz.all_atoms, LANES:] = low
        q_ref[sz.factors + at : sz.factors + at + sz.all_atoms, :LANES] = high


def tile_at(sz, index):
    turn_y, turn_x = divmod(index, sz.tiles_x)
    tile_x = partner(lax.axis_index("dx"), turn_x, sz.tiles_x)
    tile_y = partner(lax.axis_index("dy"), turn_y, sz.tiles_y)
    return tile_x, tile_y


def add_projectors(sz, a_ref, q_ref, emit):
    part = sz.cells // 2
    for at in range(0, sz.cells, part):
        emit(at, part, halves(dot(a_ref[at : at + part, :], q_ref[...])))


def weights_kernel(sz, *refs):
    params, (w_ref, a_ref, wz_ref, par_ref, wx_ref, wy_ref) = refs[: sz.tiles_y], refs[sz.tiles_y :]
    for index in range(sz.tiles_x * sz.tiles_y):
        turn_y, turn_x = divmod(index, sz.tiles_x)
        tile_x, tile_y = tile_at(sz, index)
        tile = tile_x * sz.tiles_y + tile_y
        for k in range(2):
            at = turn_x * sz.param_rows + k * sz.atoms
            par_ref[k, pl.ds(tile * sz.atoms, sz.atoms), :] = params[turn_y][at : at + sz.atoms, :]
    owners = lax.broadcasted_iota(jnp.int32, (sz.all_atoms, LANES), 0) // sz.atoms
    lane = lanes_of(sz.all_atoms)
    meta = pltpu.roll(par_ref[0], LANES - META_LANE, 1)
    meta = meta + jnp.where(lane == 0, (owners // sz.tiles_y * sz.tile_x).astype(jnp.float32), 0.0)
    meta = meta + jnp.where(lane == 1, (owners % sz.tiles_y * sz.tile_y).astype(jnp.float32), 0.0)
    par_ref[2] = meta
    depth_weights(meta, wz_ref)
    plane_weights(sz, meta, w_ref, a_ref, wx_ref, wy_ref)


def first_kernel(sz, *refs):
    blocks, refs = refs[: sz.tiles_x * sz.tiles_y], refs[sz.tiles_x * sz.tiles_y :]
    (w_ref, wz_ref, par_ref, psi, zkin, inner_ref, parts) = refs
    nx, ny = sz.grid_x, sz.grid_y
    for index, block in enumerate(blocks):
        tile_x, tile_y = tile_at(sz, index)
        at_y = pl.multiple_of(tile_y * sz.tile_y, 16)
        for x in range(sz.tile_x):
            value = block[0, x]
            cell_x = tile_x * sz.tile_x + x
            psi[cell_x + 3, pl.ds(at_y + SUBLANES, sz.tile_y), :] = value
            rows = pl.ds(pl.multiple_of(cell_x * ny + at_y, 16), sz.tile_y)
            high, low = split(value)
            parts[rows, :LANES] = high
            parts[rows, LANES:] = low
    fill_rims(psi, 3, nx, ny)
    meta = par_ref[2]
    active = active_columns(meta)
    sums = None
    for x0 in range(0, nx, BLOCK):
        term = plane_sums(sz, w_ref, parts, x0, x0 + BLOCK)
        sums = term if sums is None else sums + term
    columns = intersections(sz, sums, wz_ref, active)
    zkin[...] = dot(parts[...], depth_matrix())
    inner = inner_lanes(columns)
    inner_ref[...] = inner


def second_kernel(sz, *refs):
    (psi, zkin, inner_ref, a_ref, wz_ref, par_ref, hpsi, spsi, sums_ref, q_ref) = refs
    nx, ny = sz.grid_x, sz.grid_y
    q_ref[sz.factors :, LANES:] = jnp.zeros((sz.factors, LANES), jnp.bfloat16)
    active = active_columns(par_ref[2])
    projector_sources(sz, par_ref[1], inner_ref[...], active, wz_ref, q_ref)

    def emit_s(at, rows, value):
        x0, count = at // ny, rows // ny
        center = psi[x0 + 3 : x0 + 3 + count, SUBLANES : SUBLANES + ny, :]
        spsi[x0 : x0 + count] = center + (1.0 / DEPTH_SCALE) * value.reshape(count, ny, LANES)

    add_projectors(sz, a_ref, q_ref, emit_s)
    projector_sources(sz, par_ref[0], inner_ref[...], active, wz_ref, q_ref)
    for x0 in range(0, nx, BLOCK):
        for y0 in range(0, ny, SUBLANES):
            for x, (center, value) in enumerate(planar_kinetic(psi, x0, y0, SUBLANES, BLOCK)):
                hpsi[x0 + x, y0 : y0 + SUBLANES, :] = value + (-1.5 * STENCIL[0]) * center
    found = []

    def emit_h(at, rows, value):
        planes = slice(at // ny, (at + rows) // ny)
        shape = (rows // ny, ny, LANES)
        center = psi[at // ny + 3 : (at + rows) // ny + 3, SUBLANES : SUBLANES + ny, :]
        value = (1.0 / DEPTH_SCALE) * (value + zkin[at : at + rows, :]).reshape(shape)
        value = value + hpsi[planes]
        hpsi[planes] = value
        found.append((folded(value * center), folded(spsi[planes] * center)))

    add_projectors(sz, a_ref, q_ref, emit_h)
    for row in range(2):
        total = found[0][row] + found[1][row]
        sums_ref[row : row + 1, :] = jnp.sum(total, axis=0, keepdims=True)


def folded(value):
    return jnp.sum(value.reshape(-1, SUBLANES, LANES), axis=0)


def pair_lanes(value, step):
    lane = lanes_of(1)
    other = jnp.where(
        (lane // step) % 2 == 1, pltpu.roll(value, step, 1), pltpu.roll(value, LANES - step, 1)
    )
    return value + other


def level_numbers(level):
    return 0.5 / 4.0**level, RELAXATION / diagonal_of(level)


def restrict_planes(count_x, count_y, level, source, emit):
    spread, guess = level_numbers(level)
    weight, step = spread * guess, 2**level
    for x in range(count_x // 2):
        for y0 in range(0, count_y // 2, SUBLANES):
            at = lambda dx, dy: source[
                2 * x + dx + 1, pl.ds(SUBLANES + 2 * y0 + dy, SUBLANES, stride=2), :
            ]
            inside = (at(0, 0) + at(0, 1)) + (at(1, 0) + at(1, 1))
            beside = (at(-1, 0) + at(-1, 1)) + (at(2, 0) + at(2, 1))
            beside = beside + ((at(0, -1) + at(1, -1)) + (at(0, 2) + at(1, 2)))
            beside = beside + shifted_pair(inside, step)
            total = (0.125 * (1.0 - RELAXATION + 2.0 * weight)) * inside + (0.125 * weight) * beside
            emit(x, y0, pair_lanes(total, step))


def coarsest(source):
    spread, guess = level_numbers(2)
    count, rows = len(source), source[0].shape[0]
    planes = [guess * b for b in source]
    for _ in range(COARSE_SWEEPS):
        fresh = []
        for x, b in enumerate(source):
            center = planes[x]
            around = planes[x - 1] + planes[(x + 1) % count]
            around = around + (pltpu.roll(center, 1, 0) + pltpu.roll(center, rows - 1, 0))
            around = around + shifted_pair(center, 4)
            fresh.append((1.0 - RELAXATION) * center + guess * b + (guess * spread) * around)
        planes = fresh
    return planes


def relax_rows(count_x, count_y, level, guess_ref, source, emit, after_block=lambda x0: None):
    spread, guess = level_numbers(level)
    rows = min(2 * SUBLANES, count_y)

    def body(x0):
        for y0 in range(0, count_y, rows):
            found = neighbour_block(guess_ref, x0, y0, rows, BLOCK, 2**level)
            for x, (center, around) in enumerate(found):
                right = source[x0 + x + 1, pl.ds(SUBLANES + y0, rows), :]
                value = (1.0 - RELAXATION) * center + guess * right + (guess * spread) * around
                emit(x0 + x, y0, rows, value)
        after_block(x0)

    over_blocks(count_x, body)


def prolong_into(count_x, count_y, level, coarse, source, target):
    guess = level_numbers(level)[1]

    def body(x0):
        for y0 in range(0, count_y, 2 * SUBLANES):
            for half in range(BLOCK // 2):
                value = coarse(x0 // 2 + half, y0 // 2)
                for part in range(2):
                    at = x0 + 2 * half + part + 1
                    for row in range(2):
                        rows = pl.ds(SUBLANES + y0 + row, SUBLANES, stride=2)
                        target[at, rows, :] = value + guess * source[at, rows, :]

    over_blocks(count_x, body)
    fill_rims(target, 1, count_x, count_y)


def place_potential(sz, pots, psi, pot, sums):
    per = sz.tile_x // sz.groups
    slot = lanes_of(1) // sz.chunk
    here_group = lax.axis_index("band")
    for index in range(sz.tiles_x * sz.tiles_y):
        shift_y, shift_x = divmod(index, sz.tiles_x)
        tile_x, tile_y = tile_at(sz, index)
        at_y = pl.multiple_of(tile_y * sz.tile_y, 16)
        total = jnp.zeros((sz.tile_y, LANES), jnp.float32)
        for g in range(sz.groups):
            value = None
            for shift_b in range(sz.groups):
                source = partner(here_group, shift_b, sz.groups)
                at = (shift_b * sz.tiles_x + shift_x) * sz.pot_rows
                piece = pots[shift_y][at : at + sz.pot_rows, :]
                chosen = slot == lax.rem(source + g, sz.groups)
                value = piece if value is None else jnp.where(chosen, piece, value)
            if g:
                value = pltpu.roll(value, LANES - g * sz.chunk, 1)
            for k in range(per):
                cell_x = tile_x * sz.tile_x + g * per + k
                plane = value[k * sz.tile_y : (k + 1) * sz.tile_y]
                pot[cell_x, pl.ds(at_y, sz.tile_y), :] = plane
                center = psi[cell_x + 3, pl.ds(at_y + SUBLANES, sz.tile_y), :]
                total = total + plane * (center * center)
        sums[tile_x * sz.tiles_y + tile_y] = total
    total = sums[0]
    for tile in range(1, sz.tiles_x * sz.tiles_y):
        total = total + sums[tile]
    return total


def step_kernel(sz, *refs):
    pots, refs = refs[: sz.tiles_y], refs[sz.tiles_y :]
    (psi, hpsi, spsi, w_ref, a_ref, wz_ref, par_ref, sums_ref), refs = refs[:8], refs[8:]
    (bands_ref, resid_ref, energy_ref), refs = refs[:3], refs[3:]
    (pot, res, zfield, direct, change, b1, z1, x1, parts, q_ref, zkin, tile_sums) = refs
    nx, ny = sz.grid_x, sz.grid_y
    here_x, here_y = lax.axis_index("dx"), lax.axis_index("dy")
    total = place_potential(sz, pots, psi, pot, tile_sums)
    energy = (jnp.sum(total) + jnp.sum(sums_ref[0:1, :])) / jnp.sum(sums_ref[1:2, :])
    energy_ref[0] = energy

    def residual(x0):
        for x in range(BLOCK):
            center = psi[x0 + x + 3, pl.ds(SUBLANES, ny), :]
            value = hpsi[x0 + x] + pot[x0 + x] * center - energy * spsi[x0 + x]
            pot[x0 + x] = pot[x0 + x] + (-1.5 * STENCIL[0] - energy)
            res[x0 + x + 1, pl.ds(SUBLANES, ny), :] = value

    over_blocks(nx, residual)
    fill_rims(res, 1, nx, ny)

    def emit_b1(x, y0, value):
        b1[x + 1, SUBLANES + y0 : 2 * SUBLANES + y0, :] = value

    restrict_planes(nx, ny, 0, res, emit_b1)
    fill_rims(b1, 1, nx // 2, ny // 2)
    pieces = {}

    def emit_b2(x, y0, value):
        pieces[x, y0] = value

    restrict_planes(nx // 2, ny // 2, 1, b1, emit_b2)
    tops = range(0, ny // 4, SUBLANES)
    planes = coarsest(
        [jnp.concatenate([pieces[x, y0] for y0 in tops], axis=0) for x in range(nx // 4)]
    )
    coarse_two = lambda x, y: planes[x][y : y + SUBLANES]
    prolong_into(nx // 2, ny // 2, 1, coarse_two, b1, z1)

    def emit_one(x, y0, rows, value):
        x1[x, pl.ds(y0, rows), :] = value

    relax_rows(nx // 2, ny // 2, 1, z1, b1, emit_one)
    prolong_into(nx, ny, 0, lambda x, y: x1[x, pl.ds(y, SUBLANES), :], res, zfield)

    def emit_zero(x, y0, rows, value):
        direct[x + 3, pl.ds(SUBLANES + y0, rows), :] = value
        cells = slice(x * ny + y0, x * ny + y0 + rows)
        high, low = split(value)
        parts[cells, :LANES] = high
        parts[cells, LANES:] = low

    found, waiting = [], []

    def after_block(x0):
        cells = slice(x0 * ny, (x0 + BLOCK) * ny)
        zkin[cells, :] = dot(parts[cells, :], depth_matrix())
        waiting.append(x0)
        if len(waiting) == LUMP or x0 + BLOCK == nx:
            term = plane_sums(sz, w_ref, parts, waiting[0], x0 + BLOCK)
            found.append(term if not found else found[-1] + term)
            waiting.clear()

    relax_rows(nx, ny, 0, zfield, res, emit_zero, after_block)
    fill_rims(direct, 3, nx, ny)
    active = active_columns(par_ref[2])
    columns = intersections(sz, found[-1], wz_ref, active)
    for x0 in range(0, nx, BLOCK):
        for y0 in range(0, ny, SUBLANES):
            for x, (center, value) in enumerate(planar_kinetic(direct, x0, y0, SUBLANES, BLOCK)):
                rows = slice(y0, y0 + SUBLANES)
                change[x0 + x, rows, :] = value + pot[x0 + x, rows, :] * center
    q_ref[sz.factors :, LANES:] = jnp.zeros((sz.factors, LANES), jnp.bfloat16)
    matrix = par_ref[0] - energy * par_ref[1]
    projector_sources(sz, matrix, inner_lanes(columns), active, wz_ref, q_ref)
    found = []

    def emit_change(at, rows, value):
        planes = slice(at // ny, (at + rows) // ny)
        shape = (rows // ny, ny, LANES)
        value = (1.0 / DEPTH_SCALE) * (value + zkin[at : at + rows, :]).reshape(shape)
        value = value + change[planes]
        change[planes] = value
        before = res[at // ny + 1 : (at + rows) // ny + 1, SUBLANES : SUBLANES + ny, :]
        found.append((folded(value * before), folded(value * value)))

    add_projectors(sz, a_ref, q_ref, emit_change)
    over, under = (found[0][k] + found[1][k] for k in range(2))
    step = -jnp.sum(over) / jnp.sum(under)
    at_x, at_y = here_x * sz.tile_x, pl.multiple_of(here_y * sz.tile_y, 16)
    for x in range(sz.tile_x):
        cell = at_x + x
        inner = pl.ds(at_y + SUBLANES, sz.tile_y)
        bands_ref[0, x] = psi[cell + 3, inner, :] + step * direct[cell + 3, inner, :]
        resid_ref[0, x] = res[cell + 1, inner, :] + step * change[cell, pl.ds(at_y, sz.tile_y), :]


def partner(here, turn, count):
    return here ^ turn if count & (count - 1) == 0 else (here + turn) % count


def gathered(value, axis):
    count = lax.axis_size(axis)
    pairs = lambda turn: [(partner(i, turn, count), i) for i in range(count)]
    found = [value]
    for turn in range(1, count):
        found.append(lax.ppermute(value, axis, pairs(turn)))
    return found


def replicated(sz, wave_bands, potential, atom_offsets, proj_counts, dh_matrix, ds_matrix):
    vmem = pl.BlockSpec(memory_space=pltpu.VMEM)
    smem = pl.BlockSpec(memory_space=pltpu.SMEM)
    hbm = pl.BlockSpec(memory_space=pltpu.HBM)
    shape = lambda *dims: jax.ShapeDtypeStruct(dims, jnp.float32)
    half = lambda *dims: jax.ShapeDtypeStruct(dims, jnp.bfloat16)
    scratch = lambda *dims: pltpu.VMEM(dims, jnp.float32)
    grant = pltpu.CompilerParams(vmem_limit_bytes=VMEM_GRANT)
    cost = lambda flops: pl.CostEstimate(flops=flops, transcendentals=0, bytes_accessed=0)
    inputs = (
        potential,
        atom_offsets.transpose(0, 3, 1, 2),
        proj_counts,
        dh_matrix.transpose(0, 1, 3, 2, 4),
        ds_matrix.transpose(0, 1, 3, 2, 4),
        wave_bands,
    )
    own, wave = pl.pallas_call(
        functools.partial(pack_kernel, sz),
        out_shape=(shape(sz.rows, LANES), shape(*wave_bands.shape)),
        in_specs=[hbm] * 6,
        out_specs=(vmem, vmem),
        scratch_shapes=[
            scratch(*inputs[0].shape),
            pltpu.SMEM(inputs[1].shape, jnp.int32),
            pltpu.SMEM(inputs[2].shape, jnp.int32),
            scratch(*inputs[3].shape),
            scratch(*inputs[4].shape),
            pltpu.SemaphoreType.DMA((6,)),
        ],
        compiler_params=grant,
        name="pack",
    )(*(pltpu.with_memory_space_constraint(value, pltpu.HBM) for value in inputs))
    small = gathered(own, "dx")
    line = gathered(wave, "dx")
    chunk = jnp.concatenate([block[: sz.pot_rows] for block in small], axis=0)
    chunks = jnp.concatenate(gathered(chunk, "band"), axis=0)
    params = gathered(jnp.concatenate([block[sz.pot_rows :] for block in small], axis=0), "dy")
    crossed = [gathered(block, "dy") for block in line]
    blocks = [each[turn] for turn in range(sz.tiles_y) for each in crossed]
    pots = gathered(chunks, "dy")
    nx, ny = sz.grid_x, sz.grid_y
    padded = lambda x, y, width: (x + 2 * width, y + 2 * SUBLANES, LANES)
    q_scratch = pltpu.VMEM((2 * sz.factors, 2 * LANES), jnp.bfloat16)
    w, a, wz, par = pl.pallas_call(
        functools.partial(weights_kernel, sz),
        out_shape=(
            half(2 * sz.factors, sz.cells),
            half(sz.cells, 2 * sz.factors),
            shape(6, sz.all_atoms, LANES),
            shape(3, sz.all_atoms, LANES),
        ),
        in_specs=[vmem] * len(params),
        out_specs=(vmem,) * 4,
        scratch_shapes=[scratch(2 * sz.factors // LANES, n, LANES) for n in (nx, ny)],
        compiler_params=grant,
        cost_estimate=cost(1_000_000_000),
        name="weights",
    )(*params)
    psi, zkin, inner = pl.pallas_call(
        functools.partial(first_kernel, sz),
        out_shape=(shape(*padded(nx, ny, 3)), shape(sz.cells, LANES), shape(sz.all_atoms, LANES)),
        in_specs=[vmem] * (len(blocks) + 3),
        out_specs=(vmem,) * 3,
        scratch_shapes=[pltpu.VMEM((sz.cells, 2 * LANES), jnp.bfloat16)],
        compiler_params=grant,
        cost_estimate=cost(2_000_000_000),
        name="first",
    )(*blocks, w, wz, par)
    hpsi, spsi, sums = pl.pallas_call(
        functools.partial(second_kernel, sz),
        out_shape=(shape(nx, ny, LANES), shape(nx, ny, LANES), shape(2, LANES)),
        in_specs=[vmem] * 6,
        out_specs=(vmem,) * 3,
        scratch_shapes=[q_scratch],
        compiler_params=grant,
        cost_estimate=cost(2_000_000_000),
        name="second",
    )(psi, zkin, inner, a, wz, par)
    made = (psi, hpsi, spsi, w, a, wz, par, sums)
    return pl.pallas_call(
        functools.partial(step_kernel, sz),
        out_shape=(
            jax.ShapeDtypeStruct(wave_bands.shape, jnp.float32),
            jax.ShapeDtypeStruct(wave_bands.shape, jnp.float32),
            shape(1),
        ),
        in_specs=[vmem] * (len(pots) + 8),
        out_specs=(vmem, vmem, smem),
        scratch_shapes=[
            scratch(nx, ny, LANES),
            scratch(*padded(nx, ny, 1)),
            scratch(*padded(nx, ny, 1)),
            scratch(*padded(nx, ny, 3)),
            scratch(nx, ny, LANES),
            scratch(*padded(nx // 2, ny // 2, 1)),
            scratch(*padded(nx // 2, ny // 2, 1)),
            scratch(nx // 2, ny // 2, LANES),
            pltpu.VMEM((sz.cells, 2 * LANES), jnp.bfloat16),
            pltpu.VMEM((2 * sz.factors, 2 * LANES), jnp.bfloat16),
            scratch(sz.cells, LANES),
            scratch(sz.tiles_x * sz.tiles_y, sz.tile_y, LANES),
        ],
        compiler_params=grant,
        cost_estimate=cost(6_000_000_000),
        name="step",
    )(*pots, *made)


def on_device(wave_bands, potential, atom_offsets, proj_counts, dh_matrix, ds_matrix):
    sz = Sizes(
        wave_bands,
        potential,
        proj_counts.shape[2],
        lax.axis_size("dx"),
        lax.axis_size("dy"),
        lax.axis_size("band"),
    )
    step = functools.partial(replicated, sz) if sz.fits(VMEM_BUDGET) else distributed
    return step(wave_bands, potential, atom_offsets, proj_counts, dh_matrix, ds_matrix)


def solution(mesh):
    return jax.shard_map(
        on_device,
        mesh=mesh,
        in_specs=(
            P("band", "dx", "dy", None),
            P("dx", "dy", "band"),
            P("dx", "dy", None, None),
            P("dx", "dy", None),
            P("dx", "dy", None, None, None),
            P("dx", "dy", None, None, None),
        ),
        out_specs=(P("band", "dx", "dy", None), P("band", "dx", "dy", None), P("band")),
        check_vma=False,
    )
```
